512 devices in a mesh: stn: 16 (over x_lo, z), chan: 32 (over x_hi, y, core).
Axes of the slice: x: 4 (x_hi: 2, x_lo: 2; x = x_hi * 2 + x_lo), y: 8, z: 8, core: 2. Of those that a mesh axis runs over, the one named last changes fastest.
Arguments:
- positions: float32 [3, 256], P(None, 'stn'), may hold values from -1 to 1
- catalogue: float32 [7, 1024], P(None, 'chan'), may hold values from -1.5 to 1, as said below
- cluster_ids: int32 [16, 64], replicated, may hold values from 0 to 1023, as said below
- counts: int32 [16], replicated, may hold values from 16 to 64, as said below
- flag_mask: int32 [32, 256, 256], P('chan', 'stn'), may hold values 0 or 1
- thermal_noise: float32 [2, 4, 32, 256, 256], P(None, None, 'chan', 'stn'), may hold values from -3 to 3
- true_gains: float32 [2, 4, 16, 256], P(None, None, None, 'stn'), may hold values from -0.5 to 1.5, as said below
- start_gains: float32 [2, 4, 16, 256], P(None, None, None, 'stn'), may hold values from -0.5 to 1.2, as said below
Outputs:
- final_gains: float32 [2, 4, 16, 256], P(None, None, None, 'stn')
- residual: float32 [2, 4, 32, 256, 256], P(None, None, 'chan', 'stn')
The draws below stay inside these ranges and needn't reach their ends.
Inputs may be any that keep to these rules, and one draw needn't show every extreme that they name: `catalogue`: rows: direction cosines l and m within -0.4 to 0.4, Stokes I from 0.02 to 1, Stokes Q, U and V each at most 0.3 I in size, spectral index from -1.5 to -0.5. `cluster_ids`: each of the 1024 catalogue entries appears exactly once. Direction d uses the first counts[d] slots of its row of cluster_ids; some direction uses all 64. `true_gains`: real parts of the diagonal entries lie in 0.5 to 1.5; every other entry lies in -0.5 to 0.5. `start_gains`: real parts of the diagonal entries lie in 0.8 to 1.2; every other entry lies in -0.5 to 0.5.
All inputs are finite; a program needn't handle non-finite values. No bound on the sum of `flag_mask` on one device may be relied on, other than what follows from the above.
Results may differ from the reference program's by a relative error of at most 0.0003.
Values sent between devices are 32-bit elements; how exact they have to be, the bound alone decides.
A program may use at most 128 MiB of HBM per device.

```python
import math
import jax
import jax.numpy as jnp
from jax import lax

DIRS = 16
KMAX = 64
ITERS = 3
NST = 256
NCH = 32
CAT = 1024


def jones_draw(key, diag_low, diag_high, spread):
    subkeys = jax.random.split(key, 2)
    shape_all = (2, 4, DIRS, NST)
    others = jnp.clip(spread * jax.random.normal(subkeys[0], shape_all, jnp.float32), -0.5, 0.5)
    diagonal = jax.random.uniform(subkeys[1], shape_all, jnp.float32, diag_low, diag_high)
    entry_index = jnp.arange(4)[None, :, None, None]
    part_index = jnp.arange(2)[:, None, None, None]
    on_diagonal = ((entry_index == 0) | (entry_index == 3)) & (part_index == 0)
    return jnp.where(on_diagonal, diagonal, others)


def draw_true_gains(key, part):
    return jones_draw(jax.random.fold_in(key, 11), 0.5, 1.5, 0.25)


def draw_start_gains(key, part):
    return jones_draw(jax.random.fold_in(key, 12), 0.8, 1.2, 0.1)


def draw_catalogue(key, part):
    subkeys = jax.random.split(jax.random.fold_in(key, 13), 4)
    direction = jax.random.uniform(subkeys[0], (2, CAT), jnp.float32, -0.3, 0.3)
    flux = jnp.exp(jax.random.uniform(subkeys[1], (CAT,), jnp.float32, jnp.log(0.05), jnp.log(0.5)))
    fraction = jnp.clip(0.1 * jax.random.normal(subkeys[2], (3, CAT), jnp.float32), -0.3, 0.3)
    spectral = jax.random.uniform(subkeys[3], (CAT,), jnp.float32, -1.2, -0.7)
    return jnp.concatenate([direction, flux[None], flux[None] * fraction, spectral[None]], axis=0)


def draw_cluster_ids(key, part):
    return jax.random.permutation(jax.random.fold_in(key, 21), CAT).reshape(DIRS, KMAX).astype(jnp.int32)


def draw_counts(key, part):
    subkeys = jax.random.split(jax.random.fold_in(key, 22), 2)
    lengths = jax.random.randint(subkeys[0], (DIRS,), KMAX // 4, KMAX + 1)
    fullest = jax.random.randint(subkeys[1], (), 0, DIRS)
    return jnp.where(jnp.arange(DIRS) == fullest, KMAX, lengths).astype(jnp.int32)


def set_ends(entries, own_key, low, high):
    longest = entries.shape.index(max(entries.shape))
    spots = []
    for shift in (0, 1):
        where = [jax.random.randint(jax.random.fold_in(own_key, axis), (), 0, length) for axis, length in enumerate(entries.shape)]
        where[longest] = (where[longest] + shift) % entries.shape[longest]
        spots.append(tuple(where))
    return entries.at[spots[0]].set(low).at[spots[1]].set(high)


def block_levels(own_key, dims, cuts, low, largest):
    def one(axis_at, parts):
        draws = jax.random.uniform(jax.random.fold_in(jax.random.fold_in(own_key, 6), axis_at), (parts,), jnp.float32, low / len(cuts), largest / len(cuts))
        return jnp.repeat(jnp.exp(draws), dims[axis_at] // parts).reshape((-1,) + (1,) * (len(dims) - axis_at - 1))

    gain = one(*cuts[0])
    for cut in cuts[1:]:
        gain = gain * one(*cut)
    return gain


def noise(key, extent, width, most, cuts=(), kind=jnp.bfloat16):
    entries = jax.random.normal(key, extent, jnp.float32) * width
    if len(cuts) > 0:
        entries = block_levels(key, extent, cuts, -0.22, 0.18) * entries
    return jnp.clip(entries, min=-most, max=most).astype(kind)


def setup_inputs(seed: int = 0) -> dict:
    streams_of = jax.random.split(jax.random.key(seed), 9)
    return {
        "positions": jnp.clip(jax.random.uniform(streams_of[0], (3, NST), jnp.float32, -1.0, 1.0) * block_levels(streams_of[0], (3, NST), ((1, 16),), -0.4, 0.0), -1.0, 1.0),
        "catalogue": draw_catalogue(jax.random.fold_in(streams_of[8], 71), 0),
        "cluster_ids": draw_cluster_ids(jax.random.fold_in(streams_of[8], 71), 0),
        "counts": draw_counts(jax.random.fold_in(streams_of[8], 71), 0),
        "flag_mask": set_ends((jax.random.randint(streams_of[4], (NCH, NST, NST), 0, 10) < 9).astype(jnp.int32), jax.random.fold_in(streams_of[4], 1), 0, 1),
        "thermal_noise": noise(streams_of[5], (2, 4, NCH, NST, NST), 0.5, 3.0, ((2, 32), (3, 16)), jnp.float32),
        "true_gains": draw_true_gains(jax.random.fold_in(streams_of[8], 71), 0),
        "start_gains": draw_start_gains(jax.random.fold_in(streams_of[8], 71), 0),
    }


band_spread = 6.0
ridge_term = 1.0
phase_scale = 2.0 * math.pi * 20.0

def complex_mul(left_real, left_imag, right_real, right_imag):
    return (left_real * right_real - left_imag * right_imag, left_real * right_imag + left_imag * right_real)

def jones_mul(left, right):
    reals = []
    imags = []
    for out_row in range(2):
        for out_col in range(2):
            first_real, first_imag = complex_mul(left[0, 2 * out_row], left[1, 2 * out_row], right[0, out_col], right[1, out_col])
            second_real, second_imag = complex_mul(left[0, 2 * out_row + 1], left[1, 2 * out_row + 1], right[0, 2 + out_col], right[1, 2 + out_col])
            reals.append(first_real + second_real)
            imags.append(first_imag + second_imag)
    return jnp.stack([jnp.stack(reals), jnp.stack(imags)])

def jones_adjoint(matrix):
    swapped = jnp.stack([matrix[:, 0], matrix[:, 2], matrix[:, 1], matrix[:, 3]], axis=1)
    return jnp.stack([swapped[0], -swapped[1]])

def sky_terms(catalogue, cluster_ids, counts):
    chosen = catalogue[:, cluster_ids]
    slots = lax.broadcasted_iota(jnp.int32, cluster_ids.shape, 1)
    active = (slots < counts[:, None]).astype(jnp.float32)
    return (chosen, active)

def station_phase(station_pos, chosen, frequencies):
    depth = jnp.sqrt(1.0 - chosen[0] * chosen[0] - chosen[1] * chosen[1]) - 1.0
    geometry = station_pos[0][None, :, None] * chosen[0][:, None, :] + station_pos[1][None, :, None] * chosen[1][:, None, :] + station_pos[2][None, :, None] * depth[:, None, :]
    return phase_scale * frequencies[:, None, None, None] * geometry[None]

def brightness(chosen, active, frequencies):
    scaled = frequencies[:, None, None] ** chosen[6][None] * active[None]
    real_part = jnp.stack([scaled * (chosen[2] + chosen[3]), scaled * chosen[4], scaled * chosen[4], scaled * (chosen[2] - chosen[3])])
    zero_fill = jnp.zeros_like(scaled)
    imag_part = jnp.stack([zero_fill, scaled * chosen[5], -scaled * chosen[5], zero_fill])
    return (real_part, imag_part)

def near_products(phase_near, bright_real, bright_imag):
    cosine_near = jnp.cos(phase_near)[None]
    sine_near = jnp.sin(phase_near)[None]
    real_side = bright_real[:, :, :, None, :]
    imag_side = bright_imag[:, :, :, None, :]
    return (cosine_near * real_side - sine_near * imag_side, cosine_near * imag_side + sine_near * real_side)

def contract(left, right):
    return jnp.einsum('xcdpk,cdqk->xcdqp', left, right, precision=lax.Precision.HIGHEST)

def far_contract(wide_real, wide_imag, phase_far):
    cosine_far = jnp.cos(phase_far)
    sine_far = jnp.sin(phase_far)
    real_part = contract(wide_real, cosine_far) + contract(wide_imag, sine_far)
    imag_part = contract(wide_imag, cosine_far) - contract(wide_real, sine_far)
    return jnp.stack([real_part, imag_part])

def gain_update(current, numerator, normal):
    upper_diag = normal[0, 0] + ridge_term
    lower_diag = normal[0, 3] + ridge_term
    cross_real = normal[0, 1]
    cross_imag = normal[1, 1]
    determinant = upper_diag * lower_diag - cross_real * cross_real - cross_imag * cross_imag
    zero_fill = jnp.zeros_like(upper_diag)
    inverse = jnp.stack([jnp.stack([lower_diag, -cross_real, -cross_real, upper_diag]), jnp.stack([zero_fill, -cross_imag, cross_imag, zero_fill])]) / determinant
    return 0.5 * (current + jones_mul(numerator, inverse))

def literal_normals(coherent, noise_block, flag_block, true_gains, current, stations):
    weight = flag_block.astype(jnp.float32) * (stations[:, None] != stations[None, :]).astype(jnp.float32)
    product = jones_mul(coherent, jones_adjoint(current[:, :, None, :, :, None]))
    per_direction = jones_mul(current[:, :, None, :, None, :], product)
    predicted = per_direction.sum(axis=3)
    true_part = jones_mul(true_gains[:, :, None, :, None, :], jones_mul(coherent, jones_adjoint(true_gains[:, :, None, :, :, None])))
    observed = noise_block + true_part.sum(axis=3)
    misfit = weight * (observed - predicted)
    remainder = misfit[:, :, :, None] + weight[:, None] * per_direction
    numerator = jones_mul(remainder, jones_adjoint(product)).sum(axis=(2, 4))
    normal = (weight[:, None] * jones_mul(product, jones_adjoint(product))).sum(axis=(2, 4))
    return (numerator, normal, misfit)

def reference(positions, catalogue, cluster_ids, counts, flag_mask, thermal_noise, true_gains, start_gains):
    chosen, active = sky_terms(catalogue, cluster_ids, counts)
    stations = jnp.arange(NST, dtype=jnp.int32)
    frequencies = 1.0 + band_spread * jnp.arange(NCH, dtype=jnp.float32) / NCH
    noise_first = jnp.swapaxes(jnp.moveaxis(thermal_noise, 2, 0), 3, 4)
    flag_turned = jnp.swapaxes(flag_mask, 1, 2)
    current = start_gains
    residual = thermal_noise
    for iteration in range(ITERS):

        def one_channel(totals, inputs):
            noise_one, flag_one, frequency = inputs
            single = frequency[None]
            phase_all = station_phase(positions, chosen, single)
            bright_real, bright_imag = brightness(chosen, active, single)
            wide_real, wide_imag = near_products(phase_all, bright_real, bright_imag)
            coherent = far_contract(wide_real, wide_imag, phase_all)
            numerator, normal, misfit = literal_normals(coherent, noise_one[:, :, None], flag_one[None], true_gains, current, stations)
            return ((totals[0] + numerator, totals[1] + normal), misfit[:, :, 0])
        zero_terms = jnp.zeros_like(start_gains)
        sums, errors = lax.scan(one_channel, (zero_terms, zero_terms), (noise_first, flag_turned, frequencies))
        residual = jnp.swapaxes(jnp.moveaxis(errors, 0, 2), 3, 4)
        current = gain_update(current, sums[0], sums[1])
    return (current, residual)
```

```python
import math

import jax
import jax.numpy as jnp
from jax import lax
from jax.experimental import pallas as pl
from jax.experimental.pallas import tpu as pltpu
from jax.sharding import PartitionSpec as P

ITERS = 3


band_spread = 6.0
ridge_term = 1.0
phase_scale = 2.0 * math.pi * 20.0


def complex_mul(left_real, left_imag, right_real, right_imag):
    return (
        left_real * right_real - left_imag * right_imag,
        left_real * right_imag + left_imag * right_real,
    )


def jones_mul(left, right):
    reals = []
    imags = []
    for out_row in range(2):
        for out_col in range(2):
            first_real, first_imag = complex_mul(
                left[0, 2 * out_row], left[1, 2 * out_row], right[0, out_col], right[1, out_col]
            )
            second_real, second_imag = complex_mul(
                left[0, 2 * out_row + 1],
                left[1, 2 * out_row + 1],
                right[0, 2 + out_col],
                right[1, 2 + out_col],
            )
            reals.append(first_real + second_real)
            imags.append(first_imag + second_imag)
    return jnp.stack([jnp.stack(reals), jnp.stack(imags)])


def jones_mul_adj(left, right):
    reals = []
    imags = []
    for out_row in range(2):
        for out_col in range(2):
            first_real, first_imag = complex_mul(
                left[0, 2 * out_row],
                left[1, 2 * out_row],
                right[0, 2 * out_col],
                -right[1, 2 * out_col],
            )
            second_real, second_imag = complex_mul(
                left[0, 2 * out_row + 1],
                left[1, 2 * out_row + 1],
                right[0, 2 * out_col + 1],
                -right[1, 2 * out_col + 1],
            )
            reals.append(first_real + second_real)
            imags.append(first_imag + second_imag)
    return jnp.stack([jnp.stack(reals), jnp.stack(imags)])


def sky_terms(catalogue, cluster_ids, counts):
    chosen = jnp.take(catalogue, cluster_ids, axis=1)
    slots = lax.broadcasted_iota(jnp.int32, cluster_ids.shape, 1)
    active = (slots < counts[:, None]).astype(jnp.float32)
    return (chosen, active)


def station_phase(station_pos, chosen, frequencies):
    depth = jnp.sqrt(1.0 - chosen[0] * chosen[0] - chosen[1] * chosen[1]) - 1.0
    geometry = (
        station_pos[0][None, :, None] * chosen[0][:, None, :]
        + station_pos[1][None, :, None] * chosen[1][:, None, :]
        + station_pos[2][None, :, None] * depth[:, None, :]
    )
    return phase_scale * frequencies[:, None, None, None] * geometry[None]


def brightness(chosen, active, frequencies):
    scaled = frequencies[:, None, None] ** chosen[6][None] * active[None]
    real_part = jnp.stack(
        [
            scaled * (chosen[2] + chosen[3]),
            scaled * chosen[4],
            scaled * chosen[4],
            scaled * (chosen[2] - chosen[3]),
        ]
    )
    zero_fill = jnp.zeros_like(scaled)
    imag_part = jnp.stack([zero_fill, scaled * chosen[5], -scaled * chosen[5], zero_fill])
    return (real_part, imag_part)


def near_products(phase_near, bright_real, bright_imag):
    cosine_near = jnp.cos(phase_near)[None]
    sine_near = jnp.sin(phase_near)[None]
    real_side = bright_real[:, :, :, None, :]
    imag_side = bright_imag[:, :, :, None, :]
    return (
        cosine_near * real_side - sine_near * imag_side,
        cosine_near * imag_side + sine_near * real_side,
    )


def contract(left, right):
    return jnp.einsum("xcdpk,cdqk->xcdqp", left, right, precision=lax.Precision.HIGHEST)


def far_contract(wide_real, wide_imag, phase_far):
    cosine_far = jnp.cos(phase_far)
    sine_far = jnp.sin(phase_far)
    real_part = contract(wide_real, cosine_far) + contract(wide_imag, sine_far)
    imag_part = contract(wide_imag, cosine_far) - contract(wide_real, sine_far)
    return jnp.stack([real_part, imag_part])


def gain_update(current, numerator, normal):
    upper_diag = normal[0, 0] + ridge_term
    lower_diag = normal[0, 3] + ridge_term
    cross_real = normal[0, 1]
    cross_imag = normal[1, 1]
    determinant = upper_diag * lower_diag - cross_real * cross_real - cross_imag * cross_imag
    zero_fill = jnp.zeros_like(upper_diag)
    inverse = (
        jnp.stack(
            [
                jnp.stack([lower_diag, -cross_real, -cross_real, upper_diag]),
                jnp.stack([zero_fill, -cross_imag, cross_imag, zero_fill]),
            ]
        )
        / determinant
    )
    return 0.5 * (current + jones_mul(numerator, inverse))


MESH = pl.DeviceIdType.MESH


def greet(peers):
    barrier = pltpu.get_barrier_semaphore()
    for peer in peers:
        pl.semaphore_signal(barrier, inc=1, device_id=peer, device_id_type=MESH)
    pl.semaphore_wait(barrier, len(peers))


def start_copy(src, dst, send_sem, recv_sem, peer):
    copy = pltpu.make_async_remote_copy(
        src_ref=src,
        dst_ref=dst,
        send_sem=send_sem,
        recv_sem=recv_sem,
        device_id=peer,
        device_id_type=MESH,
    )
    copy.start()
    return copy


def axis_peers(axis, size):
    me = lax.axis_index(axis)
    return [{axis: lax.rem(me + step, size)} for step in range(1, size)]


def gather_kernel(axis, size, own, every, send_sem, recv_sem, local_sem):
    me = lax.axis_index(axis)
    peers = axis_peers(axis, size)
    greet(peers)
    copies = [
        start_copy(own, every.at[me], send_sem.at[step], recv_sem.at[step], peer)
        for step, peer in enumerate(peers)
    ]
    local = pltpu.make_async_copy(own, every.at[me], local_sem)
    local.start()
    local.wait()
    for copy in copies:
        copy.wait()


def gather(payload, axis, collective_id):
    size = lax.axis_size(axis)
    return pl.pallas_call(
        lambda *refs: gather_kernel(axis, size, *refs),
        out_shape=jax.ShapeDtypeStruct((size,) + payload.shape, payload.dtype),
        in_specs=[pl.BlockSpec(memory_space=pltpu.VMEM)],
        out_specs=pl.BlockSpec(memory_space=pltpu.VMEM),
        scratch_shapes=[
            pltpu.SemaphoreType.DMA((size - 1,)),
            pltpu.SemaphoreType.DMA((size - 1,)),
            pltpu.SemaphoreType.DMA,
        ],
        compiler_params=pltpu.CompilerParams(
            collective_id=collective_id, has_side_effects=True
        ),
    )(payload)


def reduce_kernel(chips, own, total, pair, mine, parts, pair_sem, send_sem, recv_sem):
    index = lax.axis_index("chan")
    chip = index // 2
    core = lax.rem(index, 2)
    sibling = {"chan": chip * 2 + 1 - core}
    half = own.shape[0] // 2
    peers = [
        {"chan": lax.rem(chip + step, chips) * 2 + core} for step in range(1, chips)
    ]
    greet([sibling] + peers)
    away = pl.ds(pl.multiple_of((1 - core) * half, half), half)
    kept = pl.ds(pl.multiple_of(core * half, half), half)
    swap = start_copy(own.at[away], pair, pair_sem.at[0], pair_sem.at[1], sibling)
    swap.wait()
    mine[...] = own[kept, :] + pair[...]
    copies = [
        start_copy(mine, parts.at[chip], send_sem.at[step], recv_sem.at[step], peer)
        for step, peer in enumerate(peers)
    ]
    parts[chip] = mine[...]
    for copy in copies:
        copy.wait()
    result = parts[0]
    for step in range(1, chips):
        result = result + parts[step]
    total[kept, :] = result
    back = start_copy(
        total.at[kept], total.at[kept], pair_sem.at[2], pair_sem.at[3], sibling
    )
    back.wait()


def reduce_all(payload, collective_id):
    chips = lax.axis_size("chan") // 2
    rows, columns = payload.shape
    return pl.pallas_call(
        lambda *refs: reduce_kernel(chips, *refs),
        out_shape=jax.ShapeDtypeStruct(payload.shape, payload.dtype),
        in_specs=[pl.BlockSpec(memory_space=pltpu.VMEM)],
        out_specs=pl.BlockSpec(memory_space=pltpu.VMEM),
        scratch_shapes=[
            pltpu.VMEM((rows // 2, columns), jnp.float32),
            pltpu.VMEM((rows // 2, columns), jnp.float32),
            pltpu.VMEM((chips, rows // 2, columns), jnp.float32),
            pltpu.SemaphoreType.DMA((4,)),
            pltpu.SemaphoreType.DMA((chips - 1,)),
            pltpu.SemaphoreType.DMA((chips - 1,)),
        ],
        compiler_params=pltpu.CompilerParams(
            collective_id=collective_id, has_side_effects=True
        ),
    )(payload)


def visit_groups(payload, block_terms, initial):
    rows, group_size = payload.shape
    flat = payload.reshape(-1)
    lines = -(-flat.shape[0] // 128)
    flat = jnp.pad(flat, (0, lines * 128 - flat.shape[0]))
    every = gather(flat.reshape(lines, 128), "stn", 1 if lines == 16 else 2)
    every = every.reshape(-1, lines * 128)[:, : rows * group_size]
    every = every.reshape(-1, rows, group_size)
    portion = jnp.swapaxes(every, 0, 1).reshape(rows, -1)
    return block_terms(initial, portion, jnp.int32(0))


def on_device(
    positions, catalogue, cluster_ids, counts, flag_mask, thermal_noise, true_gains, start_gains
):
    every_entry = jnp.swapaxes(gather(catalogue, "chan", 3), 0, 1).reshape(catalogue.shape[0], -1)
    chosen, active = sky_terms(every_entry, cluster_ids, counts)
    chan_count = thermal_noise.shape[2]
    group_size = true_gains.shape[3]
    directions = true_gains.shape[2]
    cycle_size = lax.axis_size("stn")
    total_stations = group_size * cycle_size
    channels = lax.axis_index("chan") * chan_count + jnp.arange(chan_count, dtype=jnp.int32)
    frequencies = 1.0 + band_spread * channels.astype(jnp.float32) / (
        chan_count * lax.axis_size("chan")
    )
    group_index = lax.axis_index("stn")
    near_index = group_index * group_size + jnp.arange(group_size, dtype=jnp.int32)
    bright_real, bright_imag = brightness(chosen, active, frequencies)
    wide_real, wide_imag = near_products(
        station_phase(positions, chosen, frequencies), bright_real, bright_imag
    )

    def model_terms(totals, portion, offset):
        members = portion.shape[1]
        far_true = portion[3:].reshape(2, 4, directions, members)
        coherent = far_contract(
            wide_real, wide_imag, station_phase(portion[0:3], chosen, frequencies)
        )
        noise_block = jnp.swapaxes(thermal_noise, 3, 4)
        true_part = jones_mul(
            true_gains[:, :, None, :, None, :],
            jones_mul_adj(coherent, far_true[:, :, None, :, :, None]),
        )
        observed = noise_block + true_part.sum(axis=3)
        return (coherent, observed)

    model_payload = jnp.concatenate(
        [positions, true_gains.reshape(8 * directions, group_size)], axis=0
    )
    model_initial = (
        jnp.zeros((2, 4, chan_count, directions, total_stations, group_size), jnp.float32),
        jnp.zeros((2, 4, chan_count, total_stations, group_size), jnp.float32),
    )
    coherency_all, observed_all = visit_groups(model_payload, model_terms, model_initial)
    current = start_gains
    residual = jnp.zeros((2, 4, chan_count, group_size, total_stations), jnp.float32)
    for iteration in range(ITERS):

        def block_terms(totals, portion, offset):
            members = portion.shape[1]
            far_current = portion.reshape(2, 4, directions, members)
            far_index = jnp.arange(members, dtype=jnp.int32)
            flag_block = jnp.swapaxes(flag_mask, 1, 2)
            weight = flag_block.astype(jnp.float32) * (
                far_index[:, None] != near_index[None, :]
            ).astype(jnp.float32)
            product = jones_mul_adj(coherency_all, far_current[:, :, None, :, :, None])
            predicted = jones_mul(current[:, :, None, :, None, :], product).sum(axis=3)
            misfit = weight * (observed_all - predicted)
            cross_sum = jones_mul_adj(misfit[:, :, :, None], product).sum(axis=(2, 4))
            normal = (weight[:, None] * jones_mul_adj(product, product)).sum(axis=(2, 4))
            residual = jnp.swapaxes(misfit, 3, 4)
            return (cross_sum, normal, residual)

        zero_terms = jnp.zeros_like(current)
        initial = (
            zero_terms,
            zero_terms,
            jnp.zeros((2, 4, chan_count, group_size, total_stations), jnp.float32),
        )
        cross_sum, normal, residual = visit_groups(
            current.reshape(8 * directions, group_size), block_terms, initial
        )
        solve_cross_sum = cross_sum
        solve_normal = normal
        both = jnp.stack([solve_cross_sum, solve_normal])
        both = reduce_all(both.reshape(-1, 128), 4).reshape(both.shape)
        solve_cross_sum, solve_normal = both[0], both[1]
        current = gain_update(
            current, solve_cross_sum + jones_mul(current, solve_normal), solve_normal
        )
    return (current, residual)


def solution(mesh):
    return jax.shard_map(
        on_device,
        mesh=mesh,
        in_specs=(
            P(None, "stn"),
            P(None, "chan"),
            P(),
            P(),
            P("chan", "stn", None),
            P(None, None, "chan", "stn", None),
            P(None, None, None, "stn"),
            P(None, None, None, "stn"),
        ),
        out_specs=(P(None, None, None, "stn"), P(None, None, "chan", "stn", None)),
        check_vma=False,
    )
```

```python
import math

import jax
import jax.numpy as jnp
from jax import lax
from jax.experimental import pallas as pl
from jax.experimental.pallas import tpu as pltpu
from jax.sharding import PartitionSpec as P

ITERS = 3
LANES = 128
MESH = pl.DeviceIdType.MESH

band_spread = 6.0
ridge_term = 1.0
turn_scale = 20.0

SINE = (3.1415926401307073, -5.167710083507893, 2.5500775232145596, -0.5982912856201866, 0.07765766030500078)
COSINE = (
    0.9999999997799042,
    -4.9348021370788056,
    4.0587091595557485,
    -1.3352120030440895,
    0.23493731378565055,
    -0.024396324298134327,
)


def horner(terms, square):
    value = square * terms[-1] + terms[-2]
    for term in terms[-3::-1]:
        value = value * square + term
    return value


def turn_wave(turns):
    rest = turns - jnp.floor(turns + 0.5)
    square = rest * rest
    half_sine = rest * horner(SINE, square)
    half_cosine = horner(COSINE, square)
    twice = half_sine + half_sine
    return 1.0 - twice * half_sine, twice * half_cosine


def split_pair(value):
    high = value.astype(jnp.bfloat16)
    return high, (value - high.astype(jnp.float32)).astype(jnp.bfloat16)


def cmul(a, b):
    return a[0] * b[0] - a[1] * b[1], a[0] * b[1] + a[1] * b[0]


def cmul_conj(a, b):
    return a[0] * b[0] + a[1] * b[1], a[1] * b[0] - a[0] * b[1]


def cadd(a, b):
    return a[0] + b[0], a[1] + b[1]


def mat_mul(left, right):
    return [
        cadd(cmul(left[2 * i], right[j]), cmul(left[2 * i + 1], right[2 + j]))
        for i in range(2)
        for j in range(2)
    ]


def mat_mul_adj(left, right):
    return [
        cadd(cmul_conj(left[2 * i], right[2 * j]), cmul_conj(left[2 * i + 1], right[2 * j + 1]))
        for i in range(2)
        for j in range(2)
    ]


def start_copy(src, dst, send_sem, recv_sem, peer):
    copy = pltpu.make_async_remote_copy(
        src_ref=src,
        dst_ref=dst,
        send_sem=send_sem,
        recv_sem=recv_sem,
        device_id=peer,
        device_id_type=MESH,
    )
    copy.start()
    return copy


def kernel(
    sizes,
    positions,
    catalogue,
    ids,
    counts,
    flags,
    noise,
    true_gains,
    start_gains,
    final,
    residual,
    square,
    onehot,
    own_cat,
    every_cat,
    parts_cat,
    own_place,
    every_place,
    place_rows,
    own_gains,
    every_gains,
    true_far,
    gain_far,
    near_true,
    near_gain,
    coherent,
    product,
    observed,
    predicted,
    weight,
    misfit,
    cross_sum,
    normal,
    pair,
    mine,
    sums,
    fresh,
    spread,
    cat_send,
    cat_recv,
    place_send,
    place_recv,
    gain_send,
    gain_recv,
    pair_send,
    pair_recv,
    sum_send,
    sum_recv,
    fresh_send,
    fresh_recv,
    turn_send,
    turn_recv,
):
    groups, chans, dirs, slots, members, chan_total = sizes
    chips = chans // 2
    group = lax.axis_index("stn")
    channel = lax.axis_index("chan")
    chip = channel // 2
    core = lax.rem(channel, 2)
    stations = groups * members
    entries = chans * catalogue.shape[1]
    half = members // 2

    chan_peers = [{"chan": lax.rem(channel + step, chans)} for step in range(1, chans)]
    stn_peers = [{"stn": lax.rem(group + step, groups)} for step in range(1, groups)]
    sibling = {"chan": chip * 2 + 1 - core}
    chip_peers = [{"chan": lax.rem(chip + step, chips) * 2 + core} for step in range(1, chips)]
    cross_peers = [
        {"stn": lax.rem(group + step, groups), "chan": chip * 2 + 1 - core}
        for step in range(1, groups)
    ]

    barrier = pltpu.get_barrier_semaphore()
    greeted = chan_peers + stn_peers + cross_peers
    for peer in greeted:
        pl.semaphore_signal(barrier, inc=1, device_id=peer, device_id_type=MESH)

    square[...] = jnp.zeros_like(square)
    for copy_at in range(3):
        square[32 * copy_at : 32 * copy_at + 7, 0 : catalogue.shape[1]] = catalogue[...]
    own_cat[...] = jnp.transpose(square[...])[0 : catalogue.shape[1], :]
    square[...] = jnp.zeros_like(square)
    square[:, 0:members] = true_gains[...]
    own_gains[:, 0:LANES] = jnp.transpose(square[...])[0:members, :]
    square[:, 0:members] = start_gains[...]
    own_gains[:, LANES : 2 * LANES] = jnp.transpose(square[...])[0:members, :]
    own_place[...] = jnp.zeros_like(own_place)
    own_place[0:3, 0:members] = positions[...]

    pl.semaphore_wait(barrier, len(greeted))

    cat_copies = [
        start_copy(own_cat, every_cat.at[channel], cat_send.at[i], cat_recv.at[i], peer)
        for i, peer in enumerate(chan_peers)
    ]
    place_copies = [
        start_copy(own_place, every_place.at[group], place_send.at[i], place_recv.at[i], peer)
        for i, peer in enumerate(stn_peers)
    ]
    gain_copies = [
        start_copy(own_gains, every_gains.at[group], gain_send.at[i], gain_recv.at[i], peer)
        for i, peer in enumerate(stn_peers)
    ]
    every_cat[channel] = own_cat[...]
    every_place[group] = own_place[...]
    every_gains[group] = own_gains[...]
    near_true[...] = own_gains[:, 0:LANES]
    near_gain[...] = own_gains[:, LANES : 2 * LANES]

    near_index = group * members + lax.broadcasted_iota(jnp.int32, (members, stations), 0)
    far_index = lax.broadcasted_iota(jnp.int32, (members, stations), 1)
    weight[...] = jnp.where(near_index != far_index, flags[...].astype(jnp.float32), 0.0)

    square[...] = jnp.zeros_like(square)
    square[0:dirs, 0:slots] = ids[...].astype(jnp.float32)
    ids_turned = jnp.transpose(square[...])[0:slots, :]
    square[0:slots, :] = ids_turned
    lane_column = lax.broadcasted_iota(jnp.int32, (slots, LANES), 1)
    entry_at = lax.broadcasted_iota(jnp.int32, (slots, entries), 1).astype(jnp.float32)

    def mark(direction, carry):
        named = jnp.sum(
            jnp.where(lane_column == direction, square[0:slots, :], 0.0), axis=1, keepdims=True
        )
        onehot[direction] = jnp.where(named == entry_at, 1.0, 0.0).astype(jnp.bfloat16)
        return carry

    lax.fori_loop(0, dirs, mark, 0)

    frequency = 1.0 + band_spread * channel.astype(jnp.float32) / chan_total
    log_frequency = jnp.log(jnp.full((1, LANES), frequency, jnp.float32))
    lane_row = lax.broadcasted_iota(jnp.int32, (1, LANES), 1)
    imag_lane = lane_row >= 4 * members
    entry_lane = lax.rem(lane_row // members, 4)

    for copy in cat_copies:
        copy.wait_recv()
    whole = every_cat[...].reshape(entries, LANES)
    first = whole.astype(jnp.bfloat16).astype(jnp.float32)
    second = (whole - first).astype(jnp.bfloat16).astype(jnp.float32)
    third = whole - first - second
    wide_lane = lax.broadcasted_iota(jnp.int32, (entries, LANES), 1)
    parts_cat[...] = jnp.where(
        wide_lane < 32, first, jnp.where(wide_lane < 64, second, third)
    ).astype(jnp.bfloat16)

    for copy in place_copies:
        copy.wait_recv()
    per_row = LANES // members
    scale = turn_scale * frequency
    for block in range(groups // per_row):
        joined = every_place[block * per_row]
        for at in range(1, per_row):
            joined = joined + pltpu.roll(every_place[block * per_row + at], members * at, 1)
        place_rows[:, block * LANES : (block + 1) * LANES] = joined * scale
    tiled = own_place[...] * scale
    for shift in (members, 2 * members, 4 * members):
        tiled = tiled + pltpu.roll(tiled, shift, 1)

    def model(direction, carry):
        picked = lax.dot_general(
            onehot[direction],
            parts_cat[...],
            (((1,), (0,)), ((), ())),
            preferred_element_type=jnp.float32,
        )
        picked = picked + pltpu.roll(picked, LANES - 32, 1) + pltpu.roll(picked, LANES - 64, 1)

        def column(at):
            return jnp.broadcast_to(picked[:, at : at + 1], (slots, LANES))

        cos_l, cos_m = column(0), column(1)
        depth = jnp.sqrt(1.0 - cos_l * cos_l - cos_m * cos_m) - 1.0
        rows = lax.broadcasted_iota(jnp.int32, (slots, LANES), 0)
        scaled = jnp.where(
            rows < counts[direction], jnp.exp(column(6) * log_frequency), 0.0
        )
        stokes_i, stokes_q, stokes_u, stokes_v = (scaled * column(at) for at in (2, 3, 4, 5))
        bright_real = jnp.where(
            entry_lane == 0,
            stokes_i + stokes_q,
            jnp.where(entry_lane == 3, stokes_i - stokes_q, stokes_u),
        )
        bright_imag = jnp.where(
            entry_lane == 1, stokes_v, jnp.where(entry_lane == 2, -stokes_v, 0.0)
        )
        near_cos, near_sin = turn_wave(
            tiled[0:1, :] * cos_l + tiled[1:2, :] * cos_m + tiled[2:3, :] * depth
        )
        real_side = jnp.where(imag_lane, bright_imag, bright_real)
        imag_side = jnp.where(imag_lane, bright_real, -bright_imag)
        upper = real_side * near_cos + imag_side * near_sin
        lower = real_side * near_sin - imag_side * near_cos
        near_side = jnp.transpose(jnp.concatenate([upper, lower], axis=0))
        near_high, near_low = split_pair(near_side)
        blocks = []
        for block in range(stations // LANES):
            lanes = slice(block * LANES, (block + 1) * LANES)
            blocks.append(
                jnp.concatenate(
                    turn_wave(
                        place_rows[0:1, lanes] * cos_l
                        + place_rows[1:2, lanes] * cos_m
                        + place_rows[2:3, lanes] * depth
                    ),
                    axis=0,
                )
            )
        far_high, far_low = split_pair(jnp.concatenate(blocks, axis=1))

        def times(left, right):
            return jnp.dot(left, right, preferred_element_type=jnp.float32)

        result = times(near_high, far_high) + (
            times(near_low, far_high) + times(near_high, far_low)
        )
        coherent[direction] = result.reshape(8, members, stations)
        return carry

    lax.fori_loop(0, dirs, model, 0)

    for copy in gain_copies:
        copy.wait_recv()
    turned = jnp.transpose(every_gains[:, :, 0:LANES].reshape(stations, LANES))
    true_far[...] = turned
    turned = jnp.transpose(every_gains[:, :, LANES : 2 * LANES].reshape(stations, LANES))
    gain_far[...] = turned

    near_lane = lax.broadcasted_iota(jnp.int32, (members, LANES), 1)
    halves = [slice(at * LANES, (at + 1) * LANES) for at in range(stations // LANES)]

    def near_matrix(ref, direction):
        whole_near = ref[...]
        return [
            tuple(
                jnp.sum(
                    jnp.where(near_lane == (part * 4 + entry) * dirs + direction, whole_near, 0.0),
                    axis=1,
                    keepdims=True,
                )
                for part in range(2)
            )
            for entry in range(4)
        ]

    def far_matrix(ref, direction, lanes):
        return [
            tuple(
                ref[pl.ds((part * 4 + entry) * dirs + direction, 1), :][:, lanes]
                for part in range(2)
            )
            for entry in range(4)
        ]

    def planes(ref, lanes, *lead):
        return [
            tuple(ref[(*lead, part * 4 + entry, slice(None), lanes)] for part in range(2))
            for entry in range(4)
        ]

    def add_planes(ref, lanes, matrix):
        for entry in range(4):
            for part in range(2):
                ref[part * 4 + entry, :, lanes] += matrix[entry][part]

    observed[...] = noise[...]

    def observe(direction, carry):
        near = near_matrix(near_true, direction)
        for lanes in halves:
            spun = mat_mul_adj(
                planes(coherent, lanes, direction), far_matrix(true_far, direction, lanes)
            )
            add_planes(observed, lanes, mat_mul(near, spun))
        return carry

    lax.fori_loop(0, dirs, observe, 0)

    def predict(direction, carry):
        near = near_matrix(near_gain, direction)
        totals = [0.0] * 4
        for lanes in halves:
            spun = mat_mul_adj(
                planes(coherent, lanes, direction), far_matrix(gain_far, direction, lanes)
            )
            add_planes(predicted, lanes, mat_mul(near, spun))
            for entry in range(4):
                for part in range(2):
                    product[direction, part * 4 + entry, :, lanes] = spun[entry][part]
            weighted = [
                tuple(weight[:, lanes] * value for value in spun[entry]) for entry in range(2)
            ]
            first_power = sum(
                weighted[entry][part] * spun[entry][part]
                for entry in range(2)
                for part in range(2)
            )
            second_power = weight[:, lanes] * sum(
                spun[entry][part] * spun[entry][part] for entry in (2, 3) for part in range(2)
            )
            cross = cadd(cmul_conj(weighted[0], spun[2]), cmul_conj(weighted[1], spun[3]))
            for at, value in enumerate((first_power, second_power, *cross)):
                totals[at] = totals[at] + value
        collected = normal[...]
        for at in range(4):
            collected = jnp.where(
                near_lane == at * dirs + direction,
                jnp.sum(totals[at], axis=1, keepdims=True),
                collected,
            )
        normal[...] = collected
        return carry

    def correlate(direction, carry):
        totals = [[0.0, 0.0] for entry in range(4)]
        for lanes in halves:
            found = mat_mul_adj(planes(misfit, lanes), planes(product, lanes, direction))
            for entry in range(4):
                for part in range(2):
                    totals[entry][part] = totals[entry][part] + found[entry][part]
        collected = cross_sum[...]
        for entry in range(4):
            for part in range(2):
                collected = jnp.where(
                    near_lane == (part * 4 + entry) * dirs + direction,
                    jnp.sum(totals[entry][part], axis=1, keepdims=True),
                    collected,
                )
        cross_sum[...] = collected
        return carry

    pending = cat_copies + place_copies + gain_copies
    kept = pl.ds(pl.multiple_of(core * half, half), half)
    away = pl.ds(pl.multiple_of((1 - core) * half, half), half)
    cross_sum[...] = jnp.zeros_like(cross_sum)
    normal[...] = jnp.zeros_like(normal)

    for iteration in range(ITERS):
        predicted[...] = jnp.zeros_like(predicted)
        lax.fori_loop(0, dirs, predict, 0)
        for plane in range(8):
            misfit[plane] = weight[...] * (observed[plane] - predicted[plane])
        lax.fori_loop(0, dirs, correlate, 0)
        mine[iteration, :, 0:LANES] = cross_sum[...]
        mine[iteration, :, LANES : 2 * LANES] = normal[...]

        swap = start_copy(
            mine.at[iteration, away],
            pair.at[iteration],
            pair_send.at[iteration],
            pair_recv.at[iteration],
            sibling,
        )
        swap.wait_recv()
        pending.append(swap)
        sums[iteration, chip] = mine[iteration, kept, :] + pair[iteration]
        copies = [
            start_copy(
                sums.at[iteration, chip],
                sums.at[iteration, chip],
                sum_send.at[iteration, i],
                sum_recv.at[iteration, i],
                peer,
            )
            for i, peer in enumerate(chip_peers)
        ]
        for copy in copies:
            copy.wait_recv()
        pending += copies
        total = sums[iteration, 0]
        for at in range(1, chips):
            total = total + sums[iteration, at]

        def lanes_of(array, at):
            return pltpu.roll(array, LANES - at * dirs, 1) if at else array

        gains = near_gain[kept, :]
        current = [
            tuple(lanes_of(gains, part * 4 + entry) for part in range(2)) for entry in range(4)
        ]
        gathered = [
            tuple(lanes_of(total[:, 0:LANES], part * 4 + entry) for part in range(2))
            for entry in range(4)
        ]
        upper_diag, lower_diag, cross_real, cross_imag = (
            lanes_of(total[:, LANES : 2 * LANES], at) for at in range(4)
        )
        nothing = jnp.zeros_like(upper_diag)
        hermitian = [
            (upper_diag, nothing),
            (cross_real, cross_imag),
            (cross_real, -cross_imag),
            (lower_diag, nothing),
        ]
        numerator = [
            cadd(a, b) for a, b in zip(gathered, mat_mul(current, hermitian))
        ]
        upper_diag = upper_diag + ridge_term
        lower_diag = lower_diag + ridge_term
        determinant = (
            upper_diag * lower_diag - cross_real * cross_real - cross_imag * cross_imag
        )
        inverse = [
            (lower_diag / determinant, nothing),
            (-cross_real / determinant, -cross_imag / determinant),
            (-cross_real / determinant, cross_imag / determinant),
            (upper_diag / determinant, nothing),
        ]
        estimate = mat_mul(numerator, inverse)
        updated = jnp.zeros((half, LANES), jnp.float32)
        for entry in range(4):
            for part in range(2):
                at = part * 4 + entry
                value = 0.5 * (current[entry][part] + estimate[entry][part])
                moved = pltpu.roll(value, at * dirs, 1) if at else value
                inside = near_lane[0:half] // dirs == at
                updated = jnp.where(inside, moved, updated)
        fresh[iteration] = updated

        last = iteration == ITERS - 1
        here = spread.at[iteration, group, core]
        spread[iteration, group, core] = updated
        swap = start_copy(
            fresh.at[iteration], here, turn_send.at[iteration], turn_recv.at[iteration], sibling
        )
        copies = [swap]
        if not last:
            for way, peers in enumerate((stn_peers, cross_peers)):
                copies += [
                    start_copy(
                        fresh.at[iteration],
                        here,
                        fresh_send.at[iteration, way, i],
                        fresh_recv.at[iteration, way, i],
                        peer,
                    )
                    for i, peer in enumerate(peers)
                ]
        for copy in copies:
            copy.wait_recv()
        pending += copies
        near_gain[...] = spread[iteration, group].reshape(members, LANES)
        if not last:
            turned = jnp.transpose(spread[iteration].reshape(stations, LANES))
            gain_far[...] = turned

    residual[...] = misfit[...]
    square[0:members, :] = near_gain[...]
    final[...] = jnp.transpose(square[...])[:, 0:members]
    for copy in pending:
        copy.wait_send()


def on_device(
    positions, catalogue, cluster_ids, counts, flag_mask, thermal_noise, true_gains, start_gains
):
    groups = lax.axis_size("stn")
    chans = lax.axis_size("chan")
    dirs, slots = cluster_ids.shape
    members = positions.shape[1]
    stations = groups * members
    entries = chans * catalogue.shape[1]
    chips = chans // 2
    half = members // 2
    sizes = (groups, chans, dirs, slots, members, float(chans))
    f32 = jnp.float32
    vmem = pl.BlockSpec(memory_space=pltpu.VMEM)
    smem = pl.BlockSpec(memory_space=pltpu.SMEM)
    dma = pltpu.SemaphoreType.DMA

    final, residual = pl.pallas_call(
        lambda *refs: kernel(sizes, *refs),
        name="calibrate",
        out_shape=(
            jax.ShapeDtypeStruct((8 * dirs, members), f32),
            jax.ShapeDtypeStruct((8, members, stations), f32),
        ),
        in_specs=[vmem, vmem, vmem, smem, vmem, vmem, vmem, vmem],
        out_specs=(vmem, vmem),
        scratch_shapes=[
            pltpu.VMEM((LANES, LANES), f32),
            pltpu.VMEM((dirs, slots, entries), jnp.bfloat16),
            pltpu.VMEM((catalogue.shape[1], LANES), f32),
            pltpu.VMEM((chans, catalogue.shape[1], LANES), f32),
            pltpu.VMEM((entries, LANES), jnp.bfloat16),
            pltpu.VMEM((8, LANES), f32),
            pltpu.VMEM((groups, 8, LANES), f32),
            pltpu.VMEM((8, stations), f32),
            pltpu.VMEM((members, 2 * LANES), f32),
            pltpu.VMEM((groups, members, 2 * LANES), f32),
            pltpu.VMEM((8 * dirs, stations), f32),
            pltpu.VMEM((8 * dirs, stations), f32),
            pltpu.VMEM((members, LANES), f32),
            pltpu.VMEM((members, LANES), f32),
            pltpu.VMEM((dirs, 8, members, stations), f32),
            pltpu.VMEM((dirs, 8, members, stations), f32),
            pltpu.VMEM((8, members, stations), f32),
            pltpu.VMEM((8, members, stations), f32),
            pltpu.VMEM((members, stations), f32),
            pltpu.VMEM((8, members, stations), f32),
            pltpu.VMEM((members, LANES), f32),
            pltpu.VMEM((members, LANES), f32),
            pltpu.VMEM((ITERS, half, 2 * LANES), f32),
            pltpu.VMEM((ITERS, members, 2 * LANES), f32),
            pltpu.VMEM((ITERS, chips, half, 2 * LANES), f32),
            pltpu.VMEM((ITERS, half, LANES), f32),
            pltpu.VMEM((ITERS, groups, 2, half, LANES), f32),
            dma((chans - 1,)),
            dma((chans - 1,)),
            dma((groups - 1,)),
            dma((groups - 1,)),
            dma((groups - 1,)),
            dma((groups - 1,)),
            dma((ITERS,)),
            dma((ITERS,)),
            dma((ITERS, chips - 1)),
            dma((ITERS, chips - 1)),
            dma((ITERS, 2, groups - 1)),
            dma((ITERS, 2, groups - 1)),
            dma((ITERS,)),
            dma((ITERS,)),
        ],
        compiler_params=pltpu.CompilerParams(
            collective_id=1, has_side_effects=True, vmem_limit_bytes=40 << 20
        ),
    )(
        positions,
        catalogue,
        cluster_ids,
        counts,
        flag_mask.reshape(members, stations),
        thermal_noise.reshape(8, members, stations),
        true_gains.reshape(8 * dirs, members),
        start_gains.reshape(8 * dirs, members),
    )
    return (final.reshape(true_gains.shape), residual.reshape(thermal_noise.shape))


def solution(mesh):
    return jax.shard_map(
        on_device,
        mesh=mesh,
        in_specs=(
            P(None, "stn"),
            P(None, "chan"),
            P(),
            P(),
            P("chan", "stn", None),
            P(None, None, "chan", "stn", None),
            P(None, None, None, "stn"),
            P(None, None, None, "stn"),
        ),
        out_specs=(P(None, None, None, "stn"), P(None, None, "chan", "stn", None)),
        check_vma=False,
    )
```

```python
import math

import jax
import jax.numpy as jnp
from jax import lax
from jax.experimental import pallas as pl
from jax.experimental.pallas import tpu as pltpu
from jax.sharding import PartitionSpec as P

ITERS = 3
LANES = 128
MESH = pl.DeviceIdType.MESH

band_spread = 6.0
ridge_term = 1.0
turn_scale = 20.0

SINE = (3.1415926401307073, -5.167710083507893, 2.5500775232145596, -0.5982912856201866, 0.07765766030500078)
COSINE = (
    0.9999999997799042,
    -4.9348021370788056,
    4.0587091595557485,
    -1.3352120030440895,
    0.23493731378565055,
    -0.024396324298134327,
)


def horner(terms, square):
    value = square * terms[-1] + terms[-2]
    for term in terms[-3::-1]:
        value = value * square + term
    return value


def turn_wave(turns):
    rest = turns - jnp.floor(turns + 0.5)
    square = rest * rest
    half_sine = rest * horner(SINE, square)
    half_cosine = horner(COSINE, square)
    twice = half_sine + half_sine
    return 1.0 - twice * half_sine, twice * half_cosine


def split_pair(value):
    high = value.astype(jnp.bfloat16)
    return high, (value - high.astype(jnp.float32)).astype(jnp.bfloat16)


def cmul(a, b):
    return a[0] * b[0] - a[1] * b[1], a[0] * b[1] + a[1] * b[0]


def cmul_conj(a, b):
    return a[0] * b[0] + a[1] * b[1], a[1] * b[0] - a[0] * b[1]


def cadd(a, b):
    return a[0] + b[0], a[1] + b[1]


def mat_mul(left, right):
    return [
        cadd(cmul(left[2 * i], right[j]), cmul(left[2 * i + 1], right[2 + j]))
        for i in range(2)
        for j in range(2)
    ]


def mat_mul_adj(left, right):
    return [
        cadd(cmul_conj(left[2 * i], right[2 * j]), cmul_conj(left[2 * i + 1], right[2 * j + 1]))
        for i in range(2)
        for j in range(2)
    ]


def start_copy(src, dst, send_sem, recv_sem, peer):
    copy = pltpu.make_async_remote_copy(
        src_ref=src,
        dst_ref=dst,
        send_sem=send_sem,
        recv_sem=recv_sem,
        device_id=peer,
        device_id_type=MESH,
    )
    copy.start()
    return copy


def far_first(count, stride):
    ring = count // 2
    moves = [(row, step) for row in range(2) for step in range(ring) if row or step]
    return sorted(moves, key=lambda move: -(move[0] * stride + min(move[1], ring - move[1])))


def moved_to(index, move, count):
    ring = count // 2
    row = lax.rem(index // ring + move[0], 2)
    return row * ring + lax.rem(lax.rem(index, ring) + move[1], ring)


def kernel(
    sizes,
    positions_in,
    catalogue_in,
    ids_in,
    counts_in,
    flags_in,
    noise_in,
    true_in,
    start_in,
    final,
    residual,
    positions,
    catalogue,
    ids,
    counts,
    flags,
    true_gains,
    start_gains,
    load_sem,
    square,
    own_cat,
    sibling_cat,
    every_cat,
    parts_cat,
    cat_pair_sem,
    own_place,
    every_place,
    place_rows,
    own_gains,
    every_gains,
    true_far,
    gain_far,
    near_true,
    near_gain,
    coherent,
    product,
    observed,
    predicted,
    weight,
    misfit,
    cross_sum,
    normal,
    pair,
    mine,
    sums,
    fresh,
    spread,
    cat_send,
    cat_recv,
    place_send,
    place_recv,
    gain_send,
    gain_recv,
    pair_send,
    pair_recv,
    sum_send,
    sum_recv,
    fresh_send,
    fresh_recv,
    turn_send,
    turn_recv,
):
    groups, chans, dirs, slots, members, chan_total = sizes
    chips = chans // 2
    group = lax.axis_index("stn")
    channel = lax.axis_index("chan")
    chip = channel // 2
    core = lax.rem(channel, 2)
    stations = groups * members
    half = members // 2

    loads = [
        pltpu.make_async_copy(source, target, load_sem.at[i])
        for i, (source, target) in enumerate(
            (
                (catalogue_in, catalogue),
                (positions_in, positions),
                (true_in, true_gains),
                (start_in, start_gains),
                (ids_in, ids),
                (counts_in, counts),
                (flags_in, flags),
                (noise_in, observed),
            )
        )
    ]
    for load in loads:
        load.start()

    sibling = {"chan": chip * 2 + 1 - core}
    chip_moves = [moved_to(chip, move, chips) for move in far_first(chips, 2)]
    chip_peers = [{"chan": peer * 2 + core} for peer in chip_moves]
    group_moves = [moved_to(group, move, groups) for move in far_first(groups, 1)]
    stn_peers = [{"stn": peer} for peer in group_moves]
    cross_peers = [{"stn": peer, "chan": chip * 2 + 1 - core} for peer in group_moves]

    barrier = pltpu.get_barrier_semaphore()
    greeted = chip_peers + stn_peers + cross_peers + [sibling]
    for peer in greeted:
        pl.semaphore_signal(barrier, inc=1, device_id=peer, device_id_type=MESH)

    cat_width = catalogue.shape[1]
    for load in loads[0:2]:
        load.wait()
    own_cat[...] = jnp.zeros_like(own_cat)
    own_cat[0:7, 0:cat_width] = catalogue[...]
    own_cat[...] = jnp.where(core == 0, own_cat[...], pltpu.roll(own_cat[...], cat_width, 1))
    own_place[...] = jnp.zeros_like(own_place)
    own_place[0:3, 0:members] = positions[...]
    for load in loads[2:4]:
        load.wait()
    square[...] = jnp.zeros_like(square)
    square[:, 0:members] = true_gains[...]
    own_gains[:, 0:LANES] = jnp.transpose(square[...])[0:members, :]
    square[:, 0:members] = start_gains[...]
    own_gains[:, LANES : 2 * LANES] = jnp.transpose(square[...])[0:members, :]

    pl.semaphore_wait(barrier, len(greeted))

    cat_swap = start_copy(own_cat, sibling_cat, cat_pair_sem.at[0], cat_pair_sem.at[1], sibling)
    place_copies = [
        start_copy(own_place, every_place.at[group], place_send.at[i], place_recv.at[i], peer)
        for i, peer in enumerate(stn_peers)
    ]
    cat_swap.wait_recv()
    every_cat[chip] = own_cat[...] + sibling_cat[...]
    cat_copies = [
        start_copy(
            every_cat.at[chip], every_cat.at[chip], cat_send.at[i], cat_recv.at[i], peer
        )
        for i, peer in enumerate(chip_peers)
    ]
    gain_copies = [
        start_copy(own_gains, every_gains.at[group], gain_send.at[i], gain_recv.at[i], peer)
        for i, peer in enumerate(stn_peers)
    ]
    every_place[group] = own_place[...]
    every_gains[group] = own_gains[...]
    near_true[...] = own_gains[:, 0:LANES]
    near_gain[...] = own_gains[:, LANES : 2 * LANES]
    for load in loads[4:]:
        load.wait()

    near_index = group * members + lax.broadcasted_iota(jnp.int32, (members, stations), 0)
    far_index = lax.broadcasted_iota(jnp.int32, (members, stations), 1)
    weight[...] = jnp.where(near_index != far_index, flags[...].astype(jnp.float32), 0.0)

    square[...] = jnp.zeros_like(square)
    square[0:dirs, 0:slots] = ids[...].astype(jnp.float32)
    square[...] = jnp.transpose(square[...])
    lane_column = lax.broadcasted_iota(jnp.int32, (slots, LANES), 1)
    lane_value = lane_column.astype(jnp.float32)

    frequency = 1.0 + band_spread * channel.astype(jnp.float32) / chan_total
    log_frequency = jnp.log(jnp.full((1, LANES), frequency, jnp.float32))
    lane_row = lax.broadcasted_iota(jnp.int32, (1, LANES), 1)
    imag_lane = lane_row >= 4 * members
    entry_lane = lax.rem(lane_row // members, 4)

    for copy in cat_copies:
        copy.wait_recv()
    stacked = jnp.concatenate(
        [
            every_cat[2 * at] + pltpu.roll(every_cat[2 * at + 1], 2 * cat_width, 1)
            for at in range(chips // 2)
        ]
        + [jnp.zeros((LANES - 4 * chips, LANES), jnp.float32)],
        axis=0,
    )
    whole = jnp.transpose(stacked)
    first = whole.astype(jnp.bfloat16).astype(jnp.float32)
    second = (whole - first).astype(jnp.bfloat16).astype(jnp.float32)
    third = whole - first - second
    parts_cat[:, 0:LANES] = (first + pltpu.roll(second, 64, 1)).astype(jnp.bfloat16)
    parts_cat[:, LANES : 2 * LANES] = third.astype(jnp.bfloat16)

    for copy in place_copies:
        copy.wait_recv()
    per_row = LANES // members
    scale = turn_scale * frequency
    for block in range(groups // per_row):
        joined = every_place[block * per_row]
        for at in range(1, per_row):
            joined = joined + pltpu.roll(every_place[block * per_row + at], members * at, 1)
        place_rows[:, block * LANES : (block + 1) * LANES] = joined * scale
    tiled = own_place[...] * scale
    for shift in (members, 2 * members, 4 * members):
        tiled = tiled + pltpu.roll(tiled, shift, 1)

    def model(direction, carry):
        named = jnp.sum(
            jnp.where(lane_column == direction, square[0:slots, :], 0.0), axis=1, keepdims=True
        )
        block_of = jnp.floor(named * (1.0 / LANES))
        within = named - block_of * LANES
        picked = jnp.dot(
            jnp.where(within == lane_value, 1.0, 0.0).astype(jnp.bfloat16),
            parts_cat[...],
            preferred_element_type=jnp.float32,
        )
        picked = (
            picked[:, 0:LANES]
            + pltpu.roll(picked[:, 0:LANES], 64, 1)
            + picked[:, LANES : 2 * LANES]
        )
        lane_wanted = block_of * 8.0

        def column(at):
            return jnp.broadcast_to(
                jnp.sum(
                    jnp.where(lane_value == lane_wanted + float(at), picked, 0.0),
                    axis=1,
                    keepdims=True,
                ),
                (slots, LANES),
            )

        cos_l, cos_m = column(0), column(1)
        depth = jnp.sqrt(1.0 - cos_l * cos_l - cos_m * cos_m) - 1.0
        rows = lax.broadcasted_iota(jnp.int32, (slots, LANES), 0)
        scaled = jnp.where(
            rows < counts[direction], jnp.exp(column(6) * log_frequency), 0.0
        )
        stokes_i, stokes_q, stokes_u, stokes_v = (scaled * column(at) for at in (2, 3, 4, 5))
        bright_real = jnp.where(
            entry_lane == 0,
            stokes_i + stokes_q,
            jnp.where(entry_lane == 3, stokes_i - stokes_q, stokes_u),
        )
        bright_imag = jnp.where(
            entry_lane == 1, stokes_v, jnp.where(entry_lane == 2, -stokes_v, 0.0)
        )
        near_cos, near_sin = turn_wave(
            tiled[0:1, :] * cos_l + tiled[1:2, :] * cos_m + tiled[2:3, :] * depth
        )
        real_side = jnp.where(imag_lane, bright_imag, bright_real)
        imag_side = jnp.where(imag_lane, bright_real, -bright_imag)
        upper = real_side * near_cos + imag_side * near_sin
        lower = real_side * near_sin - imag_side * near_cos
        near_side = jnp.transpose(jnp.concatenate([upper, lower], axis=0))
        near_high, near_low = split_pair(near_side)
        blocks = []
        for block in range(stations // LANES):
            lanes = slice(block * LANES, (block + 1) * LANES)
            blocks.append(
                jnp.concatenate(
                    turn_wave(
                        place_rows[0:1, lanes] * cos_l
                        + place_rows[1:2, lanes] * cos_m
                        + place_rows[2:3, lanes] * depth
                    ),
                    axis=0,
                )
            )
        far_high, far_low = split_pair(jnp.concatenate(blocks, axis=1))

        def times(left, right):
            return jnp.dot(left, right, preferred_element_type=jnp.float32)

        result = times(near_high, far_high) + (
            times(near_low, far_high) + times(near_high, far_low)
        )
        coherent[direction] = result.reshape(8, members, stations)
        return carry

    lax.fori_loop(0, dirs, model, 0, unroll=4)

    for copy in gain_copies:
        copy.wait_recv()
    turned = jnp.transpose(every_gains[:, :, 0:LANES].reshape(stations, LANES))
    true_far[...] = turned
    turned = jnp.transpose(every_gains[:, :, LANES : 2 * LANES].reshape(stations, LANES))
    gain_far[...] = turned

    near_lane = lax.broadcasted_iota(jnp.int32, (members, LANES), 1)
    halves = [slice(at * LANES, (at + 1) * LANES) for at in range(stations // LANES)]

    def near_matrix(ref, direction):
        whole_near = ref[...]
        return [
            tuple(
                jnp.sum(
                    jnp.where(near_lane == (part * 4 + entry) * dirs + direction, whole_near, 0.0),
                    axis=1,
                    keepdims=True,
                )
                for part in range(2)
            )
            for entry in range(4)
        ]

    def far_matrix(ref, direction, lanes):
        return [
            tuple(
                ref[pl.ds((part * 4 + entry) * dirs + direction, 1), :][:, lanes]
                for part in range(2)
            )
            for entry in range(4)
        ]

    def planes(ref, lanes, *lead):
        return [
            tuple(ref[(*lead, part * 4 + entry, slice(None), lanes)] for part in range(2))
            for entry in range(4)
        ]

    def add_planes(ref, lanes, matrix):
        for entry in range(4):
            for part in range(2):
                ref[part * 4 + entry, :, lanes] += matrix[entry][part]

    def observe(direction, carry):
        near = near_matrix(near_true, direction)
        for lanes in halves:
            spun = mat_mul_adj(
                planes(coherent, lanes, direction), far_matrix(true_far, direction, lanes)
            )
            add_planes(observed, lanes, mat_mul(near, spun))
        return carry

    lax.fori_loop(0, dirs, observe, 0, unroll=2)

    def predict(direction, carry):
        near = near_matrix(near_gain, direction)
        totals = [0.0] * 4
        for lanes in halves:
            spun = mat_mul_adj(
                planes(coherent, lanes, direction), far_matrix(gain_far, direction, lanes)
            )
            add_planes(predicted, lanes, mat_mul(near, spun))
            for entry in range(4):
                for part in range(2):
                    product[direction, part * 4 + entry, :, lanes] = spun[entry][part]
            weighted = [
                tuple(weight[:, lanes] * value for value in spun[entry]) for entry in range(2)
            ]
            first_power = sum(
                weighted[entry][part] * spun[entry][part]
                for entry in range(2)
                for part in range(2)
            )
            second_power = weight[:, lanes] * sum(
                spun[entry][part] * spun[entry][part] for entry in (2, 3) for part in range(2)
            )
            cross = cadd(cmul_conj(weighted[0], spun[2]), cmul_conj(weighted[1], spun[3]))
            for at, value in enumerate((first_power, second_power, *cross)):
                totals[at] = totals[at] + value
        collected = normal[...]
        for at in range(4):
            collected = jnp.where(
                near_lane == at * dirs + direction,
                jnp.sum(totals[at], axis=1, keepdims=True),
                collected,
            )
        normal[...] = collected
        return carry

    def correlate(direction, carry):
        totals = [[0.0, 0.0] for entry in range(4)]
        for lanes in halves:
            found = mat_mul_adj(planes(misfit, lanes), planes(product, lanes, direction))
            for entry in range(4):
                for part in range(2):
                    totals[entry][part] = totals[entry][part] + found[entry][part]
        collected = cross_sum[...]
        for entry in range(4):
            for part in range(2):
                collected = jnp.where(
                    near_lane == (part * 4 + entry) * dirs + direction,
                    jnp.sum(totals[entry][part], axis=1, keepdims=True),
                    collected,
                )
        cross_sum[...] = collected
        return carry

    pending = [cat_swap] + cat_copies + place_copies + gain_copies
    kept = pl.ds(pl.multiple_of(core * half, half), half)
    away = pl.ds(pl.multiple_of((1 - core) * half, half), half)
    cross_sum[...] = jnp.zeros_like(cross_sum)
    normal[...] = jnp.zeros_like(normal)

    for iteration in range(ITERS):
        predicted[...] = jnp.zeros_like(predicted)
        lax.fori_loop(0, dirs, predict, 0, unroll=2)
        for plane in range(8):
            misfit[plane] = weight[...] * (observed[plane] - predicted[plane])
        lax.fori_loop(0, dirs, correlate, 0, unroll=2)
        mine[iteration, :, 0:LANES] = cross_sum[...]
        mine[iteration, :, LANES : 2 * LANES] = normal[...]

        swap = start_copy(
            mine.at[iteration, away],
            pair.at[iteration],
            pair_send.at[iteration],
            pair_recv.at[iteration],
            sibling,
        )
        swap.wait_recv()
        pending.append(swap)
        sums[iteration, chip] = mine[iteration, kept, :] + pair[iteration]
        copies = [
            start_copy(
                sums.at[iteration, chip],
                sums.at[iteration, chip],
                sum_send.at[iteration, i],
                sum_recv.at[iteration, i],
                peer,
            )
            for i, peer in enumerate(chip_peers)
        ]
        for copy in copies:
            copy.wait_recv()
        pending += copies
        total = sums[iteration, 0]
        for at in range(1, chips):
            total = total + sums[iteration, at]

        def lanes_of(array, at):
            return pltpu.roll(array, LANES - at * dirs, 1) if at else array

        gains = near_gain[kept, :]
        current = [
            tuple(lanes_of(gains, part * 4 + entry) for part in range(2)) for entry in range(4)
        ]
        gathered = [
            tuple(lanes_of(total[:, 0:LANES], part * 4 + entry) for part in range(2))
            for entry in range(4)
        ]
        upper_diag, lower_diag, cross_real, cross_imag = (
            lanes_of(total[:, LANES : 2 * LANES], at) for at in range(4)
        )
        nothing = jnp.zeros_like(upper_diag)
        hermitian = [
            (upper_diag, nothing),
            (cross_real, cross_imag),
            (cross_real, -cross_imag),
            (lower_diag, nothing),
        ]
        numerator = [
            cadd(a, b) for a, b in zip(gathered, mat_mul(current, hermitian))
        ]
        upper_diag = upper_diag + ridge_term
        lower_diag = lower_diag + ridge_term
        determinant = (
            upper_diag * lower_diag - cross_real * cross_real - cross_imag * cross_imag
        )
        inverse = [
            (lower_diag / determinant, nothing),
            (-cross_real / determinant, -cross_imag / determinant),
            (-cross_real / determinant, cross_imag / determinant),
            (upper_diag / determinant, nothing),
        ]
        estimate = mat_mul(numerator, inverse)
        updated = jnp.zeros((half, LANES), jnp.float32)
        for entry in range(4):
            for part in range(2):
                at = part * 4 + entry
                value = 0.5 * (current[entry][part] + estimate[entry][part])
                moved = pltpu.roll(value, at * dirs, 1) if at else value
                inside = near_lane[0:half] // dirs == at
                updated = jnp.where(inside, moved, updated)
        fresh[iteration] = updated

        last = iteration == ITERS - 1
        here = spread.at[iteration, group, core]
        spread[iteration, group, core] = updated
        swap = start_copy(
            fresh.at[iteration], here, turn_send.at[iteration], turn_recv.at[iteration], sibling
        )
        copies = [swap]
        if not last:
            copies += [
                start_copy(
                    fresh.at[iteration],
                    here,
                    fresh_send.at[iteration, way, i],
                    fresh_recv.at[iteration, way, i],
                    peer,
                )
                for i, both in enumerate(zip(stn_peers, cross_peers))
                for way, peer in enumerate(both)
            ]
        for copy in copies:
            copy.wait_recv()
        pending += copies
        near_gain[...] = spread[iteration, group].reshape(members, LANES)
        if not last:
            turned = jnp.transpose(spread[iteration].reshape(stations, LANES))
            gain_far[...] = turned

    residual[...] = misfit[...]
    square[0:members, :] = near_gain[...]
    final[...] = jnp.transpose(square[...])[:, 0:members]
    for copy in pending:
        copy.wait_send()


def on_device(
    positions, catalogue, cluster_ids, counts, flag_mask, thermal_noise, true_gains, start_gains
):
    groups = lax.axis_size("stn")
    chans = lax.axis_size("chan")
    dirs, slots = cluster_ids.shape
    members = positions.shape[1]
    stations = groups * members
    chips = chans // 2
    half = members // 2
    sizes = (groups, chans, dirs, slots, members, float(chans))
    f32 = jnp.float32
    vmem = pl.BlockSpec(memory_space=pltpu.VMEM)
    hbm = pl.BlockSpec(memory_space=pltpu.HBM)
    dma = pltpu.SemaphoreType.DMA

    final, residual = pl.pallas_call(
        lambda *refs: kernel(sizes, *refs),
        name="calibrate",
        out_shape=(
            jax.ShapeDtypeStruct((8 * dirs, members), f32),
            jax.ShapeDtypeStruct((8, members, stations), f32),
        ),
        in_specs=[hbm] * 8,
        out_specs=(vmem, vmem),
        scratch_shapes=[
            pltpu.VMEM(positions.shape, f32),
            pltpu.VMEM(catalogue.shape, f32),
            pltpu.VMEM(cluster_ids.shape, jnp.int32),
            pltpu.SMEM(counts.shape, jnp.int32),
            pltpu.VMEM((members, stations), jnp.int32),
            pltpu.VMEM((8 * dirs, members), f32),
            pltpu.VMEM((8 * dirs, members), f32),
            dma((8,)),
            pltpu.VMEM((LANES, LANES), f32),
            pltpu.VMEM((8, LANES), f32),
            pltpu.VMEM((8, LANES), f32),
            pltpu.VMEM((chips, 8, LANES), f32),
            pltpu.VMEM((LANES, 2 * LANES), jnp.bfloat16),
            dma((2,)),
            pltpu.VMEM((8, LANES), f32),
            pltpu.VMEM((groups, 8, LANES), f32),
            pltpu.VMEM((8, stations), f32),
            pltpu.VMEM((members, 2 * LANES), f32),
            pltpu.VMEM((groups, members, 2 * LANES), f32),
            pltpu.VMEM((8 * dirs, stations), f32),
            pltpu.VMEM((8 * dirs, stations), f32),
            pltpu.VMEM((members, LANES), f32),
            pltpu.VMEM((members, LANES), f32),
            pltpu.VMEM((dirs, 8, members, stations), f32),
            pltpu.VMEM((dirs, 8, members, stations), f32),
            pltpu.VMEM((8, members, stations), f32),
            pltpu.VMEM((8, members, stations), f32),
            pltpu.VMEM((members, stations), f32),
            pltpu.VMEM((8, members, stations), f32),
            pltpu.VMEM((members, LANES), f32),
            pltpu.VMEM((members, LANES), f32),
            pltpu.VMEM((ITERS, half, 2 * LANES), f32),
            pltpu.VMEM((ITERS, members, 2 * LANES), f32),
            pltpu.VMEM((ITERS, chips, half, 2 * LANES), f32),
            pltpu.VMEM((ITERS, half, LANES), f32),
            pltpu.VMEM((ITERS, groups, 2, half, LANES), f32),
            dma((chips - 1,)),
            dma((chips - 1,)),
            dma((groups - 1,)),
            dma((groups - 1,)),
            dma((groups - 1,)),
            dma((groups - 1,)),
            dma((ITERS,)),
            dma((ITERS,)),
            dma((ITERS, chips - 1)),
            dma((ITERS, chips - 1)),
            dma((ITERS, 2, groups - 1)),
            dma((ITERS, 2, groups - 1)),
            dma((ITERS,)),
            dma((ITERS,)),
        ],
        compiler_params=pltpu.CompilerParams(
            collective_id=1, has_side_effects=True, vmem_limit_bytes=60 << 20
        ),
    )(
        positions,
        catalogue,
        cluster_ids,
        counts,
        flag_mask.reshape(members, stations),
        thermal_noise.reshape(8, members, stations),
        true_gains.reshape(8 * dirs, members),
        start_gains.reshape(8 * dirs, members),
    )
    return (final.reshape(true_gains.shape), residual.reshape(thermal_noise.shape))


def solution(mesh):
    return jax.shard_map(
        on_device,
        mesh=mesh,
        in_specs=(
            P(None, "stn"),
            P(None, "chan"),
            P(),
            P(),
            P("chan", "stn", None),
            P(None, None, "chan", "stn", None),
            P(None, None, None, "stn"),
            P(None, None, None, "stn"),
        ),
        out_specs=(P(None, None, None, "stn"), P(None, None, "chan", "stn", None)),
        check_vma=False,
    )
```

```python
import functools

import jax
import jax.numpy as jnp
from jax import lax
from jax.experimental import pallas as pl
from jax.experimental.pallas import tpu as pltpu
from jax.sharding import PartitionSpec as P

ITERS = 3
LANES = 128
MESH = pl.DeviceIdType.MESH

band_spread = 6.0
ridge_term = 1.0
turn_scale = 20.0

SINE = (3.1415926401307073, -5.167710083507893, 2.5500775232145596, -0.5982912856201866, 0.07765766030500078)
COSINE = (
    0.9999999997799042,
    -4.9348021370788056,
    4.0587091595557485,
    -1.3352120030440895,
    0.23493731378565055,
    -0.024396324298134327,
)


def horner(terms, square):
    value = square * terms[-1] + terms[-2]
    for term in terms[-3::-1]:
        value = value * square + term
    return value


def turn_wave(turns):
    rest = turns - jnp.floor(turns + 0.5)
    square = rest * rest
    half_sine = rest * horner(SINE, square)
    half_cosine = horner(COSINE, square)
    twice = half_sine + half_sine
    return 1.0 - twice * half_sine, twice * half_cosine


def split_pair(value):
    high = value.astype(jnp.bfloat16)
    return high, (value - high.astype(jnp.float32)).astype(jnp.bfloat16)


def cmul(a, b):
    return a[0] * b[0] - a[1] * b[1], a[0] * b[1] + a[1] * b[0]


def cmul_conj(a, b):
    return a[0] * b[0] + a[1] * b[1], a[1] * b[0] - a[0] * b[1]


def cadd(a, b):
    return a[0] + b[0], a[1] + b[1]


def mat_mul(left, right):
    return [
        cadd(cmul(left[2 * i], right[j]), cmul(left[2 * i + 1], right[2 + j]))
        for i in range(2)
        for j in range(2)
    ]


def mat_mul_adj(left, right):
    return [
        cadd(cmul_conj(left[2 * i], right[2 * j]), cmul_conj(left[2 * i + 1], right[2 * j + 1]))
        for i in range(2)
        for j in range(2)
    ]


def start_copy(src, dst, send_sem, recv_sem, peer):
    copy = pltpu.make_async_remote_copy(
        src_ref=src,
        dst_ref=dst,
        send_sem=send_sem,
        recv_sem=recv_sem,
        device_id=peer,
        device_id_type=MESH,
    )
    copy.start()
    return copy


def far_first(count, stride):
    ring = count // 2
    moves = [(row, step) for row in range(2) for step in range(ring) if row or step]
    return sorted(moves, key=lambda move: -(move[0] * stride + min(move[1], ring - move[1])))


def moved_to(index, move, count):
    ring = count // 2
    row = lax.rem(index // ring + move[0], 2)
    return row * ring + lax.rem(lax.rem(index, ring) + move[1], ring)


def kernel(
    sizes,
    positions_in,
    catalogue_in,
    ids_in,
    counts_in,
    flags_in,
    noise_in,
    true_in,
    start_in,
    final,
    residual,
    positions,
    catalogue,
    ids,
    counts,
    flags,
    true_gains,
    start_gains,
    load_sem,
    store_sem,
    square,
    own_cat,
    sibling_cat,
    every_cat,
    parts_cat,
    cat_pair_sem,
    own_place,
    every_place,
    place_rows,
    own_gains,
    every_gains,
    true_far,
    gain_far,
    near_true,
    near_gain,
    coherent,
    product,
    observed,
    predicted,
    weight,
    misfit,
    normal,
    pair,
    mine,
    sums,
    fresh,
    spread,
    cat_send,
    cat_recv,
    place_send,
    place_recv,
    gain_send,
    gain_recv,
    pair_send,
    pair_recv,
    sum_send,
    sum_recv,
    fresh_send,
    fresh_recv,
    turn_send,
    turn_recv,
):
    groups, chans, dirs, slots, members, chan_total = sizes
    chips = chans // 2
    group = lax.axis_index("stn")
    channel = lax.axis_index("chan")
    chip = channel // 2
    core = lax.rem(channel, 2)
    stations = groups * members
    half = members // 2

    loads = [
        pltpu.make_async_copy(source, target, load_sem.at[i])
        for i, (source, target) in enumerate(
            (
                (catalogue_in, catalogue),
                (positions_in, positions),
                (true_in, true_gains),
                (start_in, start_gains),
                (ids_in, ids),
                (counts_in, counts),
                (flags_in, flags),
                (noise_in, observed),
            )
        )
    ]
    for load in loads:
        load.start()

    sibling = {"chan": chip * 2 + 1 - core}
    chip_moves = [moved_to(chip, move, chips) for move in far_first(chips, 2)]
    chip_peers = [{"chan": peer * 2 + core} for peer in chip_moves]
    group_moves = [moved_to(group, move, groups) for move in far_first(groups, 1)]
    stn_peers = [{"stn": peer} for peer in group_moves]

    barrier = pltpu.get_barrier_semaphore()
    greeted = chip_peers + stn_peers + [sibling]
    for peer in greeted:
        pl.semaphore_signal(barrier, inc=1, device_id=peer, device_id_type=MESH)

    cat_width = catalogue.shape[1]
    for load in loads[0:2]:
        load.wait()
    own_cat[...] = jnp.zeros_like(own_cat)
    own_cat[0:7, 0:cat_width] = catalogue[...]
    own_cat[...] = jnp.where(core == 0, own_cat[...], pltpu.roll(own_cat[...], cat_width, 1))
    own_place[...] = jnp.zeros_like(own_place)
    own_place[0:3, 0:members] = positions[...]
    for load in loads[2:4]:
        load.wait()
    square[...] = jnp.zeros_like(square)
    square[:, 0:members] = true_gains[...]
    own_gains[:, 0:LANES] = jnp.transpose(square[...])[0:members, :]
    square[:, 0:members] = start_gains[...]
    own_gains[:, LANES : 2 * LANES] = jnp.transpose(square[...])[0:members, :]

    pl.semaphore_wait(barrier, len(greeted))

    cat_swap = start_copy(own_cat, sibling_cat, cat_pair_sem.at[0], cat_pair_sem.at[1], sibling)
    place_copies = [
        start_copy(own_place, every_place.at[group], place_send.at[i], place_recv.at[i], peer)
        for i, peer in enumerate(stn_peers)
    ]
    cat_swap.wait_recv()
    every_cat[chip] = own_cat[...] + sibling_cat[...]
    cat_copies = [
        start_copy(
            every_cat.at[chip], every_cat.at[chip], cat_send.at[i], cat_recv.at[i], peer
        )
        for i, peer in enumerate(chip_peers)
    ]
    gain_copies = [
        start_copy(own_gains, every_gains.at[group], gain_send.at[i], gain_recv.at[i], peer)
        for i, peer in enumerate(stn_peers)
    ]
    every_place[group] = own_place[...]
    every_gains[group] = own_gains[...]
    near_true[...] = own_gains[:, 0:LANES]
    near_gain[...] = own_gains[:, LANES : 2 * LANES]
    for load in loads[4:]:
        load.wait()

    near_index = group * members + lax.broadcasted_iota(jnp.int32, (members, stations), 0)
    far_index = lax.broadcasted_iota(jnp.int32, (members, stations), 1)
    weight[...] = jnp.where(near_index != far_index, flags[...].astype(jnp.float32), 0.0)

    square[...] = jnp.zeros_like(square)
    square[0:dirs, 0:slots] = ids[...].astype(jnp.float32)
    square[...] = jnp.transpose(square[...])
    lane_column = lax.broadcasted_iota(jnp.int32, (slots, LANES), 1)
    lane_value = lane_column.astype(jnp.float32)

    frequency = 1.0 + band_spread * channel.astype(jnp.float32) / chan_total
    log_frequency = jnp.log(jnp.full((1, LANES), frequency, jnp.float32))
    lane_row = lax.broadcasted_iota(jnp.int32, (1, LANES), 1)
    imag_lane = lane_row >= 4 * members
    entry_lane = lax.rem(lane_row // members, 4)

    for copy in reversed(cat_copies):
        copy.wait_recv()
    stacked = jnp.concatenate(
        [
            every_cat[2 * at] + pltpu.roll(every_cat[2 * at + 1], 2 * cat_width, 1)
            for at in range(chips // 2)
        ]
        + [jnp.zeros((LANES - 4 * chips, LANES), jnp.float32)],
        axis=0,
    )
    whole = jnp.transpose(stacked)
    first = whole.astype(jnp.bfloat16).astype(jnp.float32)
    second = (whole - first).astype(jnp.bfloat16).astype(jnp.float32)
    third = whole - first - second
    parts_cat[:, 0:LANES] = (first + pltpu.roll(second, 64, 1)).astype(jnp.bfloat16)
    parts_cat[:, LANES : 2 * LANES] = third.astype(jnp.bfloat16)

    for copy in reversed(place_copies):
        copy.wait_recv()
    per_row = LANES // members
    scale = turn_scale * frequency
    for block in range(groups // per_row):
        joined = every_place[block * per_row]
        for at in range(1, per_row):
            joined = joined + pltpu.roll(every_place[block * per_row + at], members * at, 1)
        place_rows[:, block * LANES : (block + 1) * LANES] = joined * scale
    tiled = own_place[...] * scale
    for shift in (members, 2 * members, 4 * members):
        tiled = tiled + pltpu.roll(tiled, shift, 1)

    def model(direction, carry):
        named = jnp.sum(
            jnp.where(lane_column == direction, square[0:slots, :], 0.0), axis=1, keepdims=True
        )
        block_of = jnp.floor(named * (1.0 / LANES))
        within = named - block_of * LANES
        picked = jnp.dot(
            jnp.where(within == lane_value, 1.0, 0.0).astype(jnp.bfloat16),
            parts_cat[...],
            preferred_element_type=jnp.float32,
        )
        picked = (
            picked[:, 0:LANES]
            + pltpu.roll(picked[:, 0:LANES], 64, 1)
            + picked[:, LANES : 2 * LANES]
        )
        lane_wanted = block_of * 8.0

        def column(at):
            return jnp.broadcast_to(
                jnp.sum(
                    jnp.where(lane_value == lane_wanted + float(at), picked, 0.0),
                    axis=1,
                    keepdims=True,
                ),
                (slots, LANES),
            )

        cos_l, cos_m = column(0), column(1)
        depth = jnp.sqrt(1.0 - cos_l * cos_l - cos_m * cos_m) - 1.0
        rows = lax.broadcasted_iota(jnp.int32, (slots, LANES), 0)
        scaled = jnp.where(
            rows < counts[direction], jnp.exp(column(6) * log_frequency), 0.0
        )
        stokes_i, stokes_q, stokes_u, stokes_v = (scaled * column(at) for at in (2, 3, 4, 5))
        bright_real = jnp.where(
            entry_lane == 0,
            stokes_i + stokes_q,
            jnp.where(entry_lane == 3, stokes_i - stokes_q, stokes_u),
        )
        bright_imag = jnp.where(
            entry_lane == 1, stokes_v, jnp.where(entry_lane == 2, -stokes_v, 0.0)
        )
        near_cos, near_sin = turn_wave(
            tiled[0:1, :] * cos_l + tiled[1:2, :] * cos_m + tiled[2:3, :] * depth
        )
        real_side = jnp.where(imag_lane, bright_imag, bright_real)
        imag_side = jnp.where(imag_lane, bright_real, -bright_imag)
        upper = real_side * near_cos + imag_side * near_sin
        lower = real_side * near_sin - imag_side * near_cos
        near_side = jnp.transpose(jnp.concatenate([upper, lower], axis=0))
        near_high, near_low = split_pair(near_side)
        blocks = []
        for block in range(stations // LANES):
            lanes = slice(block * LANES, (block + 1) * LANES)
            blocks.append(
                jnp.concatenate(
                    turn_wave(
                        place_rows[0:1, lanes] * cos_l
                        + place_rows[1:2, lanes] * cos_m
                        + place_rows[2:3, lanes] * depth
                    ),
                    axis=0,
                )
            )
        far_high, far_low = split_pair(jnp.concatenate(blocks, axis=1))

        def times(left, right):
            return jnp.dot(left, right, preferred_element_type=jnp.float32)

        result = times(near_high, far_high) + (
            times(near_low, far_high) + times(near_high, far_low)
        )
        coherent[direction] = result.reshape(8, members, stations)
        return carry

    lax.fori_loop(0, dirs, model, 0, unroll=4)

    for copy in reversed(gain_copies):
        copy.wait_recv()
    turned = jnp.transpose(every_gains[:, :, 0:LANES].reshape(stations, LANES))
    true_far[...] = turned
    turned = jnp.transpose(every_gains[:, :, LANES : 2 * LANES].reshape(stations, LANES))
    gain_far[...] = turned

    near_lane = lax.broadcasted_iota(jnp.int32, (members, LANES), 1)
    halves = [slice(at * LANES, (at + 1) * LANES) for at in range(stations // LANES)]

    def near_matrix(ref, direction):
        whole_near = ref[...]
        return [
            tuple(
                jnp.sum(
                    jnp.where(near_lane == (part * 4 + entry) * dirs + direction, whole_near, 0.0),
                    axis=1,
                    keepdims=True,
                )
                for part in range(2)
            )
            for entry in range(4)
        ]

    def far_matrix(ref, direction, lanes):
        return [
            tuple(
                ref[pl.ds((part * 4 + entry) * dirs + direction, 1), :][:, lanes]
                for part in range(2)
            )
            for entry in range(4)
        ]

    def planes(ref, lanes, *lead):
        return [
            tuple(ref[(*lead, part * 4 + entry, slice(None), lanes)] for part in range(2))
            for entry in range(4)
        ]

    def add_planes(ref, lanes, matrix):
        for entry in range(4):
            for part in range(2):
                ref[part * 4 + entry, :, lanes] += matrix[entry][part]

    def predict(step, carry, with_truth):
        directions = [step * 2, step * 2 + 1]
        near = [near_matrix(near_gain, direction) for direction in directions]
        if with_truth:
            near_sky = [near_matrix(near_true, direction) for direction in directions]
        totals = [[0.0] * 4 for direction in directions]
        for lanes in halves:
            modelled, truth = [], []
            for at, direction in enumerate(directions):
                seen = planes(coherent, lanes, direction)
                if with_truth:
                    spun = mat_mul_adj(seen, far_matrix(true_far, direction, lanes))
                    truth.append(mat_mul(near_sky[at], spun))
                spun = mat_mul_adj(seen, far_matrix(gain_far, direction, lanes))
                modelled.append(mat_mul(near[at], spun))
                for entry in range(4):
                    for part in range(2):
                        product[direction, part * 4 + entry, :, lanes] = spun[entry][part]
                weighted = [
                    tuple(weight[:, lanes] * value for value in spun[entry]) for entry in range(2)
                ]
                first_power = sum(
                    weighted[entry][part] * spun[entry][part]
                    for entry in range(2)
                    for part in range(2)
                )
                second_power = weight[:, lanes] * sum(
                    spun[entry][part] * spun[entry][part] for entry in (2, 3) for part in range(2)
                )
                cross = cadd(cmul_conj(weighted[0], spun[2]), cmul_conj(weighted[1], spun[3]))
                for kind, value in enumerate((first_power, second_power, *cross)):
                    totals[at][kind] = totals[at][kind] + value
            add_planes(predicted, lanes, [cadd(a, b) for a, b in zip(*modelled)])
            if with_truth:
                add_planes(observed, lanes, [cadd(a, b) for a, b in zip(*truth)])
        collected = normal[...]
        for at, direction in enumerate(directions):
            for kind in range(4):
                collected = jnp.where(
                    near_lane == kind * dirs + direction,
                    jnp.sum(totals[at][kind], axis=1, keepdims=True),
                    collected,
                )
        normal[...] = collected
        return carry

    half_lane = near_lane[0:half]

    def correlate(rows, at, iteration):
        def body(direction, carry):
            missed = [
                tuple(misfit[part * 4 + entry, rows, :] for part in range(2))
                for entry in range(4)
            ]
            turned_back = [
                tuple(product[direction, part * 4 + entry, rows, :] for part in range(2))
                for entry in range(4)
            ]
            found = mat_mul_adj(missed, turned_back)
            collected = mine[iteration, at, :, 0:LANES]
            for entry in range(4):
                for part in range(2):
                    value = sum(found[entry][part][:, lanes] for lanes in halves)
                    collected = jnp.where(
                        half_lane == (part * 4 + entry) * dirs + direction,
                        jnp.sum(value, axis=1, keepdims=True),
                        collected,
                    )
            mine[iteration, at, :, 0:LANES] = collected
            return carry

        mine[iteration, at] = jnp.zeros((half, 2 * LANES), jnp.float32)
        lax.fori_loop(0, dirs, body, 0, unroll=4)
        mine[iteration, at, :, LANES : 2 * LANES] = normal[rows, :]

    pending = [cat_swap] + cat_copies + place_copies + gain_copies

    def settle(copies):
        for copy in pending:
            copy.wait_send()
        pending.clear()
        for copy in reversed(copies):
            copy.wait_recv()
        pending.extend(copies)
    kept = pl.ds(pl.multiple_of(core * half, half), half)
    away = pl.ds(pl.multiple_of((1 - core) * half, half), half)
    normal[...] = jnp.zeros_like(normal)

    for iteration in range(ITERS):
        predicted[...] = jnp.zeros_like(predicted)
        lax.fori_loop(
            0,
            dirs // 2,
            functools.partial(predict, with_truth=iteration == 0),
            0,
            unroll=1,
        )
        for plane in range(8):
            misfit[plane] = weight[...] * (observed[plane] - predicted[plane])
        last = iteration == ITERS - 1
        if last:
            store = pltpu.make_async_copy(misfit, residual, store_sem)
            store.start()

        correlate(away, 0, iteration)
        swap = start_copy(
            mine.at[iteration, 0],
            pair.at[iteration],
            pair_send.at[iteration],
            pair_recv.at[iteration],
            sibling,
        )
        correlate(kept, 1, iteration)
        swap.wait_recv()
        pending.append(swap)
        sums[iteration, chip] = mine[iteration, 1] + pair[iteration]
        copies = [
            start_copy(
                sums.at[iteration, chip],
                sums.at[iteration, chip],
                sum_send.at[iteration, i],
                sum_recv.at[iteration, i],
                peer,
            )
            for i, peer in enumerate(chip_peers)
        ]
        settle(copies)
        total = sums[iteration, 0]
        for at in range(1, chips):
            total = total + sums[iteration, at]

        def lanes_of(array, at):
            return pltpu.roll(array, LANES - at * dirs, 1) if at else array

        gains = near_gain[kept, :]
        current = [
            tuple(lanes_of(gains, part * 4 + entry) for part in range(2)) for entry in range(4)
        ]
        gathered = [
            tuple(lanes_of(total[:, 0:LANES], part * 4 + entry) for part in range(2))
            for entry in range(4)
        ]
        upper_diag, lower_diag, cross_real, cross_imag = (
            lanes_of(total[:, LANES : 2 * LANES], at) for at in range(4)
        )
        nothing = jnp.zeros_like(upper_diag)
        hermitian = [
            (upper_diag, nothing),
            (cross_real, cross_imag),
            (cross_real, -cross_imag),
            (lower_diag, nothing),
        ]
        numerator = [
            cadd(a, b) for a, b in zip(gathered, mat_mul(current, hermitian))
        ]
        upper_diag = upper_diag + ridge_term
        lower_diag = lower_diag + ridge_term
        determinant = (
            upper_diag * lower_diag - cross_real * cross_real - cross_imag * cross_imag
        )
        inverse = [
            (lower_diag / determinant, nothing),
            (-cross_real / determinant, -cross_imag / determinant),
            (-cross_real / determinant, cross_imag / determinant),
            (upper_diag / determinant, nothing),
        ]
        estimate = mat_mul(numerator, inverse)
        updated = jnp.zeros((half, LANES), jnp.float32)
        for entry in range(4):
            for part in range(2):
                at = part * 4 + entry
                value = 0.5 * (current[entry][part] + estimate[entry][part])
                moved = pltpu.roll(value, at * dirs, 1) if at else value
                inside = near_lane[0:half] // dirs == at
                updated = jnp.where(inside, moved, updated)
        fresh[iteration] = updated

        spread[iteration, core, group] = updated
        if not last:
            settle(
                [
                    start_copy(
                        fresh.at[iteration],
                        spread.at[iteration, core, group],
                        fresh_send.at[iteration, i],
                        fresh_recv.at[iteration, i],
                        peer,
                    )
                    for i, peer in enumerate(stn_peers)
                ]
            )
            handed = spread.at[iteration, core]
        else:
            handed = spread.at[iteration, core, group]
        settle(
            [
                start_copy(
                    handed, handed, turn_send.at[iteration], turn_recv.at[iteration], sibling
                )
            ]
        )
        near_gain[...] = jnp.concatenate(
            [spread[iteration, at, group] for at in range(2)], axis=0
        )
        if not last:
            gain_far[...] = jnp.transpose(
                jnp.concatenate(
                    [
                        spread[iteration, at, other]
                        for other in range(groups)
                        for at in range(2)
                    ],
                    axis=0,
                )
            )

    square[0:members, :] = near_gain[...]
    final[...] = jnp.transpose(square[...])[:, 0:members]
    store.wait()
    for copy in pending:
        copy.wait_send()


def on_device(
    positions, catalogue, cluster_ids, counts, flag_mask, thermal_noise, true_gains, start_gains
):
    groups = lax.axis_size("stn")
    chans = lax.axis_size("chan")
    dirs, slots = cluster_ids.shape
    members = positions.shape[1]
    stations = groups * members
    chips = chans // 2
    half = members // 2
    sizes = (groups, chans, dirs, slots, members, float(chans))
    f32 = jnp.float32
    vmem = pl.BlockSpec(memory_space=pltpu.VMEM)
    hbm = pl.BlockSpec(memory_space=pltpu.HBM)
    dma = pltpu.SemaphoreType.DMA

    final, residual = pl.pallas_call(
        lambda *refs: kernel(sizes, *refs),
        name="calibrate",
        out_shape=(
            jax.ShapeDtypeStruct((8 * dirs, members), f32),
            jax.ShapeDtypeStruct((8, members, stations), f32),
        ),
        in_specs=[hbm] * 8,
        out_specs=(vmem, hbm),
        scratch_shapes=[
            pltpu.VMEM(positions.shape, f32),
            pltpu.VMEM(catalogue.shape, f32),
            pltpu.VMEM(cluster_ids.shape, jnp.int32),
            pltpu.SMEM(counts.shape, jnp.int32),
            pltpu.VMEM((members, stations), jnp.int32),
            pltpu.VMEM((8 * dirs, members), f32),
            pltpu.VMEM((8 * dirs, members), f32),
            dma((8,)),
            dma,
            pltpu.VMEM((LANES, LANES), f32),
            pltpu.VMEM((8, LANES), f32),
            pltpu.VMEM((8, LANES), f32),
            pltpu.VMEM((chips, 8, LANES), f32),
            pltpu.VMEM((LANES, 2 * LANES), jnp.bfloat16),
            dma((2,)),
            pltpu.VMEM((8, LANES), f32),
            pltpu.VMEM((groups, 8, LANES), f32),
            pltpu.VMEM((8, stations), f32),
            pltpu.VMEM((members, 2 * LANES), f32),
            pltpu.VMEM((groups, members, 2 * LANES), f32),
            pltpu.VMEM((8 * dirs, stations), f32),
            pltpu.VMEM((8 * dirs, stations), f32),
            pltpu.VMEM((members, LANES), f32),
            pltpu.VMEM((members, LANES), f32),
            pltpu.VMEM((dirs, 8, members, stations), f32),
            pltpu.VMEM((dirs, 8, members, stations), f32),
            pltpu.VMEM((8, members, stations), f32),
            pltpu.VMEM((8, members, stations), f32),
            pltpu.VMEM((members, stations), f32),
            pltpu.VMEM((8, members, stations), f32),
            pltpu.VMEM((members, LANES), f32),
            pltpu.VMEM((ITERS, half, 2 * LANES), f32),
            pltpu.VMEM((ITERS, 2, half, 2 * LANES), f32),
            pltpu.VMEM((ITERS, chips, half, 2 * LANES), f32),
            pltpu.VMEM((ITERS, half, LANES), f32),
            pltpu.VMEM((ITERS, 2, groups, half, LANES), f32),
            dma((chips - 1,)),
            dma((chips - 1,)),
            dma((groups - 1,)),
            dma((groups - 1,)),
            dma((groups - 1,)),
            dma((groups - 1,)),
            dma((ITERS,)),
            dma((ITERS,)),
            dma((ITERS, chips - 1)),
            dma((ITERS, chips - 1)),
            dma((ITERS, groups - 1)),
            dma((ITERS, groups - 1)),
            dma((ITERS,)),
            dma((ITERS,)),
        ],
        compiler_params=pltpu.CompilerParams(
            collective_id=1, has_side_effects=True, vmem_limit_bytes=60 << 20
        ),
    )(
        positions,
        catalogue,
        cluster_ids,
        counts,
        flag_mask.reshape(members, stations),
        thermal_noise.reshape(8, members, stations),
        true_gains.reshape(8 * dirs, members),
        start_gains.reshape(8 * dirs, members),
    )
    return (final.reshape(true_gains.shape), residual.reshape(thermal_noise.shape))


def solution(mesh):
    return jax.shard_map(
        on_device,
        mesh=mesh,
        in_specs=(
            P(None, "stn"),
            P(None, "chan"),
            P(),
            P(),
            P("chan", "stn", None),
            P(None, None, "chan", "stn", None),
            P(None, None, None, "stn"),
            P(None, None, None, "stn"),
        ),
        out_specs=(P(None, None, None, "stn"), P(None, None, "chan", "stn", None)),
        check_vma=False,
    )
```

```python
import functools

import jax
import jax.numpy as jnp
from jax import lax
from jax.experimental import pallas as pl
from jax.experimental.pallas import tpu as pltpu
from jax.sharding import PartitionSpec as P

ITERS = 3
LANES = 128
MESH = pl.DeviceIdType.MESH

band_spread = 6.0
ridge_term = 1.0
turn_scale = 20.0

SINE = (3.1415926401307073, -5.167710083507893, 2.5500775232145596, -0.5982912856201866, 0.07765766030500078)
COSINE = (
    0.9999999997799042,
    -4.9348021370788056,
    4.0587091595557485,
    -1.3352120030440895,
    0.23493731378565055,
    -0.024396324298134327,
)


def horner(terms, square):
    value = square * terms[-1] + terms[-2]
    for term in terms[-3::-1]:
        value = value * square + term
    return value


def turn_wave(turns):
    rest = turns - jnp.floor(turns + 0.5)
    square = rest * rest
    half_sine = rest * horner(SINE, square)
    half_cosine = horner(COSINE, square)
    twice = half_sine + half_sine
    return 1.0 - twice * half_sine, twice * half_cosine


def split_pair(value):
    high = value.astype(jnp.bfloat16)
    return high, (value - high.astype(jnp.float32)).astype(jnp.bfloat16)


def cmul(a, b):
    return a[0] * b[0] - a[1] * b[1], a[0] * b[1] + a[1] * b[0]


def cmul_conj(a, b):
    return a[0] * b[0] + a[1] * b[1], a[1] * b[0] - a[0] * b[1]


def cadd(a, b):
    return a[0] + b[0], a[1] + b[1]


def mat_mul(left, right):
    return [
        cadd(cmul(left[2 * i], right[j]), cmul(left[2 * i + 1], right[2 + j]))
        for i in range(2)
        for j in range(2)
    ]


def mat_mul_adj(left, right):
    return [
        cadd(cmul_conj(left[2 * i], right[2 * j]), cmul_conj(left[2 * i + 1], right[2 * j + 1]))
        for i in range(2)
        for j in range(2)
    ]


def start_copy(src, dst, send_sem, recv_sem, peer):
    copy = pltpu.make_async_remote_copy(
        src_ref=src,
        dst_ref=dst,
        send_sem=send_sem,
        recv_sem=recv_sem,
        device_id=peer,
        device_id_type=MESH,
    )
    copy.start()
    return copy


def far_first(count, stride):
    ring = count // 2
    moves = [(row, step) for row in range(2) for step in range(ring) if row or step]
    return sorted(moves, key=lambda move: -(move[0] * stride + min(move[1], ring - move[1])))


def moved_to(index, move, count):
    ring = count // 2
    row = lax.rem(index // ring + move[0], 2)
    return row * ring + lax.rem(lax.rem(index, ring) + move[1], ring)


def kernel(
    sizes,
    positions_in,
    catalogue_in,
    ids_in,
    counts_in,
    flags_in,
    noise_in,
    true_in,
    start_in,
    final,
    residual,
    positions,
    catalogue,
    ids,
    counts,
    flags,
    true_gains,
    start_gains,
    load_sem,
    square,
    own_cat,
    sibling_cat,
    every_cat,
    parts_cat,
    onehot,
    picks,
    cat_pair_sem,
    own_place,
    every_place,
    place_rows,
    own_gains,
    every_gains,
    true_far,
    gain_far,
    near_true,
    near_gain,
    coherent,
    product,
    observed,
    predicted,
    weight,
    misfit,
    normal,
    pair,
    mine,
    sums,
    fresh,
    spread,
    cat_send,
    cat_recv,
    place_send,
    place_recv,
    gain_send,
    gain_recv,
    pair_send,
    pair_recv,
    sum_send,
    sum_recv,
    fresh_send,
    fresh_recv,
    turn_send,
    turn_recv,
):
    groups, chans, dirs, slots, members, chan_total = sizes
    chips = chans // 2
    group = lax.axis_index("stn")
    channel = lax.axis_index("chan")
    chip = channel // 2
    core = lax.rem(channel, 2)
    stations = groups * members
    half = members // 2

    loads = [
        pltpu.make_async_copy(source, target, load_sem.at[i])
        for i, (source, target) in enumerate(
            (
                (catalogue_in, catalogue),
                (positions_in, positions),
                (true_in, true_gains),
                (start_in, start_gains),
                (ids_in, ids),
                (counts_in, counts),
                (flags_in, flags),
                (noise_in, observed),
            )
        )
    ]
    for load in loads:
        load.start()

    sibling = {"chan": chip * 2 + 1 - core}
    chip_moves = [moved_to(chip, move, chips) for move in far_first(chips, 2)]
    chip_peers = [{"chan": peer * 2 + core} for peer in chip_moves]
    group_moves = [moved_to(group, move, groups) for move in far_first(groups, 1)]
    stn_peers = [{"stn": peer} for peer in group_moves]

    barrier = pltpu.get_barrier_semaphore()
    greeted = chip_peers + stn_peers + [sibling]
    for peer in greeted:
        pl.semaphore_signal(barrier, inc=1, device_id=peer, device_id_type=MESH)

    cat_width = catalogue.shape[1]
    for load in loads[0:2]:
        load.wait()
    own_cat[...] = jnp.zeros_like(own_cat)
    own_cat[0:7, 0:cat_width] = catalogue[...]
    own_cat[...] = jnp.where(core == 0, own_cat[...], pltpu.roll(own_cat[...], cat_width, 1))
    own_place[...] = jnp.zeros_like(own_place)
    own_place[0:3, 0:members] = positions[...]
    pl.semaphore_wait(barrier, len(greeted))

    cat_swap = start_copy(own_cat, sibling_cat, cat_pair_sem.at[0], cat_pair_sem.at[1], sibling)
    place_copies = [
        start_copy(own_place, every_place.at[group], place_send.at[i], place_recv.at[i], peer)
        for i, peer in enumerate(stn_peers)
    ]
    cat_swap.wait_recv()
    every_cat[chip] = own_cat[...] + sibling_cat[...]
    cat_copies = [
        start_copy(
            every_cat.at[chip], every_cat.at[chip], cat_send.at[i], cat_recv.at[i], peer
        )
        for i, peer in enumerate(chip_peers)
    ]
    for load in loads[2:4]:
        load.wait()
    square[...] = jnp.zeros_like(square)
    square[:, 0:members] = true_gains[...]
    own_gains[:, 0:LANES] = jnp.transpose(square[...])[0:members, :]
    square[:, 0:members] = start_gains[...]
    own_gains[:, LANES : 2 * LANES] = jnp.transpose(square[...])[0:members, :]

    gain_copies = [
        start_copy(own_gains, every_gains.at[group], gain_send.at[i], gain_recv.at[i], peer)
        for i, peer in enumerate(stn_peers)
    ]
    every_place[group] = own_place[...]
    every_gains[group] = own_gains[...]
    near_true[...] = own_gains[:, 0:LANES]
    near_gain[...] = own_gains[:, LANES : 2 * LANES]
    for load in loads[4:]:
        load.wait()

    near_index = group * members + lax.broadcasted_iota(jnp.int32, (members, stations), 0)
    far_index = lax.broadcasted_iota(jnp.int32, (members, stations), 1)
    weight[...] = jnp.where(near_index != far_index, flags[...].astype(jnp.float32), 0.0)

    square[...] = jnp.zeros_like(square)
    square[0:dirs, 0:slots] = ids[...].astype(jnp.float32)
    square[...] = jnp.transpose(square[...])
    lane_column = lax.broadcasted_iota(jnp.int32, (slots, LANES), 1)
    lane_value = lane_column.astype(jnp.float32)
    lane_block = (lane_column // 8).astype(jnp.float32)

    def mark(direction, carry):
        named = jnp.sum(
            jnp.where(lane_column == direction, square[0:slots, :], 0.0), axis=1, keepdims=True
        )
        block_of = jnp.floor(named * (1.0 / LANES))
        within = named - block_of * LANES
        onehot[direction] = jnp.where(within == lane_value, 1.0, 0.0).astype(jnp.bfloat16)
        picks[direction] = jnp.where(lane_block == block_of, 1.0, 0.0)
        return carry

    lax.fori_loop(0, dirs, mark, 0, unroll=4)

    frequency = 1.0 + band_spread * channel.astype(jnp.float32) / chan_total
    log_frequency = jnp.log(jnp.full((1, LANES), frequency, jnp.float32))
    lane_row = lax.broadcasted_iota(jnp.int32, (1, LANES), 1)
    imag_lane = lane_row >= 4 * members
    entry_lane = lax.rem(lane_row // members, 4)

    for copy in reversed(cat_copies):
        copy.wait_recv()
    stacked = jnp.concatenate(
        [
            every_cat[2 * at] + pltpu.roll(every_cat[2 * at + 1], 2 * cat_width, 1)
            for at in range(chips // 2)
        ]
        + [jnp.zeros((LANES - 4 * chips, LANES), jnp.float32)],
        axis=0,
    )
    whole = jnp.transpose(stacked)
    first = whole.astype(jnp.bfloat16).astype(jnp.float32)
    second = (whole - first).astype(jnp.bfloat16).astype(jnp.float32)
    third = whole - first - second
    parts_cat[:, 0:LANES] = (first + pltpu.roll(second, 64, 1)).astype(jnp.bfloat16)
    parts_cat[:, LANES : 2 * LANES] = third.astype(jnp.bfloat16)

    found = jnp.dot(
        onehot[...].reshape(dirs * slots, LANES),
        parts_cat[...],
        preferred_element_type=jnp.float32,
    )
    found = (
        found[:, 0:LANES] + pltpu.roll(found[:, 0:LANES], 64, 1) + found[:, LANES : 2 * LANES]
    )
    picks[...] = picks[...] * found.reshape(dirs, slots, LANES)
    lane_kind = lax.rem(lane_column, 8)

    for copy in reversed(place_copies):
        copy.wait_recv()
    per_row = LANES // members
    scale = turn_scale * frequency
    for block in range(groups // per_row):
        joined = every_place[block * per_row]
        for at in range(1, per_row):
            joined = joined + pltpu.roll(every_place[block * per_row + at], members * at, 1)
        place_rows[:, block * LANES : (block + 1) * LANES] = joined * scale
    tiled = own_place[...] * scale
    for shift in (members, 2 * members, 4 * members):
        tiled = tiled + pltpu.roll(tiled, shift, 1)

    def model(direction, carry):
        picked = picks[direction]

        def column(at):
            return jnp.broadcast_to(
                jnp.sum(
                    jnp.where(lane_kind == at, picked, 0.0),
                    axis=1,
                    keepdims=True,
                ),
                (slots, LANES),
            )

        cos_l, cos_m = column(0), column(1)
        depth = jnp.sqrt(1.0 - cos_l * cos_l - cos_m * cos_m) - 1.0
        rows = lax.broadcasted_iota(jnp.int32, (slots, LANES), 0)
        scaled = jnp.where(
            rows < counts[direction], jnp.exp(column(6) * log_frequency), 0.0
        )
        stokes_i, stokes_q, stokes_u, stokes_v = (scaled * column(at) for at in (2, 3, 4, 5))
        bright_real = jnp.where(
            entry_lane == 0,
            stokes_i + stokes_q,
            jnp.where(entry_lane == 3, stokes_i - stokes_q, stokes_u),
        )
        bright_imag = jnp.where(
            entry_lane == 1, stokes_v, jnp.where(entry_lane == 2, -stokes_v, 0.0)
        )
        near_cos, near_sin = turn_wave(
            tiled[0:1, :] * cos_l + tiled[1:2, :] * cos_m + tiled[2:3, :] * depth
        )
        real_side = jnp.where(imag_lane, bright_imag, bright_real)
        imag_side = jnp.where(imag_lane, bright_real, -bright_imag)
        upper = real_side * near_cos + imag_side * near_sin
        lower = real_side * near_sin - imag_side * near_cos
        near_side = jnp.transpose(jnp.concatenate([upper, lower], axis=0))
        near_high, near_low = split_pair(near_side)
        blocks = []
        for block in range(stations // LANES):
            lanes = slice(block * LANES, (block + 1) * LANES)
            blocks.append(
                jnp.concatenate(
                    turn_wave(
                        place_rows[0:1, lanes] * cos_l
                        + place_rows[1:2, lanes] * cos_m
                        + place_rows[2:3, lanes] * depth
                    ),
                    axis=0,
                )
            )
        far_high, far_low = split_pair(jnp.concatenate(blocks, axis=1))

        def times(left, right):
            return jnp.dot(left, right, preferred_element_type=jnp.float32)

        result = times(near_high, far_high) + (
            times(near_low, far_high) + times(near_high, far_low)
        )
        coherent[direction] = result.reshape(8, members, stations)
        return carry

    lax.fori_loop(0, dirs, model, 0, unroll=4)

    for copy in reversed(gain_copies):
        copy.wait_recv()
    turned = jnp.transpose(every_gains[:, :, 0:LANES].reshape(stations, LANES))
    true_far[...] = turned
    turned = jnp.transpose(every_gains[:, :, LANES : 2 * LANES].reshape(stations, LANES))
    gain_far[...] = turned

    near_lane = lax.broadcasted_iota(jnp.int32, (members, LANES), 1)
    halves = [slice(at * LANES, (at + 1) * LANES) for at in range(stations // LANES)]

    def near_matrix(ref, direction):
        whole_near = ref[...]
        return [
            tuple(
                jnp.sum(
                    jnp.where(near_lane == (part * 4 + entry) * dirs + direction, whole_near, 0.0),
                    axis=1,
                    keepdims=True,
                )
                for part in range(2)
            )
            for entry in range(4)
        ]

    def far_matrix(ref, direction, lanes):
        return [
            tuple(
                ref[pl.ds((part * 4 + entry) * dirs + direction, 1), :][:, lanes]
                for part in range(2)
            )
            for entry in range(4)
        ]

    def planes(ref, lanes, *lead):
        return [
            tuple(ref[(*lead, part * 4 + entry, slice(None), lanes)] for part in range(2))
            for entry in range(4)
        ]

    def add_planes(ref, lanes, matrix):
        for entry in range(4):
            for part in range(2):
                ref[part * 4 + entry, :, lanes] += matrix[entry][part]

    def predict(step, carry, with_truth):
        directions = [step * 2, step * 2 + 1]
        near = [near_matrix(near_gain, direction) for direction in directions]
        if with_truth:
            near_sky = [near_matrix(near_true, direction) for direction in directions]
        totals = [[0.0] * 4 for direction in directions]
        for lanes in halves:
            modelled, truth = [], []
            for at, direction in enumerate(directions):
                seen = planes(coherent, lanes, direction)
                if with_truth:
                    spun = mat_mul_adj(seen, far_matrix(true_far, direction, lanes))
                    truth.append(mat_mul(near_sky[at], spun))
                spun = mat_mul_adj(seen, far_matrix(gain_far, direction, lanes))
                modelled.append(mat_mul(near[at], spun))
                for entry in range(4):
                    for part in range(2):
                        product[direction, part * 4 + entry, :, lanes] = spun[entry][part]
                weighted = [
                    tuple(weight[:, lanes] * value for value in spun[entry]) for entry in range(2)
                ]
                first_power = sum(
                    weighted[entry][part] * spun[entry][part]
                    for entry in range(2)
                    for part in range(2)
                )
                second_power = weight[:, lanes] * sum(
                    spun[entry][part] * spun[entry][part] for entry in (2, 3) for part in range(2)
                )
                cross = cadd(cmul_conj(weighted[0], spun[2]), cmul_conj(weighted[1], spun[3]))
                for kind, value in enumerate((first_power, second_power, *cross)):
                    totals[at][kind] = totals[at][kind] + value
            add_planes(predicted, lanes, [cadd(a, b) for a, b in zip(*modelled)])
            if with_truth:
                add_planes(observed, lanes, [cadd(a, b) for a, b in zip(*truth)])
        collected = normal[...]
        for at, direction in enumerate(directions):
            for kind in range(4):
                collected = jnp.where(
                    near_lane == kind * dirs + direction,
                    jnp.sum(totals[at][kind], axis=1, keepdims=True),
                    collected,
                )
        normal[...] = collected
        return carry

    half_lane = near_lane[0:half]

    def correlate(rows, at, iteration):
        def body(direction, carry):
            missed = [
                tuple(misfit[part * 4 + entry, rows, :] for part in range(2))
                for entry in range(4)
            ]
            turned_back = [
                tuple(product[direction, part * 4 + entry, rows, :] for part in range(2))
                for entry in range(4)
            ]
            found = mat_mul_adj(missed, turned_back)
            collected = mine[iteration, at, :, 0:LANES]
            for entry in range(4):
                for part in range(2):
                    value = sum(found[entry][part][:, lanes] for lanes in halves)
                    collected = jnp.where(
                        half_lane == (part * 4 + entry) * dirs + direction,
                        jnp.sum(value, axis=1, keepdims=True),
                        collected,
                    )
            mine[iteration, at, :, 0:LANES] = collected
            return carry

        mine[iteration, at] = jnp.zeros((half, 2 * LANES), jnp.float32)
        lax.fori_loop(0, dirs, body, 0, unroll=4)
        mine[iteration, at, :, LANES : 2 * LANES] = normal[rows, :]

    pending = [cat_swap] + cat_copies + place_copies + gain_copies

    def settle(copies):
        for copy in pending:
            copy.wait_send()
        pending.clear()
        for copy in reversed(copies):
            copy.wait_recv()
        pending.extend(copies)
    kept = pl.ds(pl.multiple_of(core * half, half), half)
    away = pl.ds(pl.multiple_of((1 - core) * half, half), half)
    normal[...] = jnp.zeros_like(normal)

    for iteration in range(ITERS):
        predicted[...] = jnp.zeros_like(predicted)
        lax.fori_loop(
            0,
            dirs // 2,
            functools.partial(predict, with_truth=iteration == 0),
            0,
            unroll=1,
        )
        for plane in range(8):
            misfit[plane] = weight[...] * (observed[plane] - predicted[plane])
        last = iteration == ITERS - 1
        if last:
            residual[...] = misfit[...]

        correlate(away, 0, iteration)
        swap = start_copy(
            mine.at[iteration, 0],
            pair.at[iteration],
            pair_send.at[iteration],
            pair_recv.at[iteration],
            sibling,
        )
        correlate(kept, 1, iteration)
        swap.wait_recv()
        pending.append(swap)
        sums[iteration, chip] = mine[iteration, 1] + pair[iteration]
        copies = [
            start_copy(
                sums.at[iteration, chip],
                sums.at[iteration, chip],
                sum_send.at[iteration, i],
                sum_recv.at[iteration, i],
                peer,
            )
            for i, peer in enumerate(chip_peers)
        ]
        settle(copies)
        total = sums[iteration, 0]
        for at in range(1, chips):
            total = total + sums[iteration, at]

        def lanes_of(array, at):
            return pltpu.roll(array, LANES - at * dirs, 1) if at else array

        gains = near_gain[kept, :]
        current = [
            tuple(lanes_of(gains, part * 4 + entry) for part in range(2)) for entry in range(4)
        ]
        gathered = [
            tuple(lanes_of(total[:, 0:LANES], part * 4 + entry) for part in range(2))
            for entry in range(4)
        ]
        upper_diag, lower_diag, cross_real, cross_imag = (
            lanes_of(total[:, LANES : 2 * LANES], at) for at in range(4)
        )
        nothing = jnp.zeros_like(upper_diag)
        hermitian = [
            (upper_diag, nothing),
            (cross_real, cross_imag),
            (cross_real, -cross_imag),
            (lower_diag, nothing),
        ]
        numerator = [
            cadd(a, b) for a, b in zip(gathered, mat_mul(current, hermitian))
        ]
        upper_diag = upper_diag + ridge_term
        lower_diag = lower_diag + ridge_term
        determinant = (
            upper_diag * lower_diag - cross_real * cross_real - cross_imag * cross_imag
        )
        inverse = [
            (lower_diag / determinant, nothing),
            (-cross_real / determinant, -cross_imag / determinant),
            (-cross_real / determinant, cross_imag / determinant),
            (upper_diag / determinant, nothing),
        ]
        estimate = mat_mul(numerator, inverse)
        updated = jnp.zeros((half, LANES), jnp.float32)
        for entry in range(4):
            for part in range(2):
                at = part * 4 + entry
                value = 0.5 * (current[entry][part] + estimate[entry][part])
                moved = pltpu.roll(value, at * dirs, 1) if at else value
                inside = near_lane[0:half] // dirs == at
                updated = jnp.where(inside, moved, updated)
        fresh[iteration] = updated

        spread[iteration, core, group] = updated
        if not last:
            settle(
                [
                    start_copy(
                        fresh.at[iteration],
                        spread.at[iteration, core, group],
                        fresh_send.at[iteration, i],
                        fresh_recv.at[iteration, i],
                        peer,
                    )
                    for i, peer in enumerate(stn_peers)
                ]
            )
            handed = spread.at[iteration, core]
        else:
            handed = spread.at[iteration, core, group]
        settle(
            [
                start_copy(
                    handed, handed, turn_send.at[iteration], turn_recv.at[iteration], sibling
                )
            ]
        )
        near_gain[...] = jnp.concatenate(
            [spread[iteration, at, group] for at in range(2)], axis=0
        )
        if not last:
            gain_far[...] = jnp.transpose(
                jnp.concatenate(
                    [
                        spread[iteration, at, other]
                        for other in range(groups)
                        for at in range(2)
                    ],
                    axis=0,
                )
            )

    square[0:members, :] = near_gain[...]
    final[...] = jnp.transpose(square[...])[:, 0:members]
    for copy in pending:
        copy.wait_send()


def on_device(
    positions, catalogue, cluster_ids, counts, flag_mask, thermal_noise, true_gains, start_gains
):
    groups = lax.axis_size("stn")
    chans = lax.axis_size("chan")
    dirs, slots = cluster_ids.shape
    members = positions.shape[1]
    stations = groups * members
    chips = chans // 2
    half = members // 2
    sizes = (groups, chans, dirs, slots, members, float(chans))
    f32 = jnp.float32
    vmem = pl.BlockSpec(memory_space=pltpu.VMEM)
    hbm = pl.BlockSpec(memory_space=pltpu.HBM)
    dma = pltpu.SemaphoreType.DMA

    final, residual = pl.pallas_call(
        lambda *refs: kernel(sizes, *refs),
        name="calibrate",
        out_shape=(
            jax.ShapeDtypeStruct((8 * dirs, members), f32),
            jax.ShapeDtypeStruct((8, members, stations), f32),
        ),
        in_specs=[hbm] * 8,
        out_specs=(vmem, vmem),
        scratch_shapes=[
            pltpu.VMEM(positions.shape, f32),
            pltpu.VMEM(catalogue.shape, f32),
            pltpu.VMEM(cluster_ids.shape, jnp.int32),
            pltpu.SMEM(counts.shape, jnp.int32),
            pltpu.VMEM((members, stations), jnp.int32),
            pltpu.VMEM((8 * dirs, members), f32),
            pltpu.VMEM((8 * dirs, members), f32),
            dma((8,)),
            pltpu.VMEM((LANES, LANES), f32),
            pltpu.VMEM((8, LANES), f32),
            pltpu.VMEM((8, LANES), f32),
            pltpu.VMEM((chips, 8, LANES), f32),
            pltpu.VMEM((LANES, 2 * LANES), jnp.bfloat16),
            pltpu.VMEM((dirs, slots, LANES), jnp.bfloat16),
            pltpu.VMEM((dirs, slots, LANES), f32),
            dma((2,)),
            pltpu.VMEM((8, LANES), f32),
            pltpu.VMEM((groups, 8, LANES), f32),
            pltpu.VMEM((8, stations), f32),
            pltpu.VMEM((members, 2 * LANES), f32),
            pltpu.VMEM((groups, members, 2 * LANES), f32),
            pltpu.VMEM((8 * dirs, stations), f32),
            pltpu.VMEM((8 * dirs, stations), f32),
            pltpu.VMEM((members, LANES), f32),
            pltpu.VMEM((members, LANES), f32),
            pltpu.VMEM((dirs, 8, members, stations), f32),
            pltpu.VMEM((dirs, 8, members, stations), f32),
            pltpu.VMEM((8, members, stations), f32),
            pltpu.VMEM((8, members, stations), f32),
            pltpu.VMEM((members, stations), f32),
            pltpu.VMEM((8, members, stations), f32),
            pltpu.VMEM((members, LANES), f32),
            pltpu.VMEM((ITERS, half, 2 * LANES), f32),
            pltpu.VMEM((ITERS, 2, half, 2 * LANES), f32),
            pltpu.VMEM((ITERS, chips, half, 2 * LANES), f32),
            pltpu.VMEM((ITERS, half, LANES), f32),
            pltpu.VMEM((ITERS, 2, groups, half, LANES), f32),
            dma((chips - 1,)),
            dma((chips - 1,)),
            dma((groups - 1,)),
            dma((groups - 1,)),
            dma((groups - 1,)),
            dma((groups - 1,)),
            dma((ITERS,)),
            dma((ITERS,)),
            dma((ITERS, chips - 1)),
            dma((ITERS, chips - 1)),
            dma((ITERS, groups - 1)),
            dma((ITERS, groups - 1)),
            dma((ITERS,)),
            dma((ITERS,)),
        ],
        compiler_params=pltpu.CompilerParams(
            collective_id=1, has_side_effects=True, vmem_limit_bytes=24 << 20
        ),
    )(
        *(
            pltpu.with_memory_space_constraint(array, pltpu.HBM)
            for array in (
                positions,
                catalogue,
                cluster_ids,
                counts,
                flag_mask.reshape(members, stations),
                thermal_noise.reshape(8, members, stations),
                true_gains.reshape(8 * dirs, members),
                start_gains.reshape(8 * dirs, members),
            )
        )
    )
    return (final.reshape(true_gains.shape), residual.reshape(thermal_noise.shape))


def solution(mesh):
    return jax.shard_map(
        on_device,
        mesh=mesh,
        in_specs=(
            P(None, "stn"),
            P(None, "chan"),
            P(),
            P(),
            P("chan", "stn", None),
            P(None, None, "chan", "stn", None),
            P(None, None, None, "stn"),
            P(None, None, None, "stn"),
        ),
        out_specs=(P(None, None, None, "stn"), P(None, None, "chan", "stn", None)),
        check_vma=False,
    )
```

```python
import functools

import jax
import jax.numpy as jnp
from jax import lax
from jax.experimental import pallas as pl
from jax.experimental.pallas import tpu as pltpu
from jax.sharding import PartitionSpec as P

ITERS = 3
LANES = 128
MESH = pl.DeviceIdType.MESH

band_spread = 6.0
ridge_term = 1.0
turn_scale = 20.0

SINE = (3.1415926401307073, -5.167710083507893, 2.5500775232145596, -0.5982912856201866, 0.07765766030500078)
COSINE = (
    0.9999999997799042,
    -4.9348021370788056,
    4.0587091595557485,
    -1.3352120030440895,
    0.23493731378565055,
    -0.024396324298134327,
)


def horner(terms, square):
    value = square * terms[-1] + terms[-2]
    for term in terms[-3::-1]:
        value = value * square + term
    return value


def turn_wave(turns):
    rest = turns - jnp.floor(turns + 0.5)
    square = rest * rest
    half_sine = rest * horner(SINE, square)
    half_cosine = horner(COSINE, square)
    twice = half_sine + half_sine
    return 1.0 - twice * half_sine, twice * half_cosine


def split_pair(value):
    high = value.astype(jnp.bfloat16)
    return high, (value - high.astype(jnp.float32)).astype(jnp.bfloat16)


def cmul(a, b):
    return a[0] * b[0] - a[1] * b[1], a[0] * b[1] + a[1] * b[0]


def cmul_conj(a, b):
    return a[0] * b[0] + a[1] * b[1], a[1] * b[0] - a[0] * b[1]


def cadd(a, b):
    return a[0] + b[0], a[1] + b[1]


def mat_mul(left, right):
    return [
        cadd(cmul(left[2 * i], right[j]), cmul(left[2 * i + 1], right[2 + j]))
        for i in range(2)
        for j in range(2)
    ]


def mat_mul_adj(left, right):
    return [
        cadd(cmul_conj(left[2 * i], right[2 * j]), cmul_conj(left[2 * i + 1], right[2 * j + 1]))
        for i in range(2)
        for j in range(2)
    ]


def start_copy(src, dst, send_sem, recv_sem, peer):
    copy = pltpu.make_async_remote_copy(
        src_ref=src,
        dst_ref=dst,
        send_sem=send_sem,
        recv_sem=recv_sem,
        device_id=peer,
        device_id_type=MESH,
    )
    copy.start()
    return copy


def far_first(count, stride):
    ring = count // 2
    moves = [(row, step) for row in range(2) for step in range(ring) if row or step]
    return sorted(moves, key=lambda move: -(move[0] * stride + min(move[1], ring - move[1])))


def moved_to(index, move, count):
    ring = count // 2
    row = lax.rem(index // ring + move[0], 2)
    return row * ring + lax.rem(lax.rem(index, ring) + move[1], ring)


def kernel(
    sizes,
    positions_in,
    catalogue_in,
    ids_in,
    counts_in,
    flags_in,
    noise_in,
    true_in,
    start_in,
    final,
    residual,
    positions,
    catalogue,
    ids,
    counts,
    flags,
    true_gains,
    start_gains,
    load_sem,
    square,
    own_cat,
    sibling_cat,
    every_cat,
    parts_cat,
    onehot,
    picks,
    cat_pair_sem,
    own_place,
    every_place,
    place_rows,
    own_gains,
    every_gains,
    gain_pair_sem,
    true_far,
    gain_far,
    near_true,
    near_gain,
    coherent,
    product,
    observed,
    predicted,
    weight,
    misfit,
    normal,
    pair,
    mine,
    sums,
    fresh,
    spread,
    cat_send,
    cat_recv,
    place_send,
    place_recv,
    gain_send,
    gain_recv,
    pair_send,
    pair_recv,
    sum_send,
    sum_recv,
    fresh_send,
    fresh_recv,
    turn_send,
    turn_recv,
):
    groups, chans, dirs, slots, members, chan_total = sizes
    chips = chans // 2
    group = lax.axis_index("stn")
    channel = lax.axis_index("chan")
    chip = channel // 2
    core = lax.rem(channel, 2)
    stations = groups * members
    half = members // 2

    loads = [
        pltpu.make_async_copy(source, target, load_sem.at[i])
        for i, (source, target) in enumerate(
            (
                (catalogue_in, catalogue),
                (positions_in, positions),
                (true_in, true_gains),
                (start_in, start_gains),
                (ids_in, ids),
                (counts_in, counts),
                (flags_in, flags),
                (noise_in, observed),
            )
        )
    ]
    for load in loads:
        load.start()

    sibling = {"chan": chip * 2 + 1 - core}
    chip_moves = [moved_to(chip, move, chips) for move in far_first(chips, 2)]
    chip_peers = [{"chan": peer * 2 + core} for peer in chip_moves]
    group_moves = [moved_to(group, move, groups) for move in far_first(groups, 1)]
    stn_peers = [{"stn": peer} for peer in group_moves]

    barrier = pltpu.get_barrier_semaphore()
    greeted = chip_peers + stn_peers + [sibling]
    for peer in greeted:
        pl.semaphore_signal(barrier, inc=1, device_id=peer, device_id_type=MESH)

    cat_width = catalogue.shape[1]
    for load in loads[0:2]:
        load.wait()
    own_cat[...] = jnp.zeros_like(own_cat)
    own_cat[0:7, 0:cat_width] = catalogue[...]
    own_cat[...] = jnp.where(core == 0, own_cat[...], pltpu.roll(own_cat[...], cat_width, 1))
    own_place[...] = jnp.zeros_like(own_place)
    own_place[0:3, 0:members] = positions[...]
    pl.semaphore_wait(barrier, len(greeted))

    cat_swap = start_copy(own_cat, sibling_cat, cat_pair_sem.at[0], cat_pair_sem.at[1], sibling)
    place_copies = [
        start_copy(own_place, every_place.at[group], place_send.at[i], place_recv.at[i], peer)
        for i, peer in enumerate(stn_peers)
    ]
    cat_swap.wait_recv()
    every_cat[chip] = own_cat[...] + sibling_cat[...]
    cat_copies = [
        start_copy(
            every_cat.at[chip], every_cat.at[chip], cat_send.at[i], cat_recv.at[i], peer
        )
        for i, peer in enumerate(chip_peers)
    ]
    for load in loads[2:4]:
        load.wait()
    square[...] = jnp.zeros_like(square)
    square[:, 0:members] = true_gains[...]
    own_gains[:, 0:LANES] = jnp.transpose(square[...])[0:members, :]
    square[:, 0:members] = start_gains[...]
    own_gains[:, LANES : 2 * LANES] = jnp.transpose(square[...])[0:members, :]

    kept = pl.ds(pl.multiple_of(core * half, half), half)
    away = pl.ds(pl.multiple_of((1 - core) * half, half), half)
    every_gains[core, group] = own_gains[kept, :]
    gain_copies = [
        start_copy(
            every_gains.at[core, group],
            every_gains.at[core, group],
            gain_send.at[i],
            gain_recv.at[i],
            peer,
        )
        for i, peer in enumerate(stn_peers)
    ]
    every_place[group] = own_place[...]
    near_true[...] = own_gains[:, 0:LANES]
    near_gain[...] = own_gains[:, LANES : 2 * LANES]
    for load in loads[4:]:
        load.wait()

    near_index = group * members + lax.broadcasted_iota(jnp.int32, (members, stations), 0)
    far_index = lax.broadcasted_iota(jnp.int32, (members, stations), 1)
    weight[...] = jnp.where(near_index != far_index, flags[...].astype(jnp.float32), 0.0)

    square[...] = jnp.zeros_like(square)
    square[0:dirs, 0:slots] = ids[...].astype(jnp.float32)
    square[...] = jnp.transpose(square[...])
    lane_column = lax.broadcasted_iota(jnp.int32, (slots, LANES), 1)
    lane_value = lane_column.astype(jnp.float32)
    lane_block = (lane_column // 8).astype(jnp.float32)

    def mark(direction, carry):
        named = jnp.sum(
            jnp.where(lane_column == direction, square[0:slots, :], 0.0), axis=1, keepdims=True
        )
        block_of = jnp.floor(named * (1.0 / LANES))
        within = named - block_of * LANES
        onehot[direction] = jnp.where(within == lane_value, 1.0, 0.0).astype(jnp.bfloat16)
        picks[direction] = jnp.where(lane_block == block_of, 1.0, 0.0)
        return carry

    lax.fori_loop(0, dirs, mark, 0, unroll=4)

    frequency = 1.0 + band_spread * channel.astype(jnp.float32) / chan_total
    log_frequency = jnp.log(jnp.full((1, LANES), frequency, jnp.float32))
    lane_row = lax.broadcasted_iota(jnp.int32, (1, LANES), 1)
    imag_lane = lane_row >= 4 * members
    entry_lane = lax.rem(lane_row // members, 4)

    for copy in reversed(cat_copies):
        copy.wait_recv()
    stacked = jnp.concatenate(
        [
            every_cat[2 * at] + pltpu.roll(every_cat[2 * at + 1], 2 * cat_width, 1)
            for at in range(chips // 2)
        ]
        + [jnp.zeros((LANES - 4 * chips, LANES), jnp.float32)],
        axis=0,
    )
    whole = jnp.transpose(stacked)
    first = whole.astype(jnp.bfloat16).astype(jnp.float32)
    second = (whole - first).astype(jnp.bfloat16).astype(jnp.float32)
    third = whole - first - second
    parts_cat[:, 0:LANES] = (first + pltpu.roll(second, 64, 1)).astype(jnp.bfloat16)
    parts_cat[:, LANES : 2 * LANES] = third.astype(jnp.bfloat16)

    found = jnp.dot(
        onehot[...].reshape(dirs * slots, LANES),
        parts_cat[...],
        preferred_element_type=jnp.float32,
    )
    found = (
        found[:, 0:LANES] + pltpu.roll(found[:, 0:LANES], 64, 1) + found[:, LANES : 2 * LANES]
    )
    picks[...] = picks[...] * found.reshape(dirs, slots, LANES)
    lane_kind = lax.rem(lane_column, 8)

    for copy in reversed(place_copies):
        copy.wait_recv()
    per_row = LANES // members
    scale = turn_scale * frequency
    for block in range(groups // per_row):
        joined = every_place[block * per_row]
        for at in range(1, per_row):
            joined = joined + pltpu.roll(every_place[block * per_row + at], members * at, 1)
        place_rows[:, block * LANES : (block + 1) * LANES] = joined * scale
    tiled = own_place[...] * scale
    for shift in (members, 2 * members, 4 * members):
        tiled = tiled + pltpu.roll(tiled, shift, 1)

    def model(direction, carry):
        picked = picks[direction]

        def column(at):
            return jnp.broadcast_to(
                jnp.sum(
                    jnp.where(lane_kind == at, picked, 0.0),
                    axis=1,
                    keepdims=True,
                ),
                (slots, LANES),
            )

        cos_l, cos_m = column(0), column(1)
        depth = jnp.sqrt(1.0 - cos_l * cos_l - cos_m * cos_m) - 1.0
        rows = lax.broadcasted_iota(jnp.int32, (slots, LANES), 0)
        scaled = jnp.where(
            rows < counts[direction], jnp.exp(column(6) * log_frequency), 0.0
        )
        stokes_i, stokes_q, stokes_u, stokes_v = (scaled * column(at) for at in (2, 3, 4, 5))
        bright_real = jnp.where(
            entry_lane == 0,
            stokes_i + stokes_q,
            jnp.where(entry_lane == 3, stokes_i - stokes_q, stokes_u),
        )
        bright_imag = jnp.where(
            entry_lane == 1, stokes_v, jnp.where(entry_lane == 2, -stokes_v, 0.0)
        )
        near_cos, near_sin = turn_wave(
            tiled[0:1, :] * cos_l + tiled[1:2, :] * cos_m + tiled[2:3, :] * depth
        )
        real_side = jnp.where(imag_lane, bright_imag, bright_real)
        imag_side = jnp.where(imag_lane, bright_real, -bright_imag)
        upper = real_side * near_cos + imag_side * near_sin
        lower = real_side * near_sin - imag_side * near_cos
        near_side = jnp.transpose(jnp.concatenate([upper, lower], axis=0))
        near_high, near_low = split_pair(near_side)
        blocks = []
        for block in range(stations // LANES):
            lanes = slice(block * LANES, (block + 1) * LANES)
            blocks.append(
                jnp.concatenate(
                    turn_wave(
                        place_rows[0:1, lanes] * cos_l
                        + place_rows[1:2, lanes] * cos_m
                        + place_rows[2:3, lanes] * depth
                    ),
                    axis=0,
                )
            )
        far_high, far_low = split_pair(jnp.concatenate(blocks, axis=1))

        def times(left, right):
            return jnp.dot(left, right, preferred_element_type=jnp.float32)

        result = times(near_high, far_high) + (
            times(near_low, far_high) + times(near_high, far_low)
        )
        coherent[direction] = result.reshape(8, members, stations)
        return carry

    lax.fori_loop(0, dirs // 2, model, 0, unroll=8)
    for copy in reversed(gain_copies):
        copy.wait_recv()
    gain_hand = start_copy(
        every_gains.at[core],
        every_gains.at[core],
        gain_pair_sem.at[0],
        gain_pair_sem.at[1],
        sibling,
    )
    lax.fori_loop(dirs // 2, dirs, model, 0, unroll=8)
    gain_hand.wait_recv()

    def far_rows(lanes):
        tiles = [every_gains[at, other, :, lanes] for other in range(groups) for at in range(2)]
        return jnp.transpose(jnp.concatenate(tiles, axis=0))

    true_far[...] = far_rows(slice(0, LANES))
    gain_far[...] = far_rows(slice(LANES, 2 * LANES))

    near_lane = lax.broadcasted_iota(jnp.int32, (members, LANES), 1)
    halves = [slice(at * LANES, (at + 1) * LANES) for at in range(stations // LANES)]

    def near_matrix(ref, direction):
        whole_near = ref[...]
        return [
            tuple(
                jnp.sum(
                    jnp.where(near_lane == (part * 4 + entry) * dirs + direction, whole_near, 0.0),
                    axis=1,
                    keepdims=True,
                )
                for part in range(2)
            )
            for entry in range(4)
        ]

    def far_matrix(ref, direction, lanes):
        return [
            tuple(
                ref[pl.ds((part * 4 + entry) * dirs + direction, 1), :][:, lanes]
                for part in range(2)
            )
            for entry in range(4)
        ]

    def planes(ref, lanes, *lead):
        return [
            tuple(ref[(*lead, part * 4 + entry, slice(None), lanes)] for part in range(2))
            for entry in range(4)
        ]

    def add_planes(ref, lanes, matrix):
        for entry in range(4):
            for part in range(2):
                ref[part * 4 + entry, :, lanes] += matrix[entry][part]

    def predict(step, carry, with_truth):
        directions = [step * 2, step * 2 + 1]
        near = [near_matrix(near_gain, direction) for direction in directions]
        if with_truth:
            near_sky = [near_matrix(near_true, direction) for direction in directions]
        totals = [[0.0] * 4 for direction in directions]
        for lanes in halves:
            modelled, truth = [], []
            for at, direction in enumerate(directions):
                seen = planes(coherent, lanes, direction)
                if with_truth:
                    spun = mat_mul_adj(seen, far_matrix(true_far, direction, lanes))
                    truth.append(mat_mul(near_sky[at], spun))
                spun = mat_mul_adj(seen, far_matrix(gain_far, direction, lanes))
                modelled.append(mat_mul(near[at], spun))
                for entry in range(4):
                    for part in range(2):
                        product[direction, part * 4 + entry, :, lanes] = spun[entry][part]
                weighted = [
                    tuple(weight[:, lanes] * value for value in spun[entry]) for entry in range(2)
                ]
                first_power = sum(
                    weighted[entry][part] * spun[entry][part]
                    for entry in range(2)
                    for part in range(2)
                )
                second_power = weight[:, lanes] * sum(
                    spun[entry][part] * spun[entry][part] for entry in (2, 3) for part in range(2)
                )
                cross = cadd(cmul_conj(weighted[0], spun[2]), cmul_conj(weighted[1], spun[3]))
                for kind, value in enumerate((first_power, second_power, *cross)):
                    totals[at][kind] = totals[at][kind] + value
            add_planes(predicted, lanes, [cadd(a, b) for a, b in zip(*modelled)])
            if with_truth:
                add_planes(observed, lanes, [cadd(a, b) for a, b in zip(*truth)])
        collected = normal[...]
        for at, direction in enumerate(directions):
            for kind in range(4):
                collected = jnp.where(
                    near_lane == kind * dirs + direction,
                    jnp.sum(totals[at][kind], axis=1, keepdims=True),
                    collected,
                )
        normal[...] = collected
        return carry

    half_lane = near_lane[0:half]

    def correlate(rows, at, iteration):
        def body(direction, carry):
            missed = [
                tuple(misfit[part * 4 + entry, rows, :] for part in range(2))
                for entry in range(4)
            ]
            turned_back = [
                tuple(product[direction, part * 4 + entry, rows, :] for part in range(2))
                for entry in range(4)
            ]
            found = mat_mul_adj(missed, turned_back)
            collected = mine[iteration, at, :, 0:LANES]
            for entry in range(4):
                for part in range(2):
                    value = sum(found[entry][part][:, lanes] for lanes in halves)
                    collected = jnp.where(
                        half_lane == (part * 4 + entry) * dirs + direction,
                        jnp.sum(value, axis=1, keepdims=True),
                        collected,
                    )
            mine[iteration, at, :, 0:LANES] = collected
            return carry

        mine[iteration, at] = jnp.zeros((half, 2 * LANES), jnp.float32)
        lax.fori_loop(0, dirs, body, 0, unroll=8)
        mine[iteration, at, :, LANES : 2 * LANES] = normal[rows, :]

    pending = [cat_swap, gain_hand] + cat_copies + place_copies + gain_copies

    def settle(copies):
        for copy in pending:
            copy.wait_send()
        pending.clear()
        for copy in reversed(copies):
            copy.wait_recv()
        pending.extend(copies)
    normal[...] = jnp.zeros_like(normal)

    for iteration in range(ITERS):
        predicted[...] = jnp.zeros_like(predicted)
        lax.fori_loop(
            0,
            dirs // 2,
            functools.partial(predict, with_truth=iteration == 0),
            0,
            unroll=1,
        )
        for plane in range(8):
            misfit[plane] = weight[...] * (observed[plane] - predicted[plane])
        last = iteration == ITERS - 1
        if last:
            residual[...] = misfit[...]

        correlate(away, 0, iteration)
        swap = start_copy(
            mine.at[iteration, 0],
            pair.at[iteration],
            pair_send.at[iteration],
            pair_recv.at[iteration],
            sibling,
        )
        correlate(kept, 1, iteration)
        swap.wait_recv()
        pending.append(swap)
        sums[iteration, chip] = mine[iteration, 1] + pair[iteration]
        copies = [
            start_copy(
                sums.at[iteration, chip],
                sums.at[iteration, chip],
                sum_send.at[iteration, i],
                sum_recv.at[iteration, i],
                peer,
            )
            for i, peer in enumerate(chip_peers)
        ]
        settle(copies)
        total = sums[iteration, 0]
        for at in range(1, chips):
            total = total + sums[iteration, at]

        def lanes_of(array, at):
            return pltpu.roll(array, LANES - at * dirs, 1) if at else array

        gains = near_gain[kept, :]
        current = [
            tuple(lanes_of(gains, part * 4 + entry) for part in range(2)) for entry in range(4)
        ]
        gathered = [
            tuple(lanes_of(total[:, 0:LANES], part * 4 + entry) for part in range(2))
            for entry in range(4)
        ]
        upper_diag, lower_diag, cross_real, cross_imag = (
            lanes_of(total[:, LANES : 2 * LANES], at) for at in range(4)
        )
        nothing = jnp.zeros_like(upper_diag)
        hermitian = [
            (upper_diag, nothing),
            (cross_real, cross_imag),
            (cross_real, -cross_imag),
            (lower_diag, nothing),
        ]
        numerator = [
            cadd(a, b) for a, b in zip(gathered, mat_mul(current, hermitian))
        ]
        upper_diag = upper_diag + ridge_term
        lower_diag = lower_diag + ridge_term
        determinant = (
            upper_diag * lower_diag - cross_real * cross_real - cross_imag * cross_imag
        )
        inverse = [
            (lower_diag / determinant, nothing),
            (-cross_real / determinant, -cross_imag / determinant),
            (-cross_real / determinant, cross_imag / determinant),
            (upper_diag / determinant, nothing),
        ]
        estimate = mat_mul(numerator, inverse)
        updated = jnp.zeros((half, LANES), jnp.float32)
        for entry in range(4):
            for part in range(2):
                at = part * 4 + entry
                value = 0.5 * (current[entry][part] + estimate[entry][part])
                moved = pltpu.roll(value, at * dirs, 1) if at else value
                inside = near_lane[0:half] // dirs == at
                updated = jnp.where(inside, moved, updated)
        fresh[iteration] = updated

        spread[iteration, core, group] = updated
        if not last:
            settle(
                [
                    start_copy(
                        fresh.at[iteration],
                        spread.at[iteration, core, group],
                        fresh_send.at[iteration, i],
                        fresh_recv.at[iteration, i],
                        peer,
                    )
                    for i, peer in enumerate(stn_peers)
                ]
            )
            handed = spread.at[iteration, core]
        else:
            handed = spread.at[iteration, core, group]
        settle(
            [
                start_copy(
                    handed, handed, turn_send.at[iteration], turn_recv.at[iteration], sibling
                )
            ]
        )
        near_gain[...] = jnp.concatenate(
            [spread[iteration, at, group] for at in range(2)], axis=0
        )
        if not last:
            gain_far[...] = jnp.transpose(
                jnp.concatenate(
                    [
                        spread[iteration, at, other]
                        for other in range(groups)
                        for at in range(2)
                    ],
                    axis=0,
                )
            )

    square[0:members, :] = near_gain[...]
    final[...] = jnp.transpose(square[...])[:, 0:members]
    for copy in pending:
        copy.wait_send()


def on_device(
    positions, catalogue, cluster_ids, counts, flag_mask, thermal_noise, true_gains, start_gains
):
    groups = lax.axis_size("stn")
    chans = lax.axis_size("chan")
    dirs, slots = cluster_ids.shape
    members = positions.shape[1]
    stations = groups * members
    chips = chans // 2
    half = members // 2
    sizes = (groups, chans, dirs, slots, members, float(chans))
    f32 = jnp.float32
    vmem = pl.BlockSpec(memory_space=pltpu.VMEM)
    hbm = pl.BlockSpec(memory_space=pltpu.HBM)
    dma = pltpu.SemaphoreType.DMA

    final, residual = pl.pallas_call(
        lambda *refs: kernel(sizes, *refs),
        name="calibrate",
        out_shape=(
            jax.ShapeDtypeStruct((8 * dirs, members), f32),
            jax.ShapeDtypeStruct((8, members, stations), f32),
        ),
        in_specs=[hbm] * 8,
        out_specs=(vmem, vmem),
        scratch_shapes=[
            pltpu.VMEM(positions.shape, f32),
            pltpu.VMEM(catalogue.shape, f32),
            pltpu.VMEM(cluster_ids.shape, jnp.int32),
            pltpu.SMEM(counts.shape, jnp.int32),
            pltpu.VMEM((members, stations), jnp.int32),
            pltpu.VMEM((8 * dirs, members), f32),
            pltpu.VMEM((8 * dirs, members), f32),
            dma((8,)),
            pltpu.VMEM((LANES, LANES), f32),
            pltpu.VMEM((8, LANES), f32),
            pltpu.VMEM((8, LANES), f32),
            pltpu.VMEM((chips, 8, LANES), f32),
            pltpu.VMEM((LANES, 2 * LANES), jnp.bfloat16),
            pltpu.VMEM((dirs, slots, LANES), jnp.bfloat16),
            pltpu.VMEM((dirs, slots, LANES), f32),
            dma((2,)),
            pltpu.VMEM((8, LANES), f32),
            pltpu.VMEM((groups, 8, LANES), f32),
            pltpu.VMEM((8, stations), f32),
            pltpu.VMEM((members, 2 * LANES), f32),
            pltpu.VMEM((2, groups, half, 2 * LANES), f32),
            dma((2,)),
            pltpu.VMEM((8 * dirs, stations), f32),
            pltpu.VMEM((8 * dirs, stations), f32),
            pltpu.VMEM((members, LANES), f32),
            pltpu.VMEM((members, LANES), f32),
            pltpu.VMEM((dirs, 8, members, stations), f32),
            pltpu.VMEM((dirs, 8, members, stations), f32),
            pltpu.VMEM((8, members, stations), f32),
            pltpu.VMEM((8, members, stations), f32),
            pltpu.VMEM((members, stations), f32),
            pltpu.VMEM((8, members, stations), f32),
            pltpu.VMEM((members, LANES), f32),
            pltpu.VMEM((ITERS, half, 2 * LANES), f32),
            pltpu.VMEM((ITERS, 2, half, 2 * LANES), f32),
            pltpu.VMEM((ITERS, chips, half, 2 * LANES), f32),
            pltpu.VMEM((ITERS, half, LANES), f32),
            pltpu.VMEM((ITERS, 2, groups, half, LANES), f32),
            dma((chips - 1,)),
            dma((chips - 1,)),
            dma((groups - 1,)),
            dma((groups - 1,)),
            dma((groups - 1,)),
            dma((groups - 1,)),
            dma((ITERS,)),
            dma((ITERS,)),
            dma((ITERS, chips - 1)),
            dma((ITERS, chips - 1)),
            dma((ITERS, groups - 1)),
            dma((ITERS, groups - 1)),
            dma((ITERS,)),
            dma((ITERS,)),
        ],
        compiler_params=pltpu.CompilerParams(
            collective_id=1, has_side_effects=True, vmem_limit_bytes=24 << 20
        ),
    )(
        *(
            pltpu.with_memory_space_constraint(array, pltpu.HBM)
            for array in (
                positions,
                catalogue,
                cluster_ids,
                counts,
                flag_mask.reshape(members, stations),
                thermal_noise.reshape(8, members, stations),
                true_gains.reshape(8 * dirs, members),
                start_gains.reshape(8 * dirs, members),
            )
        )
    )
    return (final.reshape(true_gains.shape), residual.reshape(thermal_noise.shape))


def solution(mesh):
    return jax.shard_map(
        on_device,
        mesh=mesh,
        in_specs=(
            P(None, "stn"),
            P(None, "chan"),
            P(),
            P(),
            P("chan", "stn", None),
            P(None, None, "chan", "stn", None),
            P(None, None, None, "stn"),
            P(None, None, None, "stn"),
        ),
        out_specs=(P(None, None, None, "stn"), P(None, None, "chan", "stn", None)),
        check_vma=False,
    )
```

```python
import functools

import jax
import jax.numpy as jnp
from jax import lax
from jax.experimental import pallas as pl
from jax.experimental.pallas import tpu as pltpu
from jax.sharding import PartitionSpec as P

ITERS = 3
LANES = 128
MESH = pl.DeviceIdType.MESH

band_spread = 6.0
ridge_term = 1.0
turn_scale = 20.0

SINE = (3.1415926401307073, -5.167710083507893, 2.5500775232145596, -0.5982912856201866, 0.07765766030500078)
COSINE = (
    0.9999999997799042,
    -4.9348021370788056,
    4.0587091595557485,
    -1.3352120030440895,
    0.23493731378565055,
    -0.024396324298134327,
)


def horner(terms, square):
    value = square * terms[-1] + terms[-2]
    for term in terms[-3::-1]:
        value = value * square + term
    return value


def turn_wave(turns):
    rest = turns - jnp.floor(turns + 0.5)
    square = rest * rest
    half_sine = rest * horner(SINE, square)
    half_cosine = horner(COSINE, square)
    twice = half_sine + half_sine
    return 1.0 - twice * half_sine, twice * half_cosine


def split_pair(value):
    high = value.astype(jnp.bfloat16)
    return high, (value - high.astype(jnp.float32)).astype(jnp.bfloat16)


def cmul(a, b):
    return a[0] * b[0] - a[1] * b[1], a[0] * b[1] + a[1] * b[0]


def cmul_conj(a, b):
    return a[0] * b[0] + a[1] * b[1], a[1] * b[0] - a[0] * b[1]


def cadd(a, b):
    return a[0] + b[0], a[1] + b[1]


def mat_mul(left, right):
    return [
        cadd(cmul(left[2 * i], right[j]), cmul(left[2 * i + 1], right[2 + j]))
        for i in range(2)
        for j in range(2)
    ]


def mat_mul_adj(left, right):
    return [
        cadd(cmul_conj(left[2 * i], right[2 * j]), cmul_conj(left[2 * i + 1], right[2 * j + 1]))
        for i in range(2)
        for j in range(2)
    ]


def start_copy(src, dst, send_sem, recv_sem, peer):
    copy = pltpu.make_async_remote_copy(
        src_ref=src,
        dst_ref=dst,
        send_sem=send_sem,
        recv_sem=recv_sem,
        device_id=peer,
        device_id_type=MESH,
    )
    copy.start()
    return copy


def far_first(count, stride):
    ring = count // 2
    moves = [(row, step) for row in range(2) for step in range(ring) if row or step]
    return sorted(moves, key=lambda move: -(move[0] * stride + min(move[1], ring - move[1])))


def moved_to(index, move, count):
    ring = count // 2
    row = lax.rem(index // ring + move[0], 2)
    return row * ring + lax.rem(lax.rem(index, ring) + move[1], ring)


def kernel(
    sizes,
    positions_in,
    catalogue_in,
    ids_in,
    counts_in,
    flags_in,
    noise_in,
    true_in,
    start_in,
    final,
    residual,
    positions,
    catalogue,
    ids,
    counts,
    flags,
    true_gains,
    start_gains,
    load_sem,
    square,
    own_cat,
    sibling_cat,
    every_cat,
    parts_cat,
    onehot,
    picks,
    cat_pair_sem,
    own_place,
    every_place,
    place_rows,
    own_gains,
    every_gains,
    gain_pair_sem,
    true_far,
    gain_far,
    near_true,
    near_gain,
    coherent,
    product,
    observed,
    predicted,
    weight,
    misfit,
    normal,
    pair,
    mine,
    sums,
    fresh,
    spread,
    cat_send,
    cat_recv,
    place_send,
    place_recv,
    gain_send,
    gain_recv,
    pair_send,
    pair_recv,
    sum_send,
    sum_recv,
    fresh_send,
    fresh_recv,
    turn_send,
    turn_recv,
):
    groups, chans, dirs, slots, members, chan_total = sizes
    chips = chans // 2
    group = lax.axis_index("stn")
    channel = lax.axis_index("chan")
    chip = channel // 2
    core = lax.rem(channel, 2)
    stations = groups * members
    half = members // 2

    loads = [
        pltpu.make_async_copy(source, target, load_sem.at[i])
        for i, (source, target) in enumerate(
            (
                (catalogue_in, catalogue),
                (positions_in, positions),
                (true_in, true_gains),
                (start_in, start_gains),
                (ids_in, ids),
                (counts_in, counts),
                (flags_in, flags),
                (noise_in, observed),
            )
        )
    ]
    for load in loads:
        load.start()

    sibling = {"chan": chip * 2 + 1 - core}
    chip_moves = [moved_to(chip, move, chips) for move in far_first(chips, 2)]
    chip_peers = [{"chan": peer * 2 + core} for peer in chip_moves]
    group_moves = [moved_to(group, move, groups) for move in far_first(groups, 1)]
    stn_peers = [{"stn": peer} for peer in group_moves]

    barrier = pltpu.get_barrier_semaphore()
    greeted = chip_peers + stn_peers + [sibling]
    for peer in greeted:
        pl.semaphore_signal(barrier, inc=1, device_id=peer, device_id_type=MESH)

    cat_width = catalogue.shape[1]
    for load in loads[0:2]:
        load.wait()
    own_cat[...] = jnp.zeros_like(own_cat)
    own_cat[0:7, 0:cat_width] = catalogue[...]
    own_cat[...] = jnp.where(core == 0, own_cat[...], pltpu.roll(own_cat[...], cat_width, 1))
    own_place[...] = jnp.zeros_like(own_place)
    own_place[0:3, 0:members] = positions[...]
    pl.semaphore_wait(barrier, len(greeted))

    cat_swap = start_copy(own_cat, sibling_cat, cat_pair_sem.at[0], cat_pair_sem.at[1], sibling)
    place_copies = [
        start_copy(own_place, every_place.at[group], place_send.at[i], place_recv.at[i], peer)
        for i, peer in enumerate(stn_peers)
    ]
    cat_swap.wait_recv()
    every_cat[chip] = own_cat[...] + sibling_cat[...]
    cat_copies = [
        start_copy(
            every_cat.at[chip], every_cat.at[chip], cat_send.at[i], cat_recv.at[i], peer
        )
        for i, peer in enumerate(chip_peers)
    ]
    for load in loads[2:4]:
        load.wait()
    square[...] = jnp.zeros_like(square)
    square[:, 0:members] = true_gains[...]
    own_gains[:, 0:LANES] = jnp.transpose(square[...])[0:members, :]
    square[:, 0:members] = start_gains[...]
    own_gains[:, LANES : 2 * LANES] = jnp.transpose(square[...])[0:members, :]

    kept = pl.ds(pl.multiple_of(core * half, half), half)
    away = pl.ds(pl.multiple_of((1 - core) * half, half), half)
    every_gains[core, group] = own_gains[kept, :]
    gain_copies = [
        start_copy(
            every_gains.at[core, group],
            every_gains.at[core, group],
            gain_send.at[i],
            gain_recv.at[i],
            peer,
        )
        for i, peer in enumerate(stn_peers)
    ]
    every_place[group] = own_place[...]
    near_true[...] = own_gains[:, 0:LANES]
    near_gain[...] = own_gains[:, LANES : 2 * LANES]
    for load in loads[4:]:
        load.wait()

    near_index = group * members + lax.broadcasted_iota(jnp.int32, (members, stations), 0)
    far_index = lax.broadcasted_iota(jnp.int32, (members, stations), 1)
    weight[...] = jnp.where(near_index != far_index, flags[...].astype(jnp.float32), 0.0)

    square[...] = jnp.zeros_like(square)
    square[0:dirs, 0:slots] = ids[...].astype(jnp.float32)
    square[...] = jnp.transpose(square[...])
    lane_column = lax.broadcasted_iota(jnp.int32, (slots, LANES), 1)
    lane_value = lane_column.astype(jnp.float32)
    lane_block = (lane_column // 8).astype(jnp.float32)

    def mark(direction, carry):
        named = jnp.sum(
            jnp.where(lane_column == direction, square[0:slots, :], 0.0), axis=1, keepdims=True
        )
        block_of = jnp.floor(named * (1.0 / LANES))
        within = named - block_of * LANES
        onehot[direction] = jnp.where(within == lane_value, 1.0, 0.0).astype(jnp.bfloat16)
        picks[direction] = jnp.where(lane_block == block_of, 1.0, 0.0)
        return carry

    lax.fori_loop(0, dirs, mark, 0, unroll=4)

    frequency = 1.0 + band_spread * channel.astype(jnp.float32) / chan_total
    log_frequency = jnp.log(jnp.full((1, LANES), frequency, jnp.float32))
    lane_row = lax.broadcasted_iota(jnp.int32, (1, LANES), 1)
    imag_lane = lane_row >= 4 * members
    entry_lane = lax.rem(lane_row // members, 4)

    for copy in reversed(cat_copies):
        copy.wait_recv()
    stacked = jnp.concatenate(
        [
            every_cat[2 * at] + pltpu.roll(every_cat[2 * at + 1], 2 * cat_width, 1)
            for at in range(chips // 2)
        ]
        + [jnp.zeros((LANES - 4 * chips, LANES), jnp.float32)],
        axis=0,
    )
    whole = jnp.transpose(stacked)
    first = whole.astype(jnp.bfloat16).astype(jnp.float32)
    second = (whole - first).astype(jnp.bfloat16).astype(jnp.float32)
    third = whole - first - second
    parts_cat[:, 0:LANES] = (first + pltpu.roll(second, 64, 1)).astype(jnp.bfloat16)
    parts_cat[:, LANES : 2 * LANES] = third.astype(jnp.bfloat16)

    found = jnp.dot(
        onehot[...].reshape(dirs * slots, LANES),
        parts_cat[...],
        preferred_element_type=jnp.float32,
    )
    found = (
        found[:, 0:LANES] + pltpu.roll(found[:, 0:LANES], 64, 1) + found[:, LANES : 2 * LANES]
    )
    picks[...] = picks[...] * found.reshape(dirs, slots, LANES)
    lane_kind = lax.rem(lane_column, 8)

    for copy in reversed(place_copies):
        copy.wait_recv()
    per_row = LANES // members
    scale = turn_scale * frequency
    for block in range(groups // per_row):
        joined = every_place[block * per_row]
        for at in range(1, per_row):
            joined = joined + pltpu.roll(every_place[block * per_row + at], members * at, 1)
        place_rows[:, block * LANES : (block + 1) * LANES] = joined * scale
    tiled = own_place[...] * scale
    for shift in (members, 2 * members, 4 * members):
        tiled = tiled + pltpu.roll(tiled, shift, 1)

    def model(direction, carry):
        picked = picks[direction]

        def column(at):
            return jnp.broadcast_to(
                jnp.sum(
                    jnp.where(lane_kind == at, picked, 0.0),
                    axis=1,
                    keepdims=True,
                ),
                (slots, LANES),
            )

        cos_l, cos_m = column(0), column(1)
        depth = jnp.sqrt(1.0 - cos_l * cos_l - cos_m * cos_m) - 1.0
        rows = lax.broadcasted_iota(jnp.int32, (slots, LANES), 0)
        scaled = jnp.where(
            rows < counts[direction], jnp.exp(column(6) * log_frequency), 0.0
        )
        stokes_i, stokes_q, stokes_u, stokes_v = (scaled * column(at) for at in (2, 3, 4, 5))
        bright_real = jnp.where(
            entry_lane == 0,
            stokes_i + stokes_q,
            jnp.where(entry_lane == 3, stokes_i - stokes_q, stokes_u),
        )
        bright_imag = jnp.where(
            entry_lane == 1, stokes_v, jnp.where(entry_lane == 2, -stokes_v, 0.0)
        )
        near_cos, near_sin = turn_wave(
            tiled[0:1, :] * cos_l + tiled[1:2, :] * cos_m + tiled[2:3, :] * depth
        )
        real_side = jnp.where(imag_lane, bright_imag, bright_real)
        imag_side = jnp.where(imag_lane, bright_real, -bright_imag)
        upper = real_side * near_cos + imag_side * near_sin
        lower = real_side * near_sin - imag_side * near_cos
        near_side = jnp.transpose(jnp.concatenate([upper, lower], axis=0))
        near_high, near_low = split_pair(near_side)
        blocks = []
        for block in range(stations // LANES):
            lanes = slice(block * LANES, (block + 1) * LANES)
            blocks.append(
                jnp.concatenate(
                    turn_wave(
                        place_rows[0:1, lanes] * cos_l
                        + place_rows[1:2, lanes] * cos_m
                        + place_rows[2:3, lanes] * depth
                    ),
                    axis=0,
                )
            )
        far_high, far_low = split_pair(jnp.concatenate(blocks, axis=1))

        def times(left, right):
            return jnp.dot(left, right, preferred_element_type=jnp.float32)

        result = times(near_high, far_high) + (
            times(near_low, far_high) + times(near_high, far_low)
        )
        coherent[direction] = result.reshape(8, members, stations)
        return carry

    lax.fori_loop(0, dirs // 2, model, 0, unroll=8)
    for copy in reversed(gain_copies):
        copy.wait_recv()
    gain_hand = start_copy(
        every_gains.at[core],
        every_gains.at[core],
        gain_pair_sem.at[0],
        gain_pair_sem.at[1],
        sibling,
    )
    lax.fori_loop(dirs // 2, dirs, model, 0, unroll=8)
    gain_hand.wait_recv()

    def far_rows(lanes):
        tiles = [every_gains[at, other, :, lanes] for other in range(groups) for at in range(2)]
        return jnp.transpose(jnp.concatenate(tiles, axis=0))

    true_far[...] = far_rows(slice(0, LANES))
    gain_far[...] = far_rows(slice(LANES, 2 * LANES))

    near_lane = lax.broadcasted_iota(jnp.int32, (members, LANES), 1)
    halves = [slice(at * LANES, (at + 1) * LANES) for at in range(stations // LANES)]

    def near_matrix(ref, direction):
        whole_near = ref[...]
        return [
            tuple(
                jnp.sum(
                    jnp.where(near_lane == (part * 4 + entry) * dirs + direction, whole_near, 0.0),
                    axis=1,
                    keepdims=True,
                )
                for part in range(2)
            )
            for entry in range(4)
        ]

    def far_matrix(ref, direction, lanes):
        return [
            tuple(
                ref[pl.ds((part * 4 + entry) * dirs + direction, 1), :][:, lanes]
                for part in range(2)
            )
            for entry in range(4)
        ]

    def planes(ref, lanes, *lead):
        return [
            tuple(ref[(*lead, part * 4 + entry, slice(None), lanes)] for part in range(2))
            for entry in range(4)
        ]

    def add_planes(ref, lanes, matrix):
        for entry in range(4):
            for part in range(2):
                ref[part * 4 + entry, :, lanes] += matrix[entry][part]

    def predict(step, carry, with_truth):
        directions = [step * 2, step * 2 + 1]
        near = [near_matrix(near_gain, direction) for direction in directions]
        if with_truth:
            near_sky = [near_matrix(near_true, direction) for direction in directions]
        totals = [[0.0] * 4 for direction in directions]
        for lanes in halves:
            modelled, truth = [], []
            for at, direction in enumerate(directions):
                seen = planes(coherent, lanes, direction)
                if with_truth:
                    spun = mat_mul_adj(seen, far_matrix(true_far, direction, lanes))
                    truth.append(mat_mul(near_sky[at], spun))
                spun = mat_mul_adj(seen, far_matrix(gain_far, direction, lanes))
                modelled.append(mat_mul(near[at], spun))
                for entry in range(4):
                    for part in range(2):
                        product[direction, part * 4 + entry, :, lanes] = spun[entry][part]
                weighted = [
                    tuple(weight[:, lanes] * value for value in spun[entry]) for entry in range(2)
                ]
                first_power = sum(
                    weighted[entry][part] * spun[entry][part]
                    for entry in range(2)
                    for part in range(2)
                )
                second_power = weight[:, lanes] * sum(
                    spun[entry][part] * spun[entry][part] for entry in (2, 3) for part in range(2)
                )
                cross = cadd(cmul_conj(weighted[0], spun[2]), cmul_conj(weighted[1], spun[3]))
                for kind, value in enumerate((first_power, second_power, *cross)):
                    totals[at][kind] = totals[at][kind] + value
            add_planes(predicted, lanes, [cadd(a, b) for a, b in zip(*modelled)])
            if with_truth:
                add_planes(observed, lanes, [cadd(a, b) for a, b in zip(*truth)])
        collected = normal[...]
        for at, direction in enumerate(directions):
            for kind in range(4):
                collected = jnp.where(
                    near_lane == kind * dirs + direction,
                    jnp.sum(totals[at][kind], axis=1, keepdims=True),
                    collected,
                )
        normal[...] = collected
        return carry

    half_lane = near_lane[0:half]

    def correlate(rows, at, iteration):
        def body(direction, carry):
            missed = [
                tuple(misfit[part * 4 + entry, rows, :] for part in range(2))
                for entry in range(4)
            ]
            turned_back = [
                tuple(product[direction, part * 4 + entry, rows, :] for part in range(2))
                for entry in range(4)
            ]
            found = mat_mul_adj(missed, turned_back)
            collected = mine[iteration, at, 0:half, :]
            for entry in range(4):
                for part in range(2):
                    value = sum(found[entry][part][:, lanes] for lanes in halves)
                    collected = jnp.where(
                        half_lane == (part * 4 + entry) * dirs + direction,
                        jnp.sum(value, axis=1, keepdims=True),
                        collected,
                    )
            mine[iteration, at, 0:half, :] = collected
            return carry

        mine[iteration, at, 0:half, :] = jnp.zeros((half, LANES), jnp.float32)
        lax.fori_loop(0, dirs, body, 0, unroll=8)
        powers = normal[rows, :]
        beside = pltpu.roll(powers, LANES // 2, 1)
        mine[iteration, at, half:, :] = jnp.where(
            half_lane[0 : half // 2] < LANES // 2, powers[0 : half // 2], beside[half // 2 :]
        )

    pending = [cat_swap, gain_hand] + cat_copies + place_copies + gain_copies

    def settle(copies):
        for copy in pending:
            copy.wait_send()
        pending.clear()
        for copy in reversed(copies):
            copy.wait_recv()
        pending.extend(copies)
    normal[...] = jnp.zeros_like(normal)

    for iteration in range(ITERS):
        predicted[...] = jnp.zeros_like(predicted)
        lax.fori_loop(
            0,
            dirs // 2,
            functools.partial(predict, with_truth=iteration == 0),
            0,
            unroll=1,
        )
        for plane in range(8):
            misfit[plane] = weight[...] * (observed[plane] - predicted[plane])
        last = iteration == ITERS - 1
        if last:
            residual[...] = misfit[...]

        correlate(away, 0, iteration)
        swap = start_copy(
            mine.at[iteration, 0],
            pair.at[iteration],
            pair_send.at[iteration],
            pair_recv.at[iteration],
            sibling,
        )
        correlate(kept, 1, iteration)
        swap.wait_recv()
        pending.append(swap)
        sums[iteration, chip] = mine[iteration, 1] + pair[iteration]
        copies = [
            start_copy(
                sums.at[iteration, chip],
                sums.at[iteration, chip],
                sum_send.at[iteration, i],
                sum_recv.at[iteration, i],
                peer,
            )
            for i, peer in enumerate(chip_peers)
        ]
        settle(copies)
        total = sums[iteration, 0]
        for at in range(1, chips):
            total = total + sums[iteration, at]

        def lanes_of(array, at):
            return pltpu.roll(array, LANES - at * dirs, 1) if at else array

        powers = total[half:, :]
        powers = jnp.concatenate([powers, pltpu.roll(powers, LANES // 2, 1)], axis=0)
        gains = near_gain[kept, :]
        current = [
            tuple(lanes_of(gains, part * 4 + entry) for part in range(2)) for entry in range(4)
        ]
        gathered = [
            tuple(lanes_of(total[0:half, :], part * 4 + entry) for part in range(2))
            for entry in range(4)
        ]
        upper_diag, lower_diag, cross_real, cross_imag = (
            lanes_of(powers, at) for at in range(4)
        )
        nothing = jnp.zeros_like(upper_diag)
        hermitian = [
            (upper_diag, nothing),
            (cross_real, cross_imag),
            (cross_real, -cross_imag),
            (lower_diag, nothing),
        ]
        numerator = [
            cadd(a, b) for a, b in zip(gathered, mat_mul(current, hermitian))
        ]
        upper_diag = upper_diag + ridge_term
        lower_diag = lower_diag + ridge_term
        determinant = (
            upper_diag * lower_diag - cross_real * cross_real - cross_imag * cross_imag
        )
        inverse = [
            (lower_diag / determinant, nothing),
            (-cross_real / determinant, -cross_imag / determinant),
            (-cross_real / determinant, cross_imag / determinant),
            (upper_diag / determinant, nothing),
        ]
        estimate = mat_mul(numerator, inverse)
        updated = jnp.zeros((half, LANES), jnp.float32)
        for entry in range(4):
            for part in range(2):
                at = part * 4 + entry
                value = 0.5 * (current[entry][part] + estimate[entry][part])
                moved = pltpu.roll(value, at * dirs, 1) if at else value
                inside = near_lane[0:half] // dirs == at
                updated = jnp.where(inside, moved, updated)
        fresh[iteration] = updated

        spread[iteration, core, group] = updated
        if not last:
            settle(
                [
                    start_copy(
                        fresh.at[iteration],
                        spread.at[iteration, core, group],
                        fresh_send.at[iteration, i],
                        fresh_recv.at[iteration, i],
                        peer,
                    )
                    for i, peer in enumerate(stn_peers)
                ]
            )
            handed = spread.at[iteration, core]
        else:
            handed = spread.at[iteration, core, group]
        settle(
            [
                start_copy(
                    handed, handed, turn_send.at[iteration], turn_recv.at[iteration], sibling
                )
            ]
        )
        near_gain[...] = jnp.concatenate(
            [spread[iteration, at, group] for at in range(2)], axis=0
        )
        if not last:
            gain_far[...] = jnp.transpose(
                jnp.concatenate(
                    [
                        spread[iteration, at, other]
                        for other in range(groups)
                        for at in range(2)
                    ],
                    axis=0,
                )
            )

    square[0:members, :] = near_gain[...]
    final[...] = jnp.transpose(square[...])[:, 0:members]
    for copy in pending:
        copy.wait_send()


def on_device(
    positions, catalogue, cluster_ids, counts, flag_mask, thermal_noise, true_gains, start_gains
):
    groups = lax.axis_size("stn")
    chans = lax.axis_size("chan")
    dirs, slots = cluster_ids.shape
    members = positions.shape[1]
    stations = groups * members
    chips = chans // 2
    half = members // 2
    sizes = (groups, chans, dirs, slots, members, float(chans))
    f32 = jnp.float32
    vmem = pl.BlockSpec(memory_space=pltpu.VMEM)
    hbm = pl.BlockSpec(memory_space=pltpu.HBM)
    dma = pltpu.SemaphoreType.DMA

    final, residual = pl.pallas_call(
        lambda *refs: kernel(sizes, *refs),
        name="calibrate",
        out_shape=(
            jax.ShapeDtypeStruct((8 * dirs, members), f32),
            jax.ShapeDtypeStruct((8, members, stations), f32),
        ),
        in_specs=[hbm] * 8,
        out_specs=(vmem, vmem),
        scratch_shapes=[
            pltpu.VMEM(positions.shape, f32),
            pltpu.VMEM(catalogue.shape, f32),
            pltpu.VMEM(cluster_ids.shape, jnp.int32),
            pltpu.SMEM(counts.shape, jnp.int32),
            pltpu.VMEM((members, stations), jnp.int32),
            pltpu.VMEM((8 * dirs, members), f32),
            pltpu.VMEM((8 * dirs, members), f32),
            dma((8,)),
            pltpu.VMEM((LANES, LANES), f32),
            pltpu.VMEM((8, LANES), f32),
            pltpu.VMEM((8, LANES), f32),
            pltpu.VMEM((chips, 8, LANES), f32),
            pltpu.VMEM((LANES, 2 * LANES), jnp.bfloat16),
            pltpu.VMEM((dirs, slots, LANES), jnp.bfloat16),
            pltpu.VMEM((dirs, slots, LANES), f32),
            dma((2,)),
            pltpu.VMEM((8, LANES), f32),
            pltpu.VMEM((groups, 8, LANES), f32),
            pltpu.VMEM((8, stations), f32),
            pltpu.VMEM((members, 2 * LANES), f32),
            pltpu.VMEM((2, groups, half, 2 * LANES), f32),
            dma((2,)),
            pltpu.VMEM((8 * dirs, stations), f32),
            pltpu.VMEM((8 * dirs, stations), f32),
            pltpu.VMEM((members, LANES), f32),
            pltpu.VMEM((members, LANES), f32),
            pltpu.VMEM((dirs, 8, members, stations), f32),
            pltpu.VMEM((dirs, 8, members, stations), f32),
            pltpu.VMEM((8, members, stations), f32),
            pltpu.VMEM((8, members, stations), f32),
            pltpu.VMEM((members, stations), f32),
            pltpu.VMEM((8, members, stations), f32),
            pltpu.VMEM((members, LANES), f32),
            pltpu.VMEM((ITERS, half + half // 2, LANES), f32),
            pltpu.VMEM((ITERS, 2, half + half // 2, LANES), f32),
            pltpu.VMEM((ITERS, chips, half + half // 2, LANES), f32),
            pltpu.VMEM((ITERS, half, LANES), f32),
            pltpu.VMEM((ITERS, 2, groups, half, LANES), f32),
            dma((chips - 1,)),
            dma((chips - 1,)),
            dma((groups - 1,)),
            dma((groups - 1,)),
            dma((groups - 1,)),
            dma((groups - 1,)),
            dma((ITERS,)),
            dma((ITERS,)),
            dma((ITERS, chips - 1)),
            dma((ITERS, chips - 1)),
            dma((ITERS, groups - 1)),
            dma((ITERS, groups - 1)),
            dma((ITERS,)),
            dma((ITERS,)),
        ],
        compiler_params=pltpu.CompilerParams(
            collective_id=1, has_side_effects=True, vmem_limit_bytes=24 << 20
        ),
    )(
        *(
            pltpu.with_memory_space_constraint(array, pltpu.HBM)
            for array in (
                positions,
                catalogue,
                cluster_ids,
                counts,
                flag_mask.reshape(members, stations),
                thermal_noise.reshape(8, members, stations),
                true_gains.reshape(8 * dirs, members),
                start_gains.reshape(8 * dirs, members),
            )
        )
    )
    return (final.reshape(true_gains.shape), residual.reshape(thermal_noise.shape))


def solution(mesh):
    return jax.shard_map(
        on_device,
        mesh=mesh,
        in_specs=(
            P(None, "stn"),
            P(None, "chan"),
            P(),
            P(),
            P("chan", "stn", None),
            P(None, None, "chan", "stn", None),
            P(None, None, None, "stn"),
            P(None, None, None, "stn"),
        ),
        out_specs=(P(None, None, None, "stn"), P(None, None, "chan", "stn", None)),
        check_vma=False,
    )
```

```python
import functools

import jax
import jax.numpy as jnp
from jax import lax
from jax.experimental import pallas as pl
from jax.experimental.pallas import tpu as pltpu
from jax.sharding import PartitionSpec as P

ITERS = 3
LANES = 128
MESH = pl.DeviceIdType.MESH

band_spread = 6.0
ridge_term = 1.0
turn_scale = 20.0

SINE = (3.1415926401307073, -5.167710083507893, 2.5500775232145596, -0.5982912856201866, 0.07765766030500078)
COSINE = (
    0.9999999997799042,
    -4.9348021370788056,
    4.0587091595557485,
    -1.3352120030440895,
    0.23493731378565055,
    -0.024396324298134327,
)


def horner(terms, square):
    value = square * terms[-1] + terms[-2]
    for term in terms[-3::-1]:
        value = value * square + term
    return value


def turn_wave(turns):
    rest = turns - jnp.floor(turns + 0.5)
    square = rest * rest
    half_sine = rest * horner(SINE, square)
    half_cosine = horner(COSINE, square)
    twice = half_sine + half_sine
    return 1.0 - twice * half_sine, twice * half_cosine


def split_pair(value):
    high = value.astype(jnp.bfloat16)
    return high, (value - high.astype(jnp.float32)).astype(jnp.bfloat16)


def cmul(a, b):
    return a[0] * b[0] - a[1] * b[1], a[0] * b[1] + a[1] * b[0]


def cmul_conj(a, b):
    return a[0] * b[0] + a[1] * b[1], a[1] * b[0] - a[0] * b[1]


def cadd(a, b):
    return a[0] + b[0], a[1] + b[1]


def mat_mul(left, right):
    return [
        cadd(cmul(left[2 * i], right[j]), cmul(left[2 * i + 1], right[2 + j]))
        for i in range(2)
        for j in range(2)
    ]


def mat_mul_adj(left, right):
    return [
        cadd(cmul_conj(left[2 * i], right[2 * j]), cmul_conj(left[2 * i + 1], right[2 * j + 1]))
        for i in range(2)
        for j in range(2)
    ]


def start_copy(src, dst, send_sem, recv_sem, peer):
    copy = pltpu.make_async_remote_copy(
        src_ref=src,
        dst_ref=dst,
        send_sem=send_sem,
        recv_sem=recv_sem,
        device_id=peer,
        device_id_type=MESH,
    )
    copy.start()
    return copy


def far_first(count, stride):
    ring = count // 2
    moves = [(row, step) for row in range(2) for step in range(ring) if row or step]
    return sorted(moves, key=lambda move: -(move[0] * stride + min(move[1], ring - move[1])))


def moved_to(index, move, count):
    ring = count // 2
    row = lax.rem(index // ring + move[0], 2)
    return row * ring + lax.rem(lax.rem(index, ring) + move[1], ring)


def kernel(
    sizes,
    positions_in,
    catalogue_in,
    ids_in,
    counts_in,
    flags_in,
    noise_in,
    true_in,
    start_in,
    final,
    residual,
    positions,
    catalogue,
    ids,
    counts,
    flags,
    true_gains,
    start_gains,
    load_sem,
    square,
    own_cat,
    sibling_cat,
    every_cat,
    parts_cat,
    onehot,
    picks,
    cat_pair_sem,
    own_place,
    every_place,
    place_rows,
    own_gains,
    every_gains,
    gain_pair_sem,
    true_far,
    gain_far,
    near_true,
    near_gain,
    coherent,
    product,
    observed,
    predicted,
    weight,
    misfit,
    normal,
    pair,
    mine,
    sums,
    fresh,
    spread,
    cat_send,
    cat_recv,
    place_send,
    place_recv,
    gain_send,
    gain_recv,
    pair_send,
    pair_recv,
    sum_send,
    sum_recv,
    fresh_send,
    fresh_recv,
    turn_send,
    turn_recv,
):
    groups, chans, dirs, slots, members, chan_total = sizes
    chips = chans // 2
    group = lax.axis_index("stn")
    channel = lax.axis_index("chan")
    chip = channel // 2
    core = lax.rem(channel, 2)
    stations = groups * members
    half = members // 2

    loads = [
        pltpu.make_async_copy(source, target, load_sem.at[i])
        for i, (source, target) in enumerate(
            (
                (catalogue_in, catalogue),
                (positions_in, positions),
                (true_in, true_gains),
                (start_in, start_gains),
                (ids_in, ids),
                (counts_in, counts),
                (flags_in, flags),
                (noise_in, observed),
            )
        )
    ]
    for load in loads:
        load.start()

    sibling = {"chan": chip * 2 + 1 - core}
    chip_moves = [moved_to(chip, move, chips) for move in far_first(chips, 2)]
    chip_peers = [{"chan": peer * 2 + core} for peer in chip_moves]
    group_moves = [moved_to(group, move, groups) for move in far_first(groups, 1)]
    stn_peers = [{"stn": peer} for peer in group_moves]

    barrier = pltpu.get_barrier_semaphore()
    greeted = chip_peers + stn_peers + [sibling]
    for peer in greeted:
        pl.semaphore_signal(barrier, inc=1, device_id=peer, device_id_type=MESH)

    cat_width = catalogue.shape[1]
    for load in loads[0:2]:
        load.wait()
    own_cat[...] = jnp.zeros_like(own_cat)
    own_cat[0:7, 0:cat_width] = catalogue[...]
    own_cat[...] = jnp.where(core == 0, own_cat[...], pltpu.roll(own_cat[...], cat_width, 1))
    own_place[...] = jnp.zeros_like(own_place)
    own_place[0:3, 0:members] = positions[...]
    pl.semaphore_wait(barrier, len(greeted))

    cat_swap = start_copy(own_cat, sibling_cat, cat_pair_sem.at[0], cat_pair_sem.at[1], sibling)
    place_copies = [
        start_copy(own_place, every_place.at[group], place_send.at[i], place_recv.at[i], peer)
        for i, peer in enumerate(stn_peers)
    ]
    cat_swap.wait_recv()
    every_cat[chip] = own_cat[...] + sibling_cat[...]
    cat_copies = [
        start_copy(
            every_cat.at[chip], every_cat.at[chip], cat_send.at[i], cat_recv.at[i], peer
        )
        for i, peer in enumerate(chip_peers)
    ]
    for load in loads[2:4]:
        load.wait()
    square[...] = jnp.zeros_like(square)
    square[:, 0:members] = true_gains[...]
    own_gains[:, 0:LANES] = jnp.transpose(square[...])[0:members, :]
    square[:, 0:members] = start_gains[...]
    own_gains[:, LANES : 2 * LANES] = jnp.transpose(square[...])[0:members, :]

    kept = pl.ds(pl.multiple_of(core * half, half), half)
    away = pl.ds(pl.multiple_of((1 - core) * half, half), half)
    every_gains[core, group] = own_gains[kept, :]
    gain_copies = [
        start_copy(
            every_gains.at[core, group],
            every_gains.at[core, group],
            gain_send.at[i],
            gain_recv.at[i],
            peer,
        )
        for i, peer in enumerate(stn_peers)
    ]
    every_place[group] = own_place[...]
    near_true[...] = own_gains[:, 0:LANES]
    near_gain[...] = own_gains[:, LANES : 2 * LANES]
    for load in loads[4:]:
        load.wait()

    near_index = group * members + lax.broadcasted_iota(jnp.int32, (members, stations), 0)
    far_index = lax.broadcasted_iota(jnp.int32, (members, stations), 1)
    weight[...] = jnp.where(near_index != far_index, flags[...].astype(jnp.float32), 0.0)

    square[...] = jnp.zeros_like(square)
    square[0:dirs, 0:slots] = ids[...].astype(jnp.float32)
    square[...] = jnp.transpose(square[...])
    lane_column = lax.broadcasted_iota(jnp.int32, (slots, LANES), 1)
    lane_value = lane_column.astype(jnp.float32)
    lane_block = (lane_column // 8).astype(jnp.float32)

    def mark(direction, carry):
        named = jnp.sum(
            jnp.where(lane_column == direction, square[0:slots, :], 0.0), axis=1, keepdims=True
        )
        block_of = jnp.floor(named * (1.0 / LANES))
        within = named - block_of * LANES
        onehot[direction] = jnp.where(within == lane_value, 1.0, 0.0).astype(jnp.bfloat16)
        picks[direction] = jnp.where(lane_block == block_of, 1.0, 0.0)
        return carry

    lax.fori_loop(0, dirs, mark, 0, unroll=4)

    frequency = 1.0 + band_spread * channel.astype(jnp.float32) / chan_total
    log_frequency = jnp.log(jnp.full((1, LANES), frequency, jnp.float32))
    lane_row = lax.broadcasted_iota(jnp.int32, (1, LANES), 1)
    imag_lane = lane_row >= 4 * members
    entry_lane = lax.rem(lane_row // members, 4)

    for copy in reversed(cat_copies):
        copy.wait_recv()
    stacked = jnp.concatenate(
        [
            every_cat[2 * at] + pltpu.roll(every_cat[2 * at + 1], 2 * cat_width, 1)
            for at in range(chips // 2)
        ]
        + [jnp.zeros((LANES - 4 * chips, LANES), jnp.float32)],
        axis=0,
    )
    whole = jnp.transpose(stacked)
    first = whole.astype(jnp.bfloat16).astype(jnp.float32)
    second = (whole - first).astype(jnp.bfloat16).astype(jnp.float32)
    third = whole - first - second
    parts_cat[:, 0:LANES] = (first + pltpu.roll(second, 64, 1)).astype(jnp.bfloat16)
    parts_cat[:, LANES : 2 * LANES] = third.astype(jnp.bfloat16)

    found = jnp.dot(
        onehot[...].reshape(dirs * slots, LANES),
        parts_cat[...],
        preferred_element_type=jnp.float32,
    )
    found = (
        found[:, 0:LANES] + pltpu.roll(found[:, 0:LANES], 64, 1) + found[:, LANES : 2 * LANES]
    )
    picks[...] = picks[...] * found.reshape(dirs, slots, LANES)
    lane_kind = lax.rem(lane_column, 8)

    for copy in reversed(place_copies):
        copy.wait_recv()
    per_row = LANES // members
    scale = turn_scale * frequency
    for block in range(groups // per_row):
        joined = every_place[block * per_row]
        for at in range(1, per_row):
            joined = joined + pltpu.roll(every_place[block * per_row + at], members * at, 1)
        place_rows[:, block * LANES : (block + 1) * LANES] = joined * scale
    tiled = own_place[...] * scale
    for shift in (members, 2 * members, 4 * members):
        tiled = tiled + pltpu.roll(tiled, shift, 1)

    def model(direction, carry):
        picked = picks[direction]

        def column(at):
            return jnp.broadcast_to(
                jnp.sum(
                    jnp.where(lane_kind == at, picked, 0.0),
                    axis=1,
                    keepdims=True,
                ),
                (slots, LANES),
            )

        cos_l, cos_m = column(0), column(1)
        depth = jnp.sqrt(1.0 - cos_l * cos_l - cos_m * cos_m) - 1.0
        rows = lax.broadcasted_iota(jnp.int32, (slots, LANES), 0)
        scaled = jnp.where(
            rows < counts[direction], jnp.exp(column(6) * log_frequency), 0.0
        )
        stokes_i, stokes_q, stokes_u, stokes_v = (scaled * column(at) for at in (2, 3, 4, 5))
        bright_real = jnp.where(
            entry_lane == 0,
            stokes_i + stokes_q,
            jnp.where(entry_lane == 3, stokes_i - stokes_q, stokes_u),
        )
        bright_imag = jnp.where(
            entry_lane == 1, stokes_v, jnp.where(entry_lane == 2, -stokes_v, 0.0)
        )
        near_cos, near_sin = turn_wave(
            tiled[0:1, :] * cos_l + tiled[1:2, :] * cos_m + tiled[2:3, :] * depth
        )
        real_side = jnp.where(imag_lane, bright_imag, bright_real)
        imag_side = jnp.where(imag_lane, bright_real, -bright_imag)
        upper = real_side * near_cos + imag_side * near_sin
        lower = real_side * near_sin - imag_side * near_cos
        near_side = jnp.transpose(jnp.concatenate([upper, lower], axis=0))
        near_high, near_low = split_pair(near_side)
        blocks = []
        for block in range(stations // LANES):
            lanes = slice(block * LANES, (block + 1) * LANES)
            blocks.append(
                jnp.concatenate(
                    turn_wave(
                        place_rows[0:1, lanes] * cos_l
                        + place_rows[1:2, lanes] * cos_m
                        + place_rows[2:3, lanes] * depth
                    ),
                    axis=0,
                )
            )
        far_high, far_low = split_pair(jnp.concatenate(blocks, axis=1))

        def times(left, right):
            return jnp.dot(left, right, preferred_element_type=jnp.float32)

        result = times(
            jnp.concatenate([near_high, near_low], axis=1),
            jnp.concatenate([far_high, far_high], axis=0),
        ) + times(near_high, far_low)
        coherent[direction] = result.reshape(8, members, stations)
        return carry

    lax.fori_loop(0, dirs // 2, model, 0, unroll=8)
    for copy in reversed(gain_copies):
        copy.wait_recv()
    gain_hand = start_copy(
        every_gains.at[core],
        every_gains.at[core],
        gain_pair_sem.at[0],
        gain_pair_sem.at[1],
        sibling,
    )
    lax.fori_loop(dirs // 2, dirs, model, 0, unroll=8)
    gain_hand.wait_recv()

    def far_rows(lanes):
        tiles = [every_gains[at, other, :, lanes] for other in range(groups) for at in range(2)]
        return jnp.transpose(jnp.concatenate(tiles, axis=0))

    true_far[...] = far_rows(slice(0, LANES))
    gain_far[...] = far_rows(slice(LANES, 2 * LANES))

    near_lane = lax.broadcasted_iota(jnp.int32, (members, LANES), 1)
    halves = [slice(at * LANES, (at + 1) * LANES) for at in range(stations // LANES)]

    def near_matrix(ref, direction):
        whole_near = ref[...]
        return [
            tuple(
                jnp.sum(
                    jnp.where(near_lane == (part * 4 + entry) * dirs + direction, whole_near, 0.0),
                    axis=1,
                    keepdims=True,
                )
                for part in range(2)
            )
            for entry in range(4)
        ]

    def far_matrix(ref, direction, lanes):
        return [
            tuple(
                ref[pl.ds((part * 4 + entry) * dirs + direction, 1), :][:, lanes]
                for part in range(2)
            )
            for entry in range(4)
        ]

    def planes(ref, lanes, *lead):
        return [
            tuple(ref[(*lead, part * 4 + entry, slice(None), lanes)] for part in range(2))
            for entry in range(4)
        ]

    def add_planes(ref, lanes, matrix):
        for entry in range(4):
            for part in range(2):
                ref[part * 4 + entry, :, lanes] += matrix[entry][part]

    def predict(step, carry, with_truth):
        directions = [step * 2, step * 2 + 1]
        near = [near_matrix(near_gain, direction) for direction in directions]
        if with_truth:
            near_sky = [near_matrix(near_true, direction) for direction in directions]
        totals = [[0.0] * 4 for direction in directions]
        for lanes in halves:
            modelled, truth = [], []
            for at, direction in enumerate(directions):
                seen = planes(coherent, lanes, direction)
                if with_truth:
                    spun = mat_mul_adj(seen, far_matrix(true_far, direction, lanes))
                    truth.append(mat_mul(near_sky[at], spun))
                spun = mat_mul_adj(seen, far_matrix(gain_far, direction, lanes))
                modelled.append(mat_mul(near[at], spun))
                for entry in range(4):
                    for part in range(2):
                        product[direction, part * 4 + entry, :, lanes] = spun[entry][part]
                weighted = [
                    tuple(weight[:, lanes] * value for value in spun[entry]) for entry in range(2)
                ]
                first_power = sum(
                    weighted[entry][part] * spun[entry][part]
                    for entry in range(2)
                    for part in range(2)
                )
                second_power = weight[:, lanes] * sum(
                    spun[entry][part] * spun[entry][part] for entry in (2, 3) for part in range(2)
                )
                cross = cadd(cmul_conj(weighted[0], spun[2]), cmul_conj(weighted[1], spun[3]))
                for kind, value in enumerate((first_power, second_power, *cross)):
                    totals[at][kind] = totals[at][kind] + value
            add_planes(predicted, lanes, [cadd(a, b) for a, b in zip(*modelled)])
            if with_truth:
                add_planes(observed, lanes, [cadd(a, b) for a, b in zip(*truth)])
        collected = normal[...]
        for at, direction in enumerate(directions):
            for kind in range(4):
                collected = jnp.where(
                    near_lane == kind * dirs + direction,
                    jnp.sum(totals[at][kind], axis=1, keepdims=True),
                    collected,
                )
        normal[...] = collected
        return carry

    half_lane = near_lane[0:half]

    def correlate(rows, at, iteration):
        def body(direction, carry):
            missed = [
                tuple(misfit[part * 4 + entry, rows, :] for part in range(2))
                for entry in range(4)
            ]
            turned_back = [
                tuple(product[direction, part * 4 + entry, rows, :] for part in range(2))
                for entry in range(4)
            ]
            found = mat_mul_adj(missed, turned_back)
            collected = mine[iteration, at, 0:half, :]
            for entry in range(4):
                for part in range(2):
                    value = sum(found[entry][part][:, lanes] for lanes in halves)
                    collected = jnp.where(
                        half_lane == (part * 4 + entry) * dirs + direction,
                        jnp.sum(value, axis=1, keepdims=True),
                        collected,
                    )
            mine[iteration, at, 0:half, :] = collected
            return carry

        mine[iteration, at, 0:half, :] = jnp.zeros((half, LANES), jnp.float32)
        lax.fori_loop(0, dirs, body, 0, unroll=8)
        powers = normal[rows, :]
        beside = pltpu.roll(powers, LANES // 2, 1)
        mine[iteration, at, half:, :] = jnp.where(
            half_lane[0 : half // 2] < LANES // 2, powers[0 : half // 2], beside[half // 2 :]
        )

    pending = [cat_swap, gain_hand] + cat_copies + place_copies + gain_copies

    def settle(copies):
        for copy in pending:
            copy.wait_send()
        pending.clear()
        for copy in reversed(copies):
            copy.wait_recv()
        pending.extend(copies)
    normal[...] = jnp.zeros_like(normal)

    for iteration in range(ITERS):
        predicted[...] = jnp.zeros_like(predicted)
        lax.fori_loop(
            0,
            dirs // 2,
            functools.partial(predict, with_truth=iteration == 0),
            0,
            unroll=1,
        )
        for plane in range(8):
            misfit[plane] = weight[...] * (observed[plane] - predicted[plane])
        last = iteration == ITERS - 1
        if last:
            residual[...] = misfit[...]

        correlate(away, 0, iteration)
        swap = start_copy(
            mine.at[iteration, 0],
            pair.at[iteration],
            pair_send.at[iteration],
            pair_recv.at[iteration],
            sibling,
        )
        correlate(kept, 1, iteration)
        swap.wait_recv()
        pending.append(swap)
        sums[iteration, chip] = mine[iteration, 1] + pair[iteration]
        copies = [
            start_copy(
                sums.at[iteration, chip],
                sums.at[iteration, chip],
                sum_send.at[iteration, i],
                sum_recv.at[iteration, i],
                peer,
            )
            for i, peer in enumerate(chip_peers)
        ]
        settle(copies)
        total = sums[iteration, 0]
        for at in range(1, chips):
            total = total + sums[iteration, at]

        def lanes_of(array, at):
            return pltpu.roll(array, LANES - at * dirs, 1) if at else array

        powers = total[half:, :]
        powers = jnp.concatenate([powers, pltpu.roll(powers, LANES // 2, 1)], axis=0)
        gains = near_gain[kept, :]
        current = [
            tuple(lanes_of(gains, part * 4 + entry) for part in range(2)) for entry in range(4)
        ]
        gathered = [
            tuple(lanes_of(total[0:half, :], part * 4 + entry) for part in range(2))
            for entry in range(4)
        ]
        upper_diag, lower_diag, cross_real, cross_imag = (
            lanes_of(powers, at) for at in range(4)
        )
        nothing = jnp.zeros_like(upper_diag)
        hermitian = [
            (upper_diag, nothing),
            (cross_real, cross_imag),
            (cross_real, -cross_imag),
            (lower_diag, nothing),
        ]
        numerator = [
            cadd(a, b) for a, b in zip(gathered, mat_mul(current, hermitian))
        ]
        upper_diag = upper_diag + ridge_term
        lower_diag = lower_diag + ridge_term
        determinant = (
            upper_diag * lower_diag - cross_real * cross_real - cross_imag * cross_imag
        )
        inverse = [
            (lower_diag / determinant, nothing),
            (-cross_real / determinant, -cross_imag / determinant),
            (-cross_real / determinant, cross_imag / determinant),
            (upper_diag / determinant, nothing),
        ]
        estimate = mat_mul(numerator, inverse)
        updated = jnp.zeros((half, LANES), jnp.float32)
        for entry in range(4):
            for part in range(2):
                at = part * 4 + entry
                value = 0.5 * (current[entry][part] + estimate[entry][part])
                moved = pltpu.roll(value, at * dirs, 1) if at else value
                inside = near_lane[0:half] // dirs == at
                updated = jnp.where(inside, moved, updated)
        fresh[iteration] = updated

        spread[iteration, core, group] = updated
        if not last:
            settle(
                [
                    start_copy(
                        fresh.at[iteration],
                        spread.at[iteration, core, group],
                        fresh_send.at[iteration, i],
                        fresh_recv.at[iteration, i],
                        peer,
                    )
                    for i, peer in enumerate(stn_peers)
                ]
            )
            handed = spread.at[iteration, core]
        else:
            handed = spread.at[iteration, core, group]
        settle(
            [
                start_copy(
                    handed, handed, turn_send.at[iteration], turn_recv.at[iteration], sibling
                )
            ]
        )
        near_gain[...] = jnp.concatenate(
            [spread[iteration, at, group] for at in range(2)], axis=0
        )
        if not last:
            gain_far[...] = jnp.transpose(
                jnp.concatenate(
                    [
                        spread[iteration, at, other]
                        for other in range(groups)
                        for at in range(2)
                    ],
                    axis=0,
                )
            )

    square[0:members, :] = near_gain[...]
    final[...] = jnp.transpose(square[...])[:, 0:members]
    for copy in pending:
        copy.wait_send()


def on_device(
    positions, catalogue, cluster_ids, counts, flag_mask, thermal_noise, true_gains, start_gains
):
    groups = lax.axis_size("stn")
    chans = lax.axis_size("chan")
    dirs, slots = cluster_ids.shape
    members = positions.shape[1]
    stations = groups * members
    chips = chans // 2
    half = members // 2
    sizes = (groups, chans, dirs, slots, members, float(chans))
    f32 = jnp.float32
    vmem = pl.BlockSpec(memory_space=pltpu.VMEM)
    hbm = pl.BlockSpec(memory_space=pltpu.HBM)
    dma = pltpu.SemaphoreType.DMA

    final, residual = pl.pallas_call(
        lambda *refs: kernel(sizes, *refs),
        name="calibrate",
        out_shape=(
            jax.ShapeDtypeStruct((8 * dirs, members), f32),
            jax.ShapeDtypeStruct((8, members, stations), f32),
        ),
        in_specs=[hbm] * 8,
        out_specs=(vmem, vmem),
        scratch_shapes=[
            pltpu.VMEM(positions.shape, f32),
            pltpu.VMEM(catalogue.shape, f32),
            pltpu.VMEM(cluster_ids.shape, jnp.int32),
            pltpu.SMEM(counts.shape, jnp.int32),
            pltpu.VMEM((members, stations), jnp.int32),
            pltpu.VMEM((8 * dirs, members), f32),
            pltpu.VMEM((8 * dirs, members), f32),
            dma((8,)),
            pltpu.VMEM((LANES, LANES), f32),
            pltpu.VMEM((8, LANES), f32),
            pltpu.VMEM((8, LANES), f32),
            pltpu.VMEM((chips, 8, LANES), f32),
            pltpu.VMEM((LANES, 2 * LANES), jnp.bfloat16),
            pltpu.VMEM((dirs, slots, LANES), jnp.bfloat16),
            pltpu.VMEM((dirs, slots, LANES), f32),
            dma((2,)),
            pltpu.VMEM((8, LANES), f32),
            pltpu.VMEM((groups, 8, LANES), f32),
            pltpu.VMEM((8, stations), f32),
            pltpu.VMEM((members, 2 * LANES), f32),
            pltpu.VMEM((2, groups, half, 2 * LANES), f32),
            dma((2,)),
            pltpu.VMEM((8 * dirs, stations), f32),
            pltpu.VMEM((8 * dirs, stations), f32),
            pltpu.VMEM((members, LANES), f32),
            pltpu.VMEM((members, LANES), f32),
            pltpu.VMEM((dirs, 8, members, stations), f32),
            pltpu.VMEM((dirs, 8, members, stations), f32),
            pltpu.VMEM((8, members, stations), f32),
            pltpu.VMEM((8, members, stations), f32),
            pltpu.VMEM((members, stations), f32),
            pltpu.VMEM((8, members, stations), f32),
            pltpu.VMEM((members, LANES), f32),
            pltpu.VMEM((ITERS, half + half // 2, LANES), f32),
            pltpu.VMEM((ITERS, 2, half + half // 2, LANES), f32),
            pltpu.VMEM((ITERS, chips, half + half // 2, LANES), f32),
            pltpu.VMEM((ITERS, half, LANES), f32),
            pltpu.VMEM((ITERS, 2, groups, half, LANES), f32),
            dma((chips - 1,)),
            dma((chips - 1,)),
            dma((groups - 1,)),
            dma((groups - 1,)),
            dma((groups - 1,)),
            dma((groups - 1,)),
            dma((ITERS,)),
            dma((ITERS,)),
            dma((ITERS, chips - 1)),
            dma((ITERS, chips - 1)),
            dma((ITERS, groups - 1)),
            dma((ITERS, groups - 1)),
            dma((ITERS,)),
            dma((ITERS,)),
        ],
        compiler_params=pltpu.CompilerParams(
            collective_id=1, has_side_effects=True, vmem_limit_bytes=24 << 20
        ),
    )(
        *(
            pltpu.with_memory_space_constraint(array, pltpu.HBM)
            for array in (
                positions,
                catalogue,
                cluster_ids,
                counts,
                flag_mask.reshape(members, stations),
                thermal_noise.reshape(8, members, stations),
                true_gains.reshape(8 * dirs, members),
                start_gains.reshape(8 * dirs, members),
            )
        )
    )
    return (final.reshape(true_gains.shape), residual.reshape(thermal_noise.shape))


def solution(mesh):
    return jax.shard_map(
        on_device,
        mesh=mesh,
        in_specs=(
            P(None, "stn"),
            P(None, "chan"),
            P(),
            P(),
            P("chan", "stn", None),
            P(None, None, "chan", "stn", None),
            P(None, None, None, "stn"),
            P(None, None, None, "stn"),
        ),
        out_specs=(P(None, None, None, "stn"), P(None, None, "chan", "stn", None)),
        check_vma=False,
    )
```
